256 devices in a mesh: seq: 64 (over x, z_lo, y, core), chan: 4 (over z_hi).
Axes of the slice: x: 4, y: 4, z: 8 (z_hi: 4, z_lo: 2; z = z_hi * 2 + z_lo), core: 2. Of those that a mesh axis runs over, the one named last changes fastest.
Arguments:
- layer_input: bfloat16 [16384, 1024], P('seq', 'chan'), may hold values from -6 to 6
- w_in: bfloat16 [1024, 3, 1024], P('seq', None, 'chan'), may hold values from -0.1875 to 0.1875
- filters: float32 [2, 16384, 1024], P(None, 'seq', 'chan'), may hold values from -0.1015625 to 0.1015625, as said below
- bias: float32 [2, 1024], P(None, 'chan'), may hold values from 0.25 to 1.5
- cotangent: bfloat16 [16384, 1024], P('seq', 'chan'), may hold values from -6 to 6
Outputs:
- layer_output: bfloat16 [16384, 1024], P('seq', 'chan')
- grad_u: bfloat16 [16384, 1024], P('seq', 'chan')
- grad_w: float32 [1024, 3, 1024], P('seq', None, 'chan')
- grad_filters: float32 [2, 16384, 1024], P(None, 'seq', 'chan')
- grad_bias: float32 [2, 1024], P(None, 'chan')
The draws below stay inside these ranges and needn't reach their ends.
Inputs may be any that keep to these rules, and one draw needn't show every extreme that they name: `filters`: each channel of each filter decays exponentially along the lag at a channel-dependent rate.
All inputs are finite; a program needn't handle non-finite values.
Results may differ from the reference program's by a relative error of at most 0.014.
Values may be sent and summed in bfloat16 or wider, within the bound.
A program may use at most 128 MiB of HBM per device.

```python
import math
import jax
import jax.numpy as jnp

D = 1024
TOKENS = 16384


def draw_filters(key, part):
    key_rate, key_noise = jax.random.split(jax.random.fold_in(key, 7))
    rates = jnp.exp(jax.random.uniform(key_rate, (2, 1, D), jnp.float32, math.log(0.5), math.log(8.0)))
    fraction = jnp.arange(TOKENS, dtype=jnp.float32)[None, :, None] / TOKENS
    noise = jax.random.truncated_normal(key_noise, -3.0, 3.0, (2, TOKENS, D), jnp.float32)
    amplitude = jnp.sqrt(2.0 * rates / (1.0 - jnp.exp(-2.0 * rates)) / TOKENS)
    return noise * jnp.exp(-rates * fraction) * amplitude


def block_scale(stream_key, extent, pieces, low, top_value):
    level, own = 1.0, jax.random.fold_in(stream_key, 6)
    for dim, parts in pieces:
        heights = jnp.exp(jax.random.uniform(jax.random.fold_in(own, dim), (parts,), jnp.float32, low / len(pieces), top_value / len(pieces)))
        level = level * jnp.repeat(heights, extent[dim] // parts).reshape([-1 if axis == dim else 1 for axis in range(len(extent))])
    return level


def centred(stream_key, extent, deviation, reach, cuts=(), held_as=jnp.bfloat16):
    gain = block_scale(stream_key, extent, cuts, -0.22, 0.18) if cuts else 1.0
    entries = jax.random.normal(stream_key, extent, jnp.float32) * deviation * gain
    return jnp.minimum(jnp.maximum(entries, -reach), reach).astype(held_as)


def setup_inputs(seed: int = 0) -> dict:
    seeds = jax.random.split(jax.random.key(seed), 6)
    layer_input = centred(seeds[0], (TOKENS, D), 1.0, 6.0, ((0, 64), (1, 4)))
    w_in = centred(seeds[1], (D, 3, D), D ** -0.5, 0.1875, ((0, 64), (2, 4)))
    filters = draw_filters(jax.random.fold_in(seeds[5], 71), 0)
    bias = jnp.clip(0.25 + 1.25 * jax.random.uniform(seeds[3], (2, D), jnp.float32) ** block_scale(seeds[3], (2, D), ((1, 4),), -0.2, 0.2), 0.25, 1.5)
    cotangent = centred(seeds[4], (TOKENS, D), 1.0, 6.0, ((0, 64), (1, 4)))
    return dict(layer_input=layer_input, w_in=w_in, filters=filters, bias=bias, cotangent=cotangent)


def spectrum(signal):
    return jnp.fft.rfft(signal, n=2 * TOKENS, axis=0)


def inverse(values):
    return jnp.fft.irfft(values, n=2 * TOKENS, axis=0)[:TOKENS]


def reference(layer_input, w_in, filters, bias, cotangent):
    flat = w_in.reshape(D, 3 * D)
    proj = jnp.dot(layer_input, flat, preferred_element_type=jnp.float32).reshape(TOKENS, 3, D)
    values_v = proj[:, 0]
    gate_one = proj[:, 1]
    gate_two = proj[:, 2]
    spec_h1 = spectrum(filters[0])
    spec_h2 = spectrum(filters[1])
    spec_v = spectrum(values_v)
    conv_one = inverse(spec_h1 * spec_v) + bias[0] * values_v
    mixed_one = gate_one * conv_one
    spec_z = spectrum(mixed_one)
    conv_two = inverse(spec_h2 * spec_z) + bias[1] * mixed_one
    output = (gate_two * conv_two).astype(jnp.bfloat16)
    grad_out = cotangent.astype(jnp.float32)
    grad_gate_two = grad_out * conv_two
    grad_conv_two = grad_out * gate_two
    spec_g2 = spectrum(grad_conv_two)
    grad_mixed = inverse(jnp.conj(spec_h2) * spec_g2) + bias[1] * grad_conv_two
    grad_filt_two = inverse(spec_g2 * jnp.conj(spec_z))
    bias_grad_two = jnp.sum(grad_conv_two * mixed_one, axis=0)
    grad_gate_one = grad_mixed * conv_one
    grad_conv_one = grad_mixed * gate_one
    spec_g1 = spectrum(grad_conv_one)
    grad_values = inverse(jnp.conj(spec_h1) * spec_g1) + bias[0] * grad_conv_one
    grad_filt_one = inverse(spec_g1 * jnp.conj(spec_v))
    bias_grad_one = jnp.sum(grad_conv_one * values_v, axis=0)
    grad_proj = jnp.stack([grad_values, grad_gate_one, grad_gate_two], axis=1).astype(jnp.bfloat16)
    grad_flat = grad_proj.reshape(TOKENS, 3 * D)
    grad_input = jnp.dot(grad_flat, flat.T, preferred_element_type=jnp.float32).astype(jnp.bfloat16)
    grad_weight = jnp.dot(layer_input.T, grad_flat, preferred_element_type=jnp.float32).reshape(D, 3, D)
    grad_filt = jnp.stack([grad_filt_one, grad_filt_two])
    grad_skip = jnp.stack([bias_grad_one, bias_grad_two])
    return (output, grad_input, grad_weight, grad_filt, grad_skip)
```

```python
import functools
import math

import jax
import jax.numpy as jnp
import ml_dtypes
import numpy as np
from jax import lax
from jax.experimental import pallas as pl
from jax.experimental.pallas import tpu as pltpu
from jax.sharding import PartitionSpec as P

MESH = pl.DeviceIdType.MESH
LANES = 128
BF16 = jnp.bfloat16
F32 = jnp.float32


def tables(blocks):
    period = 2 * blocks * LANES
    chips = blocks // 4
    order = np.array([4 * j + tb for tb in range(4) for j in range(chips)])
    freq = np.arange(blocks) + 0.5
    lane = np.arange(LANES)
    angle = 2.0 * math.pi * freq[:, None] * order[None, :] / (2 * blocks)
    first = np.concatenate([np.cos(angle), -np.sin(angle)], axis=0)
    turn = 2.0 * math.pi * freq[:, None] * lane[None, :] / period
    inner = 2.0 * math.pi * ((lane[:, None] * lane[None, :]) % LANES) / LANES
    cosine, sine = np.cos(inner), np.sin(inner)
    middle = np.block([[cosine, -sine], [sine, cosine]])
    last = first.T * (2.0 / period)

    def parts(table, axis):
        high = table.astype(ml_dtypes.bfloat16)
        low = (table - high.astype(np.float64)).astype(ml_dtypes.bfloat16)
        return np.concatenate([high, low, high], axis=axis)

    return (
        parts(first, 1),
        parts(middle, 0),
        parts(middle.T, 0),
        parts(last, 1),
        np.cos(turn).astype(np.float32),
        np.sin(turn).astype(np.float32),
    )


def matmul(left, right, dims=((1,), (0,))):
    return lax.dot_general(left, right, (dims, ((), ())), preferred_element_type=F32)


def split(value):
    high = value.astype(BF16)
    low = (value - high.astype(F32)).astype(BF16)
    return high, low


def greet(me, peers, group, groups):
    barrier = pltpu.get_barrier_semaphore()

    def one(step, carry):
        pl.semaphore_signal(
            barrier, inc=1, device_id=(lax.rem(me + step, peers), group), device_id_type=MESH
        )
        return carry

    lax.fori_loop(1, peers, one, 0)
    for step in range(1, groups):
        pl.semaphore_signal(
            barrier, inc=1, device_id=(me, lax.rem(group + step, groups)), device_id_type=MESH
        )
    return barrier


def wait_bytes(ref, sem):
    pltpu.make_async_copy(ref, ref, sem).wait()


def gather_kernel(
    n, groups, x_ref, w_ref, filters_ref, cot_ref,
    wg_ref, xg_ref, a_recv, b_recv,
    stage_a, a_send, stage_b, b_send, sems, x_sems,
):
    me = lax.axis_index("seq")
    group = lax.axis_index("chan")
    core = lax.rem(me, 2)
    chip = me // 2
    partner = me + 1 - 2 * core
    chips = n // 2
    quota = LANES // chips
    rows_a, rows_b = a_send.shape[1], b_send.shape[1]
    barrier = greet(me, n, group, groups)

    def stage_early(value, base):
        turned = value.T
        for half in range(2):
            for q in range(quota):
                top = half * LANES + q * chips
                for tb in range(2):
                    stage_b[pl.ds(half * rows_b + base + q * 2 + tb, chips, stride=2 * rows_b), :] = turned[
                        top : top + chips, tb * LANES : (tb + 1) * LANES
                    ]

    stage_early(filters_ref[0], 0)
    stage_early(filters_ref[1], 2 * quota)
    stage_early(cot_ref[...].astype(F32), 4 * quota)
    for peer in range(n):
        stage_b[pl.ds(peer * rows_b + 6 * quota, 2 * quota), :] = jnp.zeros((2 * quota, LANES), F32)
    b_send[...] = stage_b[...].astype(BF16).reshape(b_send.shape)
    xg_ref[core, group] = x_ref[...]
    pl.semaphore_wait(barrier, n - 1 + groups - 1)

    def send_w(step, carry):
        peer = lax.rem(me + step, n)
        pltpu.make_async_remote_copy(
            src_ref=w_ref.at[lax.rem(peer, 2)], dst_ref=wg_ref.at[me],
            send_sem=sems.at[0], recv_sem=sems.at[1],
            device_id=(peer, group), device_id_type=MESH,
        ).start()
        return carry

    for step in range(1, groups):
        pltpu.make_async_remote_copy(
            src_ref=x_ref, dst_ref=xg_ref.at[core, group],
            send_sem=sems.at[2], recv_sem=x_sems.at[group],
            device_id=(me, lax.rem(group + step, groups)), device_id_type=MESH,
        ).start()
    lax.fori_loop(1, n, send_w, 0)
    pltpu.make_async_copy(w_ref.at[core], wg_ref.at[me], sems.at[1]).start()
    pltpu.make_async_remote_copy(
        src_ref=x_ref, dst_ref=xg_ref.at[core, group],
        send_sem=sems.at[2], recv_sem=sems.at[3],
        device_id=(partner, group), device_id_type=MESH,
    ).start()

    def send_b(step, carry):
        peer = lax.rem(me + step, n)
        pltpu.make_async_remote_copy(
            src_ref=b_send.at[peer], dst_ref=b_recv.at[me],
            send_sem=sems.at[4], recv_sem=sems.at[5],
            device_id=(peer, group), device_id_type=MESH,
        ).start()
        return carry

    lax.fori_loop(1, n, send_b, 0)
    pltpu.make_async_copy(b_send.at[me], b_recv.at[me], sems.at[5]).start()

    for step in range(1, groups):
        other = lax.rem(group + groups - step, groups)
        wait_bytes(xg_ref.at[core, other], x_sems.at[other])
        pltpu.make_async_remote_copy(
            src_ref=xg_ref.at[core, other], dst_ref=xg_ref.at[core, other],
            send_sem=sems.at[6], recv_sem=sems.at[3],
            device_id=(partner, group), device_id_type=MESH,
        ).start()
    wait_bytes(wg_ref, sems.at[1])
    wait_bytes(xg_ref.at[1 - core], sems.at[3])

    depth = x_ref.shape[1]
    slots = depth // wg_ref.shape[1]
    tokens = x_ref.shape[0]
    total = None
    for c in range(groups):
        rows = xg_ref[:, c].reshape(2 * tokens, depth)
        block = wg_ref[c * slots : (c + 1) * slots].reshape(depth, wg_ref.shape[2])
        term = matmul(rows, block)
        total = term if total is None else total + term
    turned = total.T
    for a in range(3):
        for q in range(quota):
            top = a * LANES + q * chips
            for tb in range(4):
                stage_a[pl.ds((a * quota + q) * 4 + tb, chips, stride=rows_a), :] = turned[
                    top : top + chips, tb * LANES : (tb + 1) * LANES
                ]
    a_send[...] = stage_a[...].astype(BF16).reshape(a_send.shape)

    def send_a(step, carry):
        peer = lax.rem(chip + step, chips)
        pltpu.make_async_remote_copy(
            src_ref=a_send.at[peer], dst_ref=a_recv.at[chip],
            send_sem=sems.at[7], recv_sem=sems.at[8],
            device_id=(2 * peer + core, group), device_id_type=MESH,
        ).start()
        return carry

    lax.fori_loop(1, chips, send_a, 0)
    pltpu.make_async_copy(a_send.at[chip], a_recv.at[chip], sems.at[8]).start()

    wait_bytes(wg_ref.at[pl.ds(0, n - 1)], sems.at[0])
    wait_bytes(xg_ref.at[0], sems.at[2])
    if groups > 1:
        wait_bytes(xg_ref.at[0, pl.ds(0, groups - 1)], sems.at[6])
    wait_bytes(b_recv.at[pl.ds(0, n - 1)], sems.at[4])
    wait_bytes(a_recv.at[pl.ds(0, chips - 1)], sems.at[7])
    wait_bytes(b_recv, sems.at[5])
    wait_bytes(a_recv, sems.at[8])


def conv_kernel(
    n, a_recv, b_recv, bias_ref, first_ref, middle_ref, middle_t_ref, last_ref, cos_ref, sin_ref,
    a_send, b_send,
    stage_a, stage_b, spec_h1, spec_h2, spec_v, spec_z, spec_g,
):
    me = lax.axis_index("seq")
    core = lax.rem(me, 2)
    chip = me // 2
    chips = n // 2
    quota = LANES // chips
    blocks = 4 * chips
    rows_a, rows_b = a_recv.shape[1], b_recv.shape[1]
    stage_a[...] = a_recv[...].reshape(stage_a.shape).astype(F32)
    stage_b[...] = b_recv[...].reshape(stage_b.shape).astype(F32)

    def columns(start, stride):
        return jnp.concatenate(
            [
                jnp.concatenate(
                    [start(q, tb)[0][pl.ds(start(q, tb)[1], chips, stride=stride), :] for q in range(quota)],
                    axis=1,
                )
                for tb in range(4)
            ],
            axis=0,
        )

    def late(a):
        return columns(lambda q, tb: (stage_a, (a * quota + q) * 4 + tb), rows_a)

    def early(base):
        return columns(lambda q, tb: (stage_b, (tb // 2) * rows_b + base + q * 2 + tb % 2), 2 * rows_b)

    def piece(value, q):
        return value[:, q * LANES : (q + 1) * LANES]

    def forward(value, spec, exact=False):
        high, low = split(value)
        if exact:
            wide = matmul(first_ref[:, : 2 * blocks], jnp.concatenate([high, high], axis=0))
        else:
            wide = matmul(first_ref[...], jnp.concatenate([high, high, low], axis=0))
        turn_cos, turn_sin = cos_ref[...], sin_ref[...]
        for q in range(quota):
            re = piece(wide[:blocks], q)
            im = piece(wide[blocks:], q)
            high, low = split(
                jnp.concatenate([re * turn_cos + im * turn_sin, im * turn_cos - re * turn_sin], axis=1)
            )
            spec[q * blocks : (q + 1) * blocks, :] = matmul(
                jnp.concatenate([high, high, low], axis=1), middle_ref[...]
            )

    def backward(left, right, conj_left, conj_right):
        turn_cos, turn_sin = cos_ref[...], sin_ref[...]
        columns_high, columns_low = [], []
        for q in range(quota):
            rows = slice(q * blocks, (q + 1) * blocks)
            l_re, l_im = left[rows, :LANES], left[rows, LANES:]
            r_re, r_im = right[rows, :LANES], right[rows, LANES:]
            cross = l_im * r_im
            y_re = l_re * r_re - (cross if conj_left == conj_right else -cross)
            if conj_left:
                y_im = l_re * r_im - l_im * r_re
            elif conj_right:
                y_im = l_im * r_re - l_re * r_im
            else:
                y_im = l_re * r_im + l_im * r_re
            high, low = split(jnp.concatenate([y_re, y_im], axis=1))
            out = matmul(jnp.concatenate([high, high, low], axis=1), middle_t_ref[...])
            re, im = out[:, :LANES], out[:, LANES:]
            high, low = split(
                jnp.concatenate([re * turn_cos - im * turn_sin, im * turn_cos + re * turn_sin], axis=0)
            )
            columns_high.append(high)
            columns_low.append(low)
        high = jnp.concatenate(columns_high, axis=1)
        low = jnp.concatenate(columns_low, axis=1)
        return matmul(last_ref[...], jnp.concatenate([high, high, low], axis=0))

    def skip(f):
        return jnp.concatenate(
            [
                jnp.full((1, LANES), bias_ref[f, core * LANES + q * chips + chip], F32)
                for q in range(quota)
            ],
            axis=1,
        )

    def store_late(value, a):
        for q in range(quota):
            for tb in range(4):
                stage_a[pl.ds((a * quota + q) * 4 + tb, chips, stride=rows_a), :] = piece(value, q)[
                    tb * chips : (tb + 1) * chips
                ]

    def store_early(value, base):
        for q in range(quota):
            for tb in range(4):
                at = (tb // 2) * rows_b + base + q * 2 + tb % 2
                stage_b[pl.ds(at, chips, stride=2 * rows_b), :] = piece(value, q)[
                    tb * chips : (tb + 1) * chips
                ]

    def store_skip(product, f):
        lane = lax.broadcasted_iota(jnp.int32, (1, LANES), 1)
        sums = jnp.sum(product, axis=0, keepdims=True)
        for q in range(quota):
            value = jnp.sum(piece(sums, q), axis=1, keepdims=True)
            one = value.astype(BF16).astype(F32)
            two = (value - one).astype(BF16).astype(F32)
            three = value - one - two
            row = jnp.where(lane == chip, one, 0.0)
            row = jnp.where(lane == chips + chip, two, row)
            row = jnp.where(lane == 2 * chips + chip, three, row)
            for half in range(2):
                at = half * rows_b + 6 * quota + f * quota + q
                stage_b[pl.ds(at, chips, stride=2 * rows_b), :] = jnp.broadcast_to(row, (chips, LANES))

    values_v, gate_one, gate_two = late(0), late(1), late(2)
    forward(early(0), spec_h1, True)
    forward(early(2 * quota), spec_h2, True)
    grad_out = early(4 * quota)
    skip_one, skip_two = skip(0), skip(1)
    forward(values_v, spec_v, True)
    conv_one = backward(spec_h1, spec_v, False, False) + skip_one * values_v
    mixed = gate_one * conv_one
    forward(mixed, spec_z)
    conv_two = backward(spec_h2, spec_z, False, False) + skip_two * mixed
    store_early(gate_two * conv_two, 4 * quota)
    store_late(grad_out * conv_two, 2)
    grad_conv_two = grad_out * gate_two
    forward(grad_conv_two, spec_g)
    store_skip(grad_conv_two * mixed, 1)
    grad_mixed = backward(spec_h2, spec_g, True, False) + skip_two * grad_conv_two
    store_early(backward(spec_g, spec_z, False, True), 2 * quota)
    store_late(grad_mixed * conv_one, 1)
    grad_conv_one = grad_mixed * gate_one
    forward(grad_conv_one, spec_g)
    store_skip(grad_conv_one * values_v, 0)
    store_late(backward(spec_h1, spec_g, True, False) + skip_one * grad_conv_one, 0)
    store_early(backward(spec_g, spec_v, False, True), 0)
    a_send[...] = stage_a[...].astype(BF16).reshape(a_send.shape)
    b_send[...] = stage_b[...].astype(BF16).reshape(b_send.shape)


def return_kernel(
    n, groups, a_send, b_send, xg_ref, wg_ref,
    out_ref, gu_ref, gw_ref, gf_ref, gb_ref,
    a_recv, b_recv, stage_a, stage_b, turned_ref, grad_ref, u_own, u_part, u_in, u_send, u_recv,
    w_send, w_recv, sems, u_sems,
):
    me = lax.axis_index("seq")
    group = lax.axis_index("chan")
    core = lax.rem(me, 2)
    chip = me // 2
    partner = me + 1 - 2 * core
    chips = n // 2
    quota = LANES // chips
    rows_a, rows_b = a_send.shape[1], b_send.shape[1]
    barrier = greet(me, n, group, groups)
    pl.semaphore_wait(barrier, n - 1 + groups - 1)

    def send_a(step, carry):
        peer = lax.rem(chip + step, chips)
        pltpu.make_async_remote_copy(
            src_ref=a_send.at[peer], dst_ref=a_recv.at[chip],
            send_sem=sems.at[0], recv_sem=sems.at[1],
            device_id=(2 * peer + core, group), device_id_type=MESH,
        ).start()
        return carry

    def send_b(step, carry):
        peer = lax.rem(me + step, n)
        pltpu.make_async_remote_copy(
            src_ref=b_send.at[peer], dst_ref=b_recv.at[me],
            send_sem=sems.at[2], recv_sem=sems.at[3],
            device_id=(peer, group), device_id_type=MESH,
        ).start()
        return carry

    lax.fori_loop(1, chips, send_a, 0)
    pltpu.make_async_copy(a_send.at[chip], a_recv.at[chip], sems.at[1]).start()
    lax.fori_loop(1, n, send_b, 0)
    pltpu.make_async_copy(b_send.at[me], b_recv.at[me], sems.at[3]).start()

    wait_bytes(a_recv, sems.at[1])
    stage_a[...] = a_recv[...].reshape(stage_a.shape).astype(F32)
    for a in range(3):
        for q in range(quota):
            top = a * LANES + q * chips
            for tb in range(4):
                turned_ref[top : top + chips, tb * LANES : (tb + 1) * LANES] = stage_a[
                    pl.ds((a * quota + q) * 4 + tb, chips, stride=rows_a), :
                ]
    tokens, depth = xg_ref.shape[2], xg_ref.shape[3]
    grad = turned_ref[...].T.astype(BF16)
    grad_ref[...] = grad.reshape(grad_ref.shape)
    slots = depth // wg_ref.shape[1]

    def weights(c):
        return wg_ref[c * slots : (c + 1) * slots].reshape(depth, wg_ref.shape[2])

    theirs = grad_ref[1 - core]
    for c in range(groups):
        u_part[c] = matmul(theirs, weights(c), ((1,), (1,))).astype(BF16)
    pltpu.make_async_remote_copy(
        src_ref=u_part, dst_ref=u_in, send_sem=sems.at[4], recv_sem=sems.at[5],
        device_id=(partner, group), device_id_type=MESH,
    ).start()
    for c in range(groups):
        rows = xg_ref[:, c].reshape(2 * tokens, depth)
        term = matmul(rows, grad, ((0,), (0,))).astype(BF16)
        w_send[c * slots : (c + 1) * slots] = term.reshape(slots, depth // slots, term.shape[1])

    def send_w(step, carry):
        peer = lax.rem(me + step, n)
        pltpu.make_async_remote_copy(
            src_ref=w_send.at[peer], dst_ref=w_recv.at[me],
            send_sem=sems.at[6], recv_sem=sems.at[7],
            device_id=(peer, group), device_id_type=MESH,
        ).start()
        return carry

    lax.fori_loop(1, n, send_w, 0)
    pltpu.make_async_copy(w_send.at[me], w_recv.at[me], sems.at[7]).start()

    mine = grad_ref[core]
    for c in range(groups):
        u_own[c] = matmul(mine, weights(c), ((1,), (1,)))
    wait_bytes(u_in, sems.at[5])
    for c in range(groups):
        both = u_own[c] + u_in[c].astype(F32)
        u_own[c] = both
        u_send[c] = both.astype(BF16)
    for step in range(1, groups):
        other = lax.rem(group + step, groups)
        pltpu.make_async_remote_copy(
            src_ref=u_send.at[other], dst_ref=u_recv.at[group],
            send_sem=sems.at[8], recv_sem=u_sems.at[group],
            device_id=(me, other), device_id_type=MESH,
        ).start()

    wait_bytes(b_recv, sems.at[3])
    stage_b[...] = b_recv[...].reshape(stage_b.shape).astype(F32)

    def collect(base):
        for half in range(2):
            for q in range(quota):
                top = half * LANES + q * chips
                for tb in range(2):
                    turned_ref[top : top + chips, tb * LANES : (tb + 1) * LANES] = stage_b[
                        pl.ds(half * rows_b + base + q * 2 + tb, chips, stride=2 * rows_b), :
                    ]
        return turned_ref[: 2 * LANES, : 2 * LANES].T

    gf_ref[0] = collect(0)
    gf_ref[1] = collect(2 * quota)
    out_ref[...] = collect(4 * quota).astype(BF16)
    lane = lax.broadcasted_iota(jnp.int32, (1, LANES), 1)
    for f in range(2):
        for half in range(2):
            line = jnp.zeros((1, LANES), F32)
            for q in range(quota):
                at = half * rows_b + 6 * quota + f * quota + q
                row = jnp.sum(stage_b[pl.ds(at, chips, stride=2 * rows_b), :], axis=0, keepdims=True)
                full = row + pltpu.roll(row, LANES - chips, 1) + pltpu.roll(row, LANES - 2 * chips, 1)
                moved = full if q == 0 else pltpu.roll(full, q * chips, 1)
                line = jnp.where((lane >= q * chips) & (lane < (q + 1) * chips), moved, line)
            gb_ref[f : f + 1, half * LANES : (half + 1) * LANES] = line

    total = u_own[group]
    for step in range(1, groups):
        other = lax.rem(group + step, groups)
        wait_bytes(u_recv.at[other], u_sems.at[other])
        total = total + u_recv[other].astype(F32)
    gu_ref[...] = total.astype(BF16)

    wait_bytes(w_recv, sems.at[7])
    for half in range(2):
        acc = w_recv[half].astype(F32)
        for j in range(1, chips):
            acc = acc + w_recv[2 * j + half].astype(F32)
        gw_ref[half] = acc

    wait_bytes(a_recv.at[pl.ds(0, chips - 1)], sems.at[0])
    wait_bytes(b_recv.at[pl.ds(0, n - 1)], sems.at[2])
    wait_bytes(u_in, sems.at[4])
    wait_bytes(w_recv.at[pl.ds(0, n - 1)], sems.at[6])
    if groups > 1:
        wait_bytes(u_recv.at[pl.ds(0, groups - 1)], sems.at[8])


def on_device(layer_input, w_in, filters, bias, cotangent):
    n = lax.axis_size("seq")
    groups = lax.axis_size("chan")
    tokens, width = layer_input.shape
    rows = w_in.shape[0]
    chips = n // 2
    quota = LANES // chips
    rows_a, rows_b = 12 * quota, 8 * quota
    cols = 3 * LANES
    vmem = pl.BlockSpec(memory_space=pltpu.VMEM)
    smem = pl.BlockSpec(memory_space=pltpu.SMEM)
    sds = jax.ShapeDtypeStruct
    dma = pltpu.SemaphoreType.DMA
    limit = 60 * 1024 * 1024

    w_halves = w_in.reshape(rows, 3, 2, LANES).transpose(2, 0, 1, 3).reshape(2, rows, cols)
    wg, xg, a_in, b_in = pl.pallas_call(
        functools.partial(gather_kernel, n, groups),
        out_shape=(
            sds((n, rows, cols), BF16),
            sds((2, groups, tokens, width), BF16),
            sds((chips, rows_a, LANES), BF16),
            sds((n, rows_b, LANES), BF16),
        ),
        in_specs=[vmem] * 4,
        out_specs=(vmem,) * 4,
        scratch_shapes=[
            pltpu.VMEM((chips * rows_a, LANES), F32),
            pltpu.VMEM((chips, rows_a, LANES), BF16),
            pltpu.VMEM((n * rows_b, LANES), F32),
            pltpu.VMEM((n, rows_b, LANES), BF16),
            dma((9,)),
            dma((groups,)),
        ],
        compiler_params=pltpu.CompilerParams(
            collective_id=0, has_side_effects=True, vmem_limit_bytes=limit
        ),
        name="gather",
    )(layer_input, w_halves, filters, cotangent)

    blocks = 4 * chips
    spec = pltpu.VMEM((quota * blocks, 2 * LANES), F32)
    a_out, b_out = pl.pallas_call(
        functools.partial(conv_kernel, n),
        out_shape=(sds(a_in.shape, BF16), sds(b_in.shape, BF16)),
        in_specs=[vmem, vmem, smem] + [vmem] * 6,
        out_specs=(vmem, vmem),
        scratch_shapes=[
            pltpu.VMEM((chips * rows_a, LANES), F32),
            pltpu.VMEM((n * rows_b, LANES), F32),
            spec, spec, spec, spec, spec,
        ],
        compiler_params=pltpu.CompilerParams(vmem_limit_bytes=limit),
        name="convolve",
    )(a_in, b_in, bias, *(jnp.asarray(table) for table in tables(blocks)))

    out, grad_u, grad_w, grad_f, grad_b = pl.pallas_call(
        functools.partial(return_kernel, n, groups),
        out_shape=(
            sds((tokens, width), BF16),
            sds((tokens, width), BF16),
            sds((2, rows, cols), F32),
            sds((2, tokens, width), F32),
            sds((2, width), F32),
        ),
        in_specs=[vmem] * 4,
        out_specs=(vmem,) * 5,
        scratch_shapes=[
            pltpu.VMEM((chips, rows_a, LANES), BF16),
            pltpu.VMEM((n, rows_b, LANES), BF16),
            pltpu.VMEM((chips * rows_a, LANES), F32),
            pltpu.VMEM((n * rows_b, LANES), F32),
            pltpu.VMEM((cols, 2 * tokens), F32),
            pltpu.VMEM((2, tokens, cols), BF16),
            pltpu.VMEM((groups, tokens, width), F32),
            pltpu.VMEM((groups, tokens, width), BF16),
            pltpu.VMEM((groups, tokens, width), BF16),
            pltpu.VMEM((groups, tokens, width), BF16),
            pltpu.VMEM((groups, tokens, width), BF16),
            pltpu.VMEM((n, rows, cols), BF16),
            pltpu.VMEM((n, rows, cols), BF16),
            dma((9,)),
            dma((groups,)),
        ],
        compiler_params=pltpu.CompilerParams(
            collective_id=1, has_side_effects=True, vmem_limit_bytes=limit
        ),
        name="give_back",
    )(a_out, b_out, xg, wg)
    grad_w = grad_w.reshape(2, rows, 3, LANES).transpose(1, 2, 0, 3).reshape(rows, 3, width)
    return (out, grad_u, grad_w, grad_f, grad_b)


def solution(mesh):
    in_specs = (
        P("seq", "chan"),
        P("seq", None, "chan"),
        P(None, "seq", "chan"),
        P(None, "chan"),
        P("seq", "chan"),
    )
    out_specs = (
        P("seq", "chan"),
        P("seq", "chan"),
        P("seq", None, "chan"),
        P(None, "seq", "chan"),
        P(None, "chan"),
    )
    return jax.shard_map(
        on_device, mesh=mesh, in_specs=in_specs, out_specs=out_specs, check_vma=False
    )
```

```python
import functools
import math

import jax
import jax.numpy as jnp
import ml_dtypes
import numpy as np
from jax import lax
from jax.experimental import pallas as pl
from jax.experimental.pallas import tpu as pltpu
from jax.sharding import PartitionSpec as P

MESH = pl.DeviceIdType.MESH
LANES = 128
BF16 = jnp.bfloat16
F32 = jnp.float32


def tables(blocks):
    period = 2 * blocks * LANES
    chips = blocks // 4
    order = np.array([4 * j + tb for tb in range(4) for j in range(chips)])
    freq = np.arange(blocks) + 0.5
    lane = np.arange(LANES)
    angle = 2.0 * math.pi * freq[:, None] * order[None, :] / (2 * blocks)
    first = np.concatenate([np.cos(angle), -np.sin(angle)], axis=0)
    turn = 2.0 * math.pi * freq[:, None] * lane[None, :] / period
    inner = 2.0 * math.pi * ((lane[:, None] * lane[None, :]) % LANES) / LANES
    cosine, sine = np.cos(inner), np.sin(inner)
    middle = np.block([[cosine, -sine], [sine, cosine]])
    last = first.T * (2.0 / period)

    def parts(table, axis):
        high = table.astype(ml_dtypes.bfloat16)
        low = (table - high.astype(np.float64)).astype(ml_dtypes.bfloat16)
        return np.concatenate([high, low, high], axis=axis)

    return (
        parts(first, 1),
        parts(middle, 0),
        parts(middle.T, 0),
        parts(last, 1),
        np.cos(turn).astype(np.float32),
        np.sin(turn).astype(np.float32),
    )


def matmul(left, right, dims=((1,), (0,))):
    return lax.dot_general(left, right, (dims, ((), ())), preferred_element_type=F32)


def split(value):
    high = value.astype(BF16)
    low = (value - high.astype(F32)).astype(BF16)
    return high, low


def greet(me, peers, group, groups):
    barrier = pltpu.get_barrier_semaphore()

    def one(step, carry):
        pl.semaphore_signal(
            barrier, inc=1, device_id=(lax.rem(me + step, peers), group), device_id_type=MESH
        )
        return carry

    lax.fori_loop(1, peers, one, 0)
    for step in range(1, groups):
        pl.semaphore_signal(
            barrier, inc=1, device_id=(me, lax.rem(group + step, groups)), device_id_type=MESH
        )
    return barrier


def wait_bytes(ref, sem):
    pltpu.make_async_copy(ref, ref, sem).wait()


def send(src, dst, sem_out, sem_in, seq, chan):
    pltpu.make_async_remote_copy(
        src_ref=src, dst_ref=dst, send_sem=sem_out, recv_sem=sem_in,
        device_id=(seq, chan), device_id_type=MESH,
    ).start()


def layer_kernel(
    n, groups, x_ref, w_ref, filters_ref, cot_ref, bias_ref,
    first_ref, middle_ref, middle_t_ref, last_ref, cos_ref, sin_ref,
    b_back, w_own, w_far, u_own, u_recv,
    wg, w_other, xg, xt, total, stage_a, a_send, a_recv, stage_b, b_send, b_recv,
    spec_h1, spec_h2, spec_v, spec_z, spec_g1, spec_g2,
    stage_c, g_send, g_recv, stage_d, b_give, turned_ref, grad, grad_in,
    w_send, w_in, w_relay, u_acc, u_send,
    sems, x_sems, xp_sems, u_sems, gs_sems, g_sems, c_sems, ws_sems, w_sems, bs_sems, b_sems,
):
    me = lax.axis_index("seq")
    group = lax.axis_index("chan")
    core = lax.rem(me, 2)
    chip = me // 2
    partner = me + 1 - 2 * core
    chips = n // 2
    ny = min(4, chips // 2)
    nx = chips // (2 * ny)
    plane = nx * ny
    y = lax.rem(chip, ny)
    zl = lax.rem(chip // ny, 2)
    xx = chip // (2 * ny)
    here = (xx * ny + y) * 2 + core
    quota = LANES // chips
    blocks = 4 * chips
    rows_a, rows_b = a_send.shape[1], b_send.shape[1]
    rows_c = 4 * quota
    tokens, depth = x_ref.shape
    cols = wg.shape[2]
    slots = depth // wg.shape[1]

    def in_plane(p, c, z):
        return (((p // ny) * 2 + z) * ny + lax.rem(p, ny)) * 2 + c

    barrier = greet(me, n, group, groups)

    def spread(value, base):
        turned = value.T
        for half in range(2):
            for q in range(quota):
                top = half * LANES + q * chips
                for tb in range(2):
                    stage_b[pl.ds(half * rows_b + base + q * 2 + tb, chips, stride=2 * rows_b), :] = turned[
                        top : top + chips, tb * LANES : (tb + 1) * LANES
                    ]

    spread(filters_ref[0], 0)
    spread(filters_ref[1], 2 * quota)
    spread(cot_ref[...].astype(F32), 4 * quota)
    for peer in range(n):
        stage_b[pl.ds(peer * rows_b + 6 * quota, 2 * quota), :] = jnp.zeros((2 * quota, LANES), F32)
    b_send[...] = stage_b[...].astype(BF16).reshape(b_send.shape)
    xg[core, group] = x_ref[...]
    pl.semaphore_wait(barrier, n - 1 + groups - 1)

    near = [step for step in range(1, groups) if min(step, groups - step) == 1]
    far = [step for step in range(1, groups) if min(step, groups - step) > 1]
    for step in far + near:
        send(x_ref, xg.at[core, group], sems.at[2], x_sems.at[group], me, lax.rem(group + step, groups))
    z_first = in_plane(xx * ny + y, 0, 1 - zl)
    for c in range(2):
        send(w_ref.at[c], wg.at[me], sems.at[0], sems.at[3], z_first + c, group)

    def send_w(step, carry):
        peer = lax.rem(here + step, 2 * plane)
        c = lax.rem(peer, 2)
        send(w_ref.at[c], wg.at[me], sems.at[0], sems.at[1], in_plane(peer // 2, c, zl), group)
        return carry

    lax.fori_loop(1, 2 * plane, send_w, 0)
    pltpu.make_async_copy(w_ref.at[core], wg.at[me], sems.at[1]).start()
    send(x_ref, xg.at[core, group], sems.at[2], xp_sems.at[group], partner, group)
    wait_bytes(wg.at[pl.ds(z_first, 2)], sems.at[3])

    def forward_w(step, carry):
        p = lax.rem(here // 2 + step, plane)
        part = wg.at[pl.ds(z_first, 2)]
        send(part, part, sems.at[4], sems.at[5], in_plane(p, core, zl), group)
        return carry

    lax.fori_loop(1, plane, forward_w, 0)

    def relay(step):
        other = lax.rem(group + groups - step, groups)
        wait_bytes(xg.at[core, other], x_sems.at[other])
        part = xg.at[core, other]
        send(part, part, sems.at[6], xp_sems.at[other], partner, group)

    for step in near:
        relay(step)
    wait_bytes(wg.at[pl.ds(0, 2 * plane)], sems.at[1])
    wait_bytes(wg.at[pl.ds(0, 2 * plane - 2)], sems.at[5])
    send(wg, w_other, sems.at[7], sems.at[8], partner, group)

    def give_b(step, carry):
        peer = lax.rem(me + step, n)
        send(b_send.at[peer], b_recv.at[me], sems.at[9], sems.at[10], peer, group)
        return carry

    lax.fori_loop(1, n, give_b, 0)
    pltpu.make_async_copy(b_send.at[me], b_recv.at[me], sems.at[10]).start()

    def weights(ref, c):
        return ref[pl.ds(c * slots, slots)].reshape(depth, cols)

    def project(side, step):
        other = lax.rem(group + groups - step, groups)
        if side == 1:
            wait_bytes(xg.at[1 - core, other], xp_sems.at[other])
        at = core if side == 0 else 1 - core
        term = matmul(xg[at, other], weights(wg, other))
        total[at] = term if step == 0 else total[at] + term

    for step in [0] + near:
        project(0, step)
    for step in [0] + near:
        project(1, step)
    for step in far:
        relay(step)
        project(0, step)
    for step in far:
        project(1, step)
    turned = total[...].reshape(2 * tokens, cols).T
    for a in range(3):
        for q in range(quota):
            top = a * LANES + q * chips
            for tb in range(4):
                stage_a[pl.ds((a * quota + q) * 4 + tb, chips, stride=rows_a), :] = turned[
                    top : top + chips, tb * LANES : (tb + 1) * LANES
                ]
    a_send[...] = stage_a[...].astype(BF16).reshape(a_send.shape)

    def give_a(step, carry):
        peer = lax.rem(chip + step, chips)
        send(a_send.at[peer], a_recv.at[chip], sems.at[11], sems.at[12], 2 * peer + core, group)
        return carry

    lax.fori_loop(1, chips, give_a, 0)
    pltpu.make_async_copy(a_send.at[chip], a_recv.at[chip], sems.at[12]).start()

    def columns(ref, start, stride):
        return jnp.concatenate(
            [
                jnp.concatenate(
                    [ref[pl.ds(start(q, tb), chips, stride=stride), :] for q in range(quota)], axis=1
                )
                for tb in range(4)
            ],
            axis=0,
        )

    def late(a):
        return columns(stage_a, lambda q, tb: (a * quota + q) * 4 + tb, rows_a)

    def early(base):
        return columns(stage_b, lambda q, tb: (tb // 2) * rows_b + base + q * 2 + tb % 2, 2 * rows_b)

    def piece(value, q):
        return value[:, q * LANES : (q + 1) * LANES]

    def forward(value, spec, exact=False):
        high, low = split(value)
        if exact:
            wide = matmul(first_ref[:, : 2 * blocks], jnp.concatenate([high, high], axis=0))
        else:
            wide = matmul(first_ref[...], jnp.concatenate([high, high, low], axis=0))
        turn_cos, turn_sin = cos_ref[...], sin_ref[...]
        for q in range(quota):
            re = piece(wide[:blocks], q)
            im = piece(wide[blocks:], q)
            high, low = split(
                jnp.concatenate([re * turn_cos + im * turn_sin, im * turn_cos - re * turn_sin], axis=1)
            )
            spec[q * blocks : (q + 1) * blocks, :] = matmul(
                jnp.concatenate([high, high, low], axis=1), middle_ref[...]
            )

    def backward(left, right, conj_left, conj_right):
        turn_cos, turn_sin = cos_ref[...], sin_ref[...]
        columns_high, columns_low = [], []
        for q in range(quota):
            rows = slice(q * blocks, (q + 1) * blocks)
            l_re, l_im = left[rows, :LANES], left[rows, LANES:]
            r_re, r_im = right[rows, :LANES], right[rows, LANES:]
            cross = l_im * r_im
            y_re = l_re * r_re - (cross if conj_left == conj_right else -cross)
            if conj_left:
                y_im = l_re * r_im - l_im * r_re
            elif conj_right:
                y_im = l_im * r_re - l_re * r_im
            else:
                y_im = l_re * r_im + l_im * r_re
            high, low = split(jnp.concatenate([y_re, y_im], axis=1))
            out = matmul(jnp.concatenate([high, high, low], axis=1), middle_t_ref[...])
            re, im = out[:, :LANES], out[:, LANES:]
            high, low = split(
                jnp.concatenate([re * turn_cos - im * turn_sin, im * turn_cos + re * turn_sin], axis=0)
            )
            columns_high.append(high)
            columns_low.append(low)
        high = jnp.concatenate(columns_high, axis=1)
        low = jnp.concatenate(columns_low, axis=1)
        return matmul(last_ref[...], jnp.concatenate([high, high, low], axis=0))

    def skip(f):
        return jnp.concatenate(
            [
                jnp.full((1, LANES), bias_ref[f, core * LANES + q * chips + chip], F32)
                for q in range(quota)
            ],
            axis=1,
        )

    def give_late(value, a):
        for q in range(quota):
            for tb in range(4):
                stage_c[pl.ds(q * 4 + tb, chips, stride=rows_c), :] = piece(value, q)[
                    tb * chips : (tb + 1) * chips
                ]
        g_send[a] = stage_c[...].astype(BF16).reshape(chips, rows_c, LANES)

        def one(step, carry):
            peer = lax.rem(chip + step, chips)
            send(g_send.at[a, peer], g_recv.at[a, chip], gs_sems.at[a], g_sems.at[a], 2 * peer + core, group)
            return carry

        lax.fori_loop(1, chips, one, 0)
        pltpu.make_async_copy(g_send.at[a, chip], g_recv.at[a, chip], g_sems.at[a]).start()

    def put_early(value, base):
        for q in range(quota):
            for tb in range(4):
                at = (tb // 2) * rows_c + base + q * 2 + tb % 2
                stage_d[pl.ds(at, chips, stride=2 * rows_c), :] = piece(value, q)[
                    tb * chips : (tb + 1) * chips
                ]

    def put_skip(product, f):
        lane = lax.broadcasted_iota(jnp.int32, (1, LANES), 1)
        sums = jnp.sum(product, axis=0, keepdims=True)
        for q in range(quota):
            value = jnp.sum(piece(sums, q), axis=1, keepdims=True)
            one = value.astype(BF16).astype(F32)
            two = (value - one).astype(BF16).astype(F32)
            three = value - one - two
            row = jnp.where(lane == chip, one, 0.0)
            row = jnp.where(lane == chips + chip, two, row)
            row = jnp.where(lane == 2 * chips + chip, three, row)
            for half in range(2):
                at = half * rows_c + 2 * quota + f * quota + q
                stage_d[pl.ds(at, chips, stride=2 * rows_c), :] = jnp.broadcast_to(row, (chips, LANES))

    def give_early(k):
        b_give[k] = stage_d[...].astype(BF16).reshape(n, rows_c, LANES)

        def one(step, carry):
            peer = lax.rem(me + step, n)
            send(b_give.at[k, peer], b_back.at[k, me], bs_sems.at[k], b_sems.at[k], peer, group)
            return carry

        lax.fori_loop(1, n, one, 0)
        pltpu.make_async_copy(b_give.at[k, me], b_back.at[k, me], b_sems.at[k]).start()

    wait_bytes(b_recv, sems.at[10])
    stage_b[...] = b_recv[...].reshape(stage_b.shape).astype(F32)
    forward(early(0), spec_h1, True)
    forward(early(2 * quota), spec_h2, True)
    for c in range(groups):
        xt[c] = xg[:, c].reshape(2 * tokens, depth).astype(F32).T.astype(BF16)
    wait_bytes(a_recv, sems.at[12])
    stage_a[...] = a_recv[...].reshape(stage_a.shape).astype(F32)
    values_v, gate_one, gate_two = late(0), late(1), late(2)
    grad_out = early(4 * quota)
    skip_one, skip_two = skip(0), skip(1)
    forward(values_v, spec_v, True)
    conv_one = backward(spec_h1, spec_v, False, False) + skip_one * values_v
    mixed = gate_one * conv_one
    grad_conv_two = grad_out * gate_two
    forward(grad_conv_two, spec_g2)
    grad_mixed = backward(spec_h2, spec_g2, True, False) + skip_two * grad_conv_two
    give_late(grad_mixed * conv_one, 1)
    grad_conv_one = grad_mixed * gate_one
    forward(grad_conv_one, spec_g1)
    give_late(backward(spec_h1, spec_g1, True, False) + skip_one * grad_conv_one, 0)
    forward(mixed, spec_z)
    conv_two = backward(spec_h2, spec_z, False, False) + skip_two * mixed
    give_late(grad_out * conv_two, 2)
    put_early(gate_two * conv_two, 0)
    put_early(backward(spec_g2, spec_z, False, True), 2 * quota)
    give_early(0)
    put_early(backward(spec_g1, spec_v, False, True), 0)
    put_skip(grad_conv_one * values_v, 0)
    put_skip(grad_conv_two * mixed, 1)
    give_early(1)

    def take(a):
        wait_bytes(g_recv.at[a], g_sems.at[a])
        stage_c[...] = g_recv[a].reshape(stage_c.shape).astype(F32)
        for q in range(quota):
            for tb in range(4):
                turned_ref[q * chips : (q + 1) * chips, tb * LANES : (tb + 1) * LANES] = stage_c[
                    pl.ds(q * 4 + tb, chips, stride=rows_c), :
                ]
        grad[a] = turned_ref[...].T.astype(BF16).reshape(2, tokens, LANES)
        send(grad.at[a, 1 - core], grad_in.at[a], sems.at[13], c_sems.at[a], partner, group)

    def give_w(a):
        block = grad[a].reshape(2 * tokens, LANES)
        per = n // groups
        for c in range(groups):
            term = matmul(xt[c], block).astype(BF16).reshape(slots, depth // slots, LANES)
            for k in range(slots):
                s = c * slots + k
                w_send[a, s // (4 * ny), (s // (2 * ny)) % 2, s % (2 * ny)] = term[k]

        def one(step, carry):
            peer = lax.rem(here + step, 2 * plane)
            p, c = peer // 2, lax.rem(peer, 2)
            send(
                w_send.at[a, p // ny, :, lax.rem(p, ny) * 2 + c], w_in.at[a, here],
                ws_sems.at[a], w_sems.at[a], in_plane(p, c, zl), group,
            )
            return carry

        lax.fori_loop(1, 2 * plane, one, 0)
        pltpu.make_async_copy(w_send.at[a, xx, :, y * 2 + core], w_in.at[a, here], w_sems.at[a]).start()

    def both(arrays, c):
        left = jnp.concatenate([part for a in arrays for part in (grad[a, core], grad_in[a])], axis=1)
        wide = [weights(wg, c), weights(w_other, c)]
        right = jnp.concatenate([piece(part, a) for a in arrays for part in wide], axis=1)
        return matmul(left, right, ((1,), (1,)))

    take(1)
    give_w(1)
    take(0)
    give_w(0)
    wait_bytes(w_other, sems.at[8])
    for a in (1, 0):
        wait_bytes(grad_in.at[a], c_sems.at[a])
    for c in range(groups):
        u_acc[c] = both((1, 0), c)
    take(2)
    wait_bytes(grad_in.at[2], c_sems.at[2])
    for c in range(groups):
        value = u_acc[c] + both((2,), c)
        u_acc[c] = value
        u_send[c] = value.astype(BF16)
    for step in far + near:
        other = lax.rem(group + step, groups)
        send(u_send.at[other], u_recv.at[group], sems.at[14], u_sems.at[group], me, other)
    give_w(2)
    u_own[...] = u_acc[group]

    z_device = z_first + core
    for a in (1, 0, 2):
        wait_bytes(w_in.at[a], w_sems.at[a])
        for half in range(2):
            own = w_in[a, half, zl].astype(F32)
            away = w_in[a, half, 1 - zl].astype(F32)
            for p in range(1, plane):
                own = own + w_in[a, 2 * p + half, zl].astype(F32)
                away = away + w_in[a, 2 * p + half, 1 - zl].astype(F32)
            w_own[a, half] = own
            w_relay[a, half] = away
        send(w_relay.at[a], w_far.at[a], sems.at[15], sems.at[16], z_device, group)

    wait_bytes(b_back.at[0], b_sems.at[0])
    wait_bytes(b_back.at[1], b_sems.at[1])
    for step in near + far:
        other = lax.rem(group + groups - step, groups)
        wait_bytes(u_recv.at[other], u_sems.at[other])
    wait_bytes(w_far, sems.at[16])
    wait_bytes(wg.at[pl.ds(0, 2 * plane + 1)], sems.at[0])
    wait_bytes(xg.at[0], sems.at[2])
    wait_bytes(wg.at[pl.ds(0, 2 * plane - 2)], sems.at[4])
    if groups > 1:
        wait_bytes(xg.at[0, pl.ds(0, groups - 1)], sems.at[6])
        wait_bytes(u_recv.at[pl.ds(0, groups - 1)], sems.at[14])
    wait_bytes(wg, sems.at[7])
    wait_bytes(b_recv.at[pl.ds(0, n - 1)], sems.at[9])
    wait_bytes(a_recv.at[pl.ds(0, chips - 1)], sems.at[11])
    wait_bytes(grad_in, sems.at[13])
    wait_bytes(w_far, sems.at[15])
    for a in range(3):
        wait_bytes(g_recv.at[a, pl.ds(0, chips - 1)], gs_sems.at[a])
        wait_bytes(w_in.at[a, pl.ds(0, 2 * plane - 1)], ws_sems.at[a])
    for k in range(2):
        wait_bytes(b_back.at[k, pl.ds(0, n - 1)], bs_sems.at[k])


def finish_kernel(
    n, groups, b_back, w_own, w_far, u_own, u_recv, out_ref, gu_ref, gw_ref, gf_ref, gb_ref, stage, turned_ref
):
    group = lax.axis_index("chan")
    chips = n // 2
    quota = LANES // chips
    rows_c = 4 * quota

    def collect(k, base):
        for half in range(2):
            for q in range(quota):
                top = half * LANES + q * chips
                for tb in range(2):
                    turned_ref[top : top + chips, tb * LANES : (tb + 1) * LANES] = stage[
                        k, pl.ds(half * rows_c + base + q * 2 + tb, chips, stride=2 * rows_c), :
                    ]
        return turned_ref[...].T

    stage[...] = b_back[...].reshape(stage.shape).astype(F32)
    out_ref[...] = collect(0, 0).astype(BF16)
    gf_ref[1] = collect(0, 2 * quota)
    gf_ref[0] = collect(1, 0)
    lane = lax.broadcasted_iota(jnp.int32, (1, LANES), 1)
    for f in range(2):
        for half in range(2):
            line = jnp.zeros((1, LANES), F32)
            for q in range(quota):
                at = half * rows_c + 2 * quota + f * quota + q
                row = jnp.sum(stage[1, pl.ds(at, chips, stride=2 * rows_c), :], axis=0, keepdims=True)
                full = row + pltpu.roll(row, LANES - chips, 1) + pltpu.roll(row, LANES - 2 * chips, 1)
                moved = full if q == 0 else pltpu.roll(full, q * chips, 1)
                line = jnp.where((lane >= q * chips) & (lane < (q + 1) * chips), moved, line)
            gb_ref[f : f + 1, half * LANES : (half + 1) * LANES] = line
    total = u_own[...]
    for step in range(1, groups):
        total = total + u_recv[lax.rem(group + step, groups)].astype(F32)
    gu_ref[...] = total.astype(BF16)
    for a in range(3):
        for half in range(2):
            gw_ref[:, a, half * LANES : (half + 1) * LANES] = w_own[a, half] + w_far[a, half]


def on_device(layer_input, w_in, filters, bias, cotangent):
    n = lax.axis_size("seq")
    groups = lax.axis_size("chan")
    tokens, width = layer_input.shape
    rows = w_in.shape[0]
    chips = n // 2
    ny = min(4, chips // 2)
    nx = chips // (2 * ny)
    plane = nx * ny
    quota = LANES // chips
    blocks = 4 * chips
    rows_a, rows_b, rows_c = 12 * quota, 8 * quota, 4 * quota
    cols = 3 * LANES
    vmem = pl.BlockSpec(memory_space=pltpu.VMEM)
    smem = pl.BlockSpec(memory_space=pltpu.SMEM)
    sds = jax.ShapeDtypeStruct
    dma = pltpu.SemaphoreType.DMA
    limit = 58 * 1024 * 1024
    spec = pltpu.VMEM((quota * blocks, 2 * LANES), F32)

    w_halves = w_in.reshape(rows, 3, 2, LANES).transpose(2, 0, 1, 3).reshape(2, rows, cols)
    landed = pl.pallas_call(
        functools.partial(layer_kernel, n, groups),
        out_shape=(
            sds((2, n, rows_c, LANES), BF16),
            sds((3, 2, rows, LANES), F32),
            sds((3, 2, rows, LANES), F32),
            sds((tokens, width), F32),
            sds((groups, tokens, width), BF16),
        ),
        in_specs=[vmem] * 4 + [smem] + [vmem] * 6,
        out_specs=(vmem,) * 5,
        scratch_shapes=[
            pltpu.VMEM((n, rows, cols), BF16),
            pltpu.VMEM((n, rows, cols), BF16),
            pltpu.VMEM((2, groups, tokens, width), BF16),
            pltpu.VMEM((groups, width, 2 * tokens), BF16),
            pltpu.VMEM((2, tokens, cols), F32),
            pltpu.VMEM((chips * rows_a, LANES), F32),
            pltpu.VMEM((chips, rows_a, LANES), BF16),
            pltpu.VMEM((chips, rows_a, LANES), BF16),
            pltpu.VMEM((n * rows_b, LANES), F32),
            pltpu.VMEM((n, rows_b, LANES), BF16),
            pltpu.VMEM((n, rows_b, LANES), BF16),
            spec, spec, spec, spec, spec, spec,
            pltpu.VMEM((chips * rows_c, LANES), F32),
            pltpu.VMEM((3, chips, rows_c, LANES), BF16),
            pltpu.VMEM((3, chips, rows_c, LANES), BF16),
            pltpu.VMEM((n * rows_c, LANES), F32),
            pltpu.VMEM((2, n, rows_c, LANES), BF16),
            pltpu.VMEM((LANES, 2 * tokens), F32),
            pltpu.VMEM((3, 2, tokens, LANES), BF16),
            pltpu.VMEM((3, tokens, LANES), BF16),
            pltpu.VMEM((3, nx, 2, 2 * ny, rows, LANES), BF16),
            pltpu.VMEM((3, 2 * plane, 2, rows, LANES), BF16),
            pltpu.VMEM((3, 2, rows, LANES), F32),
            pltpu.VMEM((groups, tokens, width), F32),
            pltpu.VMEM((groups, tokens, width), BF16),
            dma((17,)),
            dma((groups,)), dma((groups,)), dma((groups,)),
            dma((3,)), dma((3,)), dma((3,)), dma((3,)), dma((3,)),
            dma((2,)), dma((2,)),
        ],
        compiler_params=pltpu.CompilerParams(
            collective_id=0, has_side_effects=True, vmem_limit_bytes=limit
        ),
        name="layer",
    )(layer_input, w_halves, filters, cotangent, bias, *(jnp.asarray(table) for table in tables(blocks)))

    return pl.pallas_call(
        functools.partial(finish_kernel, n, groups),
        out_shape=(
            sds((tokens, width), BF16),
            sds((tokens, width), BF16),
            sds((rows, 3, width), F32),
            sds((2, tokens, width), F32),
            sds((2, width), F32),
        ),
        in_specs=[vmem] * 5,
        out_specs=(vmem,) * 5,
        scratch_shapes=[
            pltpu.VMEM((2, n * rows_c, LANES), F32),
            pltpu.VMEM((2 * LANES, tokens), F32),
        ],
        compiler_params=pltpu.CompilerParams(vmem_limit_bytes=limit // 4),
        name="finish",
    )(*landed)


def solution(mesh):
    in_specs = (
        P("seq", "chan"),
        P("seq", None, "chan"),
        P(None, "seq", "chan"),
        P(None, "chan"),
        P("seq", "chan"),
    )
    out_specs = (
        P("seq", "chan"),
        P("seq", "chan"),
        P("seq", None, "chan"),
        P(None, "seq", "chan"),
        P(None, "chan"),
    )
    return jax.shard_map(
        on_device, mesh=mesh, in_specs=in_specs, out_specs=out_specs, check_vma=False
    )
```

```python
import functools
import math

import jax
import jax.numpy as jnp
import ml_dtypes
import numpy as np
from jax import lax
from jax.experimental import pallas as pl
from jax.experimental.pallas import tpu as pltpu
from jax.sharding import PartitionSpec as P

MESH = pl.DeviceIdType.MESH
LANES = 128
BF16 = jnp.bfloat16
F32 = jnp.float32


def tables(blocks):
    period = 2 * blocks * LANES
    chips = blocks // 4
    order = np.array([4 * j + tb for tb in range(4) for j in range(chips)])
    freq = np.arange(blocks) + 0.5
    lane = np.arange(LANES)
    angle = 2.0 * math.pi * freq[:, None] * order[None, :] / (2 * blocks)
    first = np.concatenate([np.cos(angle), -np.sin(angle)], axis=0)
    turn = 2.0 * math.pi * freq[:, None] * lane[None, :] / period
    inner = 2.0 * math.pi * ((lane[:, None] * lane[None, :]) % LANES) / LANES
    cosine, sine = np.cos(inner), np.sin(inner)
    middle = np.block([[cosine, -sine], [sine, cosine]])
    last = first.T * (2.0 / period)

    def parts(table, axis):
        high = table.astype(ml_dtypes.bfloat16)
        low = (table - high.astype(np.float64)).astype(ml_dtypes.bfloat16)
        return np.concatenate([high, low, high], axis=axis)

    return (
        parts(first, 1),
        parts(middle, 0),
        parts(middle.T, 0),
        parts(last, 1),
        np.cos(turn).astype(np.float32),
        np.sin(turn).astype(np.float32),
    )


def matmul(left, right, dims=((1,), (0,))):
    return lax.dot_general(left, right, (dims, ((), ())), preferred_element_type=F32)


def split(value):
    high = value.astype(BF16)
    low = (value - high.astype(F32)).astype(BF16)
    return high, low


def greet(me, peers, group, groups):
    barrier = pltpu.get_barrier_semaphore()

    def one(step, carry):
        pl.semaphore_signal(
            barrier, inc=1, device_id=(lax.rem(me + step, peers), group), device_id_type=MESH
        )
        return carry

    lax.fori_loop(1, peers, one, 0)
    for step in range(1, groups):
        pl.semaphore_signal(
            barrier, inc=1, device_id=(me, lax.rem(group + step, groups)), device_id_type=MESH
        )
    return barrier


def wait_bytes(ref, sem):
    pltpu.make_async_copy(ref, ref, sem).wait()


def send(src, dst, sem_out, sem_in, seq, chan):
    pltpu.make_async_remote_copy(
        src_ref=src, dst_ref=dst, send_sem=sem_out, recv_sem=sem_in,
        device_id=(seq, chan), device_id_type=MESH,
    ).start()


def layer_kernel(
    n, groups, x_ref, w_in_ref, filters_ref, cot_ref, bias_ref,
    first_ref, middle_ref, middle_t_ref, last_ref, cos_ref, sin_ref,
    b_back, w_own, w_far, u_own, u_recv,
    w_ref, wg, w_other, xg, xt, total, stage_a, a_send, a_recv, stage_b, b_send, b_recv,
    spec_h1, spec_h2, spec_v, spec_z, spec_g1, spec_g2,
    stage_c, g_send, g_recv, stage_d, b_give, turned_ref, grad, grad_in,
    w_send, w_in, w_relay, u_acc, u_send,
    sems, x_sems, xp_sems, xr_sems, u_sems, gs_sems, g_sems, cs_sems, c_sems, bs_sems, b_sems, ws_sems, w_sems,
):
    me = lax.axis_index("seq")
    group = lax.axis_index("chan")
    core = lax.rem(me, 2)
    chip = me // 2
    partner = me + 1 - 2 * core
    chips = n // 2
    ny = min(4, chips // 2)
    nx = chips // (2 * ny)
    plane = nx * ny
    y = lax.rem(chip, ny)
    zl = lax.rem(chip // ny, 2)
    xx = chip // (2 * ny)
    here = (xx * ny + y) * 2 + core
    quota = LANES // chips
    blocks = 4 * chips
    rows_a, rows_b = a_send.shape[1], b_send.shape[1]
    rows_c = 4 * quota
    tokens, depth = x_ref.shape
    cols = wg.shape[2]
    slots = depth // wg.shape[1]

    def in_plane(p, c, z):
        return (((p // ny) * 2 + z) * ny + lax.rem(p, ny)) * 2 + c

    pending = {}

    def expect(key, ref, sem):
        pending[key] = (ref, sem)

    def arrive(*key):
        wait_bytes(*pending.pop(key))

    barrier = greet(me, n, group, groups)

    for half in range(2):
        for a in range(3):
            w_ref[half, :, a * LANES : (a + 1) * LANES] = w_in_ref[a, :, half * LANES : (half + 1) * LANES]

    def spread(value, base):
        turned = value.T
        for half in range(2):
            for q in range(quota):
                top = half * LANES + q * chips
                for tb in range(2):
                    stage_b[pl.ds(half * rows_b + base + q * 2 + tb, chips, stride=2 * rows_b), :] = turned[
                        top : top + chips, tb * LANES : (tb + 1) * LANES
                    ]

    spread(filters_ref[0], 0)
    spread(filters_ref[1], 2 * quota)
    spread(cot_ref[...].astype(F32), 4 * quota)
    for peer in range(n):
        stage_b[pl.ds(peer * rows_b + 6 * quota, 2 * quota), :] = jnp.zeros((2 * quota, LANES), F32)
    b_send[...] = stage_b[...].astype(BF16).reshape(b_send.shape)
    xg[core, group] = x_ref[...]
    pl.semaphore_wait(barrier, n - 1 + groups - 1)

    near = [step for step in range(1, groups) if min(step, groups - step) == 1]
    far = [step for step in range(1, groups) if min(step, groups - step) > 1]
    for step in far + near:
        send(x_ref, xg.at[core, group], sems.at[2], x_sems.at[group], me, lax.rem(group + step, groups))
    for step in range(1, groups):
        other = lax.rem(group + groups - step, groups)
        expect(("x", step), xg.at[core, other], x_sems.at[other])
    z_first = in_plane(xx * ny + y, 0, 1 - zl)
    for c in range(2):
        send(w_ref.at[c], wg.at[me], sems.at[0], sems.at[3], z_first + c, group)

    def send_w(step, carry):
        peer = lax.rem(here + step, 2 * plane)
        c = lax.rem(peer, 2)
        send(w_ref.at[c], wg.at[me], sems.at[0], sems.at[1], in_plane(peer // 2, c, zl), group)
        return carry

    lax.fori_loop(1, 2 * plane, send_w, 0)
    pltpu.make_async_copy(w_ref.at[core], wg.at[me], sems.at[1]).start()
    send(x_ref, xg.at[core, group], sems.at[2], xp_sems.at[group], partner, group)
    expect(("x out",), xg.at[0], sems.at[2])
    expect(("w",), wg.at[pl.ds(0, 2 * plane)], sems.at[1])
    expect(("w out",), wg.at[pl.ds(0, 2 * plane + 1)], sems.at[0])
    expect(("xp", 0), xg.at[1 - core, group], xp_sems.at[group])
    wait_bytes(wg.at[pl.ds(z_first, 2)], sems.at[3])

    def forward_w(step, carry):
        p = lax.rem(here // 2 + step, plane)
        part = wg.at[pl.ds(z_first, 2)]
        send(part, part, sems.at[4], sems.at[5], in_plane(p, core, zl), group)
        return carry

    lax.fori_loop(1, plane, forward_w, 0)
    expect(("w rest",), wg.at[pl.ds(0, 2 * plane - 2)], sems.at[5])
    expect(("w rest out",), wg.at[pl.ds(0, 2 * plane - 2)], sems.at[4])

    def relay(step):
        other = lax.rem(group + groups - step, groups)
        arrive("x", step)
        part = xg.at[core, other]
        send(part, part, xr_sems.at[step], xp_sems.at[other], partner, group)
        expect(("xp", step), xg.at[1 - core, other], xp_sems.at[other])
        expect(("x relay", step), xg.at[1 - core, other], xr_sems.at[step])

    for step in near:
        relay(step)
    arrive("w")
    arrive("w rest")
    send(wg, w_other, sems.at[7], sems.at[8], partner, group)
    expect(("other",), w_other, sems.at[8])
    expect(("other out",), w_other, sems.at[7])

    def give_b(step, carry):
        peer = lax.rem(me + step, n)
        send(b_send.at[peer], b_recv.at[me], sems.at[9], sems.at[10], peer, group)
        return carry

    lax.fori_loop(1, n, give_b, 0)
    pltpu.make_async_copy(b_send.at[me], b_recv.at[me], sems.at[10]).start()
    expect(("b",), b_recv, sems.at[10])
    expect(("b out",), b_recv.at[pl.ds(0, n - 1)], sems.at[9])

    def weights(ref, c):
        return ref[pl.ds(c * slots, slots)].reshape(depth, cols)

    def project(side, step):
        other = lax.rem(group + groups - step, groups)
        if side == 1:
            arrive("xp", step)
        at = core if side == 0 else 1 - core
        term = matmul(xg[at, other], weights(wg, other))
        total[at] = term if step == 0 else total[at] + term

    for step in [0] + near:
        project(0, step)
    for step in [0] + near:
        project(1, step)
    for step in far:
        relay(step)
        project(0, step)
    for step in far:
        project(1, step)
    turned = total[...].reshape(2 * tokens, cols).T
    for a in range(3):
        for q in range(quota):
            top = a * LANES + q * chips
            for tb in range(4):
                stage_a[pl.ds((a * quota + q) * 4 + tb, chips, stride=rows_a), :] = turned[
                    top : top + chips, tb * LANES : (tb + 1) * LANES
                ]
    a_send[...] = stage_a[...].astype(BF16).reshape(a_send.shape)

    def give_a(step, carry):
        peer = lax.rem(chip + step, chips)
        send(a_send.at[peer], a_recv.at[chip], sems.at[11], sems.at[12], 2 * peer + core, group)
        return carry

    lax.fori_loop(1, chips, give_a, 0)
    pltpu.make_async_copy(a_send.at[chip], a_recv.at[chip], sems.at[12]).start()
    expect(("a",), a_recv, sems.at[12])
    expect(("a out",), a_recv.at[pl.ds(0, chips - 1)], sems.at[11])

    def columns(ref, start, stride):
        return jnp.concatenate(
            [
                jnp.concatenate(
                    [ref[pl.ds(start(q, tb), chips, stride=stride), :] for q in range(quota)], axis=1
                )
                for tb in range(4)
            ],
            axis=0,
        )

    def late(a):
        return columns(stage_a, lambda q, tb: (a * quota + q) * 4 + tb, rows_a)

    def early(base):
        return columns(stage_b, lambda q, tb: (tb // 2) * rows_b + base + q * 2 + tb % 2, 2 * rows_b)

    def piece(value, q):
        return value[:, q * LANES : (q + 1) * LANES]

    def forward(value, spec, exact=False):
        high, low = split(value)
        if exact:
            wide = matmul(first_ref[:, : 2 * blocks], jnp.concatenate([high, high], axis=0))
        else:
            wide = matmul(first_ref[...], jnp.concatenate([high, high, low], axis=0))
        turn_cos, turn_sin = cos_ref[...], sin_ref[...]
        for q in range(quota):
            re = piece(wide[:blocks], q)
            im = piece(wide[blocks:], q)
            high, low = split(
                jnp.concatenate([re * turn_cos + im * turn_sin, im * turn_cos - re * turn_sin], axis=1)
            )
            spec[q * blocks : (q + 1) * blocks, :] = matmul(
                jnp.concatenate([high, high, low], axis=1), middle_ref[...]
            )

    def backward(left, right, conj_left, conj_right):
        turn_cos, turn_sin = cos_ref[...], sin_ref[...]
        columns_high, columns_low = [], []
        for q in range(quota):
            rows = slice(q * blocks, (q + 1) * blocks)
            l_re, l_im = left[rows, :LANES], left[rows, LANES:]
            r_re, r_im = right[rows, :LANES], right[rows, LANES:]
            cross = l_im * r_im
            y_re = l_re * r_re - (cross if conj_left == conj_right else -cross)
            if conj_left:
                y_im = l_re * r_im - l_im * r_re
            elif conj_right:
                y_im = l_im * r_re - l_re * r_im
            else:
                y_im = l_re * r_im + l_im * r_re
            high, low = split(jnp.concatenate([y_re, y_im], axis=1))
            out = matmul(jnp.concatenate([high, high, low], axis=1), middle_t_ref[...])
            re, im = out[:, :LANES], out[:, LANES:]
            high, low = split(
                jnp.concatenate([re * turn_cos - im * turn_sin, im * turn_cos + re * turn_sin], axis=0)
            )
            columns_high.append(high)
            columns_low.append(low)
        high = jnp.concatenate(columns_high, axis=1)
        low = jnp.concatenate(columns_low, axis=1)
        return matmul(last_ref[...], jnp.concatenate([high, high, low], axis=0))

    def skip(f):
        return jnp.concatenate(
            [
                jnp.full((1, LANES), bias_ref[f, core * LANES + q * chips + chip], F32)
                for q in range(quota)
            ],
            axis=1,
        )

    def give_late(value, a):
        for q in range(quota):
            for tb in range(4):
                stage_c[pl.ds(q * 4 + tb, chips, stride=rows_c), :] = piece(value, q)[
                    tb * chips : (tb + 1) * chips
                ]
        g_send[a] = stage_c[...].astype(BF16).reshape(chips, rows_c, LANES)

        def one(step, carry):
            peer = lax.rem(chip + step, chips)
            send(g_send.at[a, peer], g_recv.at[a, chip], gs_sems.at[a], g_sems.at[a], 2 * peer + core, group)
            return carry

        lax.fori_loop(1, chips, one, 0)
        pltpu.make_async_copy(g_send.at[a, chip], g_recv.at[a, chip], g_sems.at[a]).start()
        expect(("g", a), g_recv.at[a], g_sems.at[a])
        expect(("g out", a), g_recv.at[a, pl.ds(0, chips - 1)], gs_sems.at[a])

    def put_early(value, base):
        for q in range(quota):
            for tb in range(4):
                at = (tb // 2) * rows_c + base + q * 2 + tb % 2
                stage_d[pl.ds(at, chips, stride=2 * rows_c), :] = piece(value, q)[
                    tb * chips : (tb + 1) * chips
                ]

    def put_skip(product, f):
        lane = lax.broadcasted_iota(jnp.int32, (1, LANES), 1)
        sums = jnp.sum(product, axis=0, keepdims=True)
        for q in range(quota):
            value = jnp.sum(piece(sums, q), axis=1, keepdims=True)
            one = value.astype(BF16).astype(F32)
            two = (value - one).astype(BF16).astype(F32)
            three = value - one - two
            row = jnp.where(lane == chip, one, 0.0)
            row = jnp.where(lane == chips + chip, two, row)
            row = jnp.where(lane == 2 * chips + chip, three, row)
            for half in range(2):
                at = half * rows_c + 2 * quota + f * quota + q
                stage_d[pl.ds(at, chips, stride=2 * rows_c), :] = jnp.broadcast_to(row, (chips, LANES))

    def give_early(k):
        b_give[k] = stage_d[...].astype(BF16).reshape(n, rows_c, LANES)

        def one(step, carry):
            peer = lax.rem(me + step, n)
            send(b_give.at[k, peer], b_back.at[k, me], bs_sems.at[k], b_sems.at[k], peer, group)
            return carry

        lax.fori_loop(1, n, one, 0)
        pltpu.make_async_copy(b_give.at[k, me], b_back.at[k, me], b_sems.at[k]).start()
        expect(("back", k), b_back.at[k], b_sems.at[k])
        expect(("back out", k), b_back.at[k, pl.ds(0, n - 1)], bs_sems.at[k])

    arrive("b")
    stage_b[...] = b_recv[...].reshape(stage_b.shape).astype(F32)
    forward(early(0), spec_h1, True)
    forward(early(2 * quota), spec_h2, True)
    for c in range(groups):
        xt[c] = xg[:, c].reshape(2 * tokens, depth).astype(F32).T.astype(BF16)
    arrive("a")
    stage_a[...] = a_recv[...].reshape(stage_a.shape).astype(F32)
    values_v, gate_one, gate_two = late(0), late(1), late(2)
    grad_out = early(4 * quota)
    skip_one, skip_two = skip(0), skip(1)
    forward(values_v, spec_v, True)
    conv_one = backward(spec_h1, spec_v, False, False) + skip_one * values_v
    mixed = gate_one * conv_one
    grad_conv_two = grad_out * gate_two
    forward(grad_conv_two, spec_g2)
    grad_mixed = backward(spec_h2, spec_g2, True, False) + skip_two * grad_conv_two
    give_late(grad_mixed * conv_one, 1)
    grad_conv_one = grad_mixed * gate_one
    forward(grad_conv_one, spec_g1)
    give_late(backward(spec_h1, spec_g1, True, False) + skip_one * grad_conv_one, 0)
    forward(mixed, spec_z)
    conv_two = backward(spec_h2, spec_z, False, False) + skip_two * mixed
    give_late(grad_out * conv_two, 2)
    put_early(gate_two * conv_two, 0)
    put_early(backward(spec_g2, spec_z, False, True), 2 * quota)
    give_early(0)
    put_early(backward(spec_g1, spec_v, False, True), 0)
    put_skip(grad_conv_one * values_v, 0)
    put_skip(grad_conv_two * mixed, 1)
    give_early(1)

    def take(a):
        arrive("g", a)
        stage_c[...] = g_recv[a].reshape(stage_c.shape).astype(F32)
        for q in range(quota):
            for tb in range(4):
                turned_ref[q * chips : (q + 1) * chips, tb * LANES : (tb + 1) * LANES] = stage_c[
                    pl.ds(q * 4 + tb, chips, stride=rows_c), :
                ]
        grad[a] = turned_ref[...].T.astype(BF16).reshape(2, tokens, LANES)
        send(grad.at[a, 1 - core], grad_in.at[a], cs_sems.at[a], c_sems.at[a], partner, group)
        expect(("grad", a), grad_in.at[a], c_sems.at[a])
        expect(("grad out", a), grad_in.at[a], cs_sems.at[a])

    def give_w(a):
        block = grad[a].reshape(2 * tokens, LANES)
        per = n // groups
        for c in range(groups):
            term = matmul(xt[c], block).astype(BF16).reshape(slots, depth // slots, LANES)
            for k in range(slots):
                s = c * slots + k
                w_send[a, s // (4 * ny), (s // (2 * ny)) % 2, s % (2 * ny)] = term[k]

        def one(step, carry):
            peer = lax.rem(here + step, 2 * plane)
            p, c = peer // 2, lax.rem(peer, 2)
            send(
                w_send.at[a, p // ny, :, lax.rem(p, ny) * 2 + c], w_in.at[a, here],
                ws_sems.at[a], w_sems.at[a], in_plane(p, c, zl), group,
            )
            return carry

        lax.fori_loop(1, 2 * plane, one, 0)
        pltpu.make_async_copy(w_send.at[a, xx, :, y * 2 + core], w_in.at[a, here], w_sems.at[a]).start()
        expect(("sum", a), w_in.at[a], w_sems.at[a])
        expect(("sum out", a), w_in.at[a, pl.ds(0, 2 * plane - 1)], ws_sems.at[a])

    def both(arrays, c):
        left = jnp.concatenate([part for a in arrays for part in (grad[a, core], grad_in[a])], axis=1)
        wide = [weights(wg, c), weights(w_other, c)]
        right = jnp.concatenate([piece(part, a) for a in arrays for part in wide], axis=1)
        return matmul(left, right, ((1,), (1,)))

    take(1)
    give_w(1)
    take(0)
    give_w(0)
    arrive("other")
    for a in (1, 0):
        arrive("grad", a)
    for c in range(groups):
        u_acc[c] = both((1, 0), c)
    take(2)
    arrive("grad", 2)
    for c in range(groups):
        value = u_acc[c] + both((2,), c)
        u_acc[c] = value
        u_send[c] = value.astype(BF16)
    for step in far + near:
        other = lax.rem(group + step, groups)
        send(u_send.at[other], u_recv.at[group], sems.at[14], u_sems.at[group], me, other)
    for step in range(1, groups):
        other = lax.rem(group + groups - step, groups)
        expect(("u", step), u_recv.at[other], u_sems.at[other])
    if groups > 1:
        expect(("u out",), u_recv.at[pl.ds(0, groups - 1)], sems.at[14])
    give_w(2)
    u_own[...] = u_acc[group]

    z_device = z_first + core
    for a in (1, 0, 2):
        arrive("sum", a)
        for half in range(2):
            own = w_in[a, half, zl].astype(F32)
            away = w_in[a, half, 1 - zl].astype(F32)
            for p in range(1, plane):
                own = own + w_in[a, 2 * p + half, zl].astype(F32)
                away = away + w_in[a, 2 * p + half, 1 - zl].astype(F32)
            w_own[a, half] = own
            w_relay[a, half] = away
        send(w_relay.at[a], w_far.at[a], ws_sems.at[3 + a], w_sems.at[3 + a], z_device, group)
        expect(("far", a), w_far.at[a], w_sems.at[3 + a])
        expect(("far out", a), w_far.at[a], ws_sems.at[3 + a])

    for key in list(pending):
        arrive(*key)


def finish_kernel(
    n, groups, b_back, w_own, w_far, u_own, u_recv, out_ref, gu_ref, gw_ref, gf_ref, gb_ref, stage, turned_ref
):
    group = lax.axis_index("chan")
    chips = n // 2
    quota = LANES // chips
    rows_c = 4 * quota

    def collect(k, base):
        for half in range(2):
            for q in range(quota):
                top = half * LANES + q * chips
                for tb in range(2):
                    turned_ref[top : top + chips, tb * LANES : (tb + 1) * LANES] = stage[
                        k, pl.ds(half * rows_c + base + q * 2 + tb, chips, stride=2 * rows_c), :
                    ]
        return turned_ref[...].T

    stage[...] = b_back[...].reshape(stage.shape).astype(F32)
    out_ref[...] = collect(0, 0).astype(BF16)
    gf_ref[1] = collect(0, 2 * quota)
    gf_ref[0] = collect(1, 0)
    lane = lax.broadcasted_iota(jnp.int32, (1, LANES), 1)
    for f in range(2):
        for half in range(2):
            line = jnp.zeros((1, LANES), F32)
            for q in range(quota):
                at = half * rows_c + 2 * quota + f * quota + q
                row = jnp.sum(stage[1, pl.ds(at, chips, stride=2 * rows_c), :], axis=0, keepdims=True)
                full = row + pltpu.roll(row, LANES - chips, 1) + pltpu.roll(row, LANES - 2 * chips, 1)
                moved = full if q == 0 else pltpu.roll(full, q * chips, 1)
                line = jnp.where((lane >= q * chips) & (lane < (q + 1) * chips), moved, line)
            gb_ref[f : f + 1, half * LANES : (half + 1) * LANES] = line
    total = u_own[...]
    for step in range(1, groups):
        total = total + u_recv[lax.rem(group + step, groups)].astype(F32)
    gu_ref[...] = total.astype(BF16)
    for a in range(3):
        for half in range(2):
            gw_ref[a, :, half * LANES : (half + 1) * LANES] = w_own[a, half] + w_far[a, half]


def on_device(layer_input, w_in, filters, bias, cotangent):
    n = lax.axis_size("seq")
    groups = lax.axis_size("chan")
    tokens, width = layer_input.shape
    rows = w_in.shape[0]
    chips = n // 2
    ny = min(4, chips // 2)
    nx = chips // (2 * ny)
    plane = nx * ny
    quota = LANES // chips
    blocks = 4 * chips
    rows_a, rows_b, rows_c = 12 * quota, 8 * quota, 4 * quota
    cols = 3 * LANES
    vmem = pl.BlockSpec(memory_space=pltpu.VMEM)
    smem = pl.BlockSpec(memory_space=pltpu.SMEM)
    sds = jax.ShapeDtypeStruct
    dma = pltpu.SemaphoreType.DMA
    limit = 58 * 1024 * 1024
    spec = pltpu.VMEM((quota * blocks, 2 * LANES), F32)

    landed = pl.pallas_call(
        functools.partial(layer_kernel, n, groups),
        out_shape=(
            sds((2, n, rows_c, LANES), BF16),
            sds((3, 2, rows, LANES), F32),
            sds((3, 2, rows, LANES), F32),
            sds((tokens, width), F32),
            sds((groups, tokens, width), BF16),
        ),
        in_specs=[vmem] * 4 + [smem] + [vmem] * 6,
        out_specs=(vmem,) * 5,
        scratch_shapes=[
            pltpu.VMEM((2, rows, cols), BF16),
            pltpu.VMEM((n, rows, cols), BF16),
            pltpu.VMEM((n, rows, cols), BF16),
            pltpu.VMEM((2, groups, tokens, width), BF16),
            pltpu.VMEM((groups, width, 2 * tokens), BF16),
            pltpu.VMEM((2, tokens, cols), F32),
            pltpu.VMEM((chips * rows_a, LANES), F32),
            pltpu.VMEM((chips, rows_a, LANES), BF16),
            pltpu.VMEM((chips, rows_a, LANES), BF16),
            pltpu.VMEM((n * rows_b, LANES), F32),
            pltpu.VMEM((n, rows_b, LANES), BF16),
            pltpu.VMEM((n, rows_b, LANES), BF16),
            spec, spec, spec, spec, spec, spec,
            pltpu.VMEM((chips * rows_c, LANES), F32),
            pltpu.VMEM((3, chips, rows_c, LANES), BF16),
            pltpu.VMEM((3, chips, rows_c, LANES), BF16),
            pltpu.VMEM((n * rows_c, LANES), F32),
            pltpu.VMEM((2, n, rows_c, LANES), BF16),
            pltpu.VMEM((LANES, 2 * tokens), F32),
            pltpu.VMEM((3, 2, tokens, LANES), BF16),
            pltpu.VMEM((3, tokens, LANES), BF16),
            pltpu.VMEM((3, nx, 2, 2 * ny, rows, LANES), BF16),
            pltpu.VMEM((3, 2 * plane, 2, rows, LANES), BF16),
            pltpu.VMEM((3, 2, rows, LANES), F32),
            pltpu.VMEM((groups, tokens, width), F32),
            pltpu.VMEM((groups, tokens, width), BF16),
            dma((17,)),
            dma((groups,)), dma((groups,)), dma((groups,)), dma((groups,)),
            dma((3,)), dma((3,)), dma((3,)), dma((3,)),
            dma((2,)), dma((2,)), dma((6,)), dma((6,)),
        ],
        compiler_params=pltpu.CompilerParams(
            collective_id=0, has_side_effects=True, vmem_limit_bytes=limit
        ),
        name="layer",
    )(layer_input, w_in.transpose(1, 0, 2), filters, cotangent, bias, *(jnp.asarray(table) for table in tables(blocks)))

    out, grad_u, grad_w, grad_f, grad_b = pl.pallas_call(
        functools.partial(finish_kernel, n, groups),
        out_shape=(
            sds((tokens, width), BF16),
            sds((tokens, width), BF16),
            sds((3, rows, width), F32),
            sds((2, tokens, width), F32),
            sds((2, width), F32),
        ),
        in_specs=[vmem] * 5,
        out_specs=(vmem,) * 5,
        scratch_shapes=[
            pltpu.VMEM((2, n * rows_c, LANES), F32),
            pltpu.VMEM((2 * LANES, tokens), F32),
        ],
        compiler_params=pltpu.CompilerParams(vmem_limit_bytes=limit),
        name="finish",
    )(*landed)
    return (out, grad_u, grad_w.transpose(1, 0, 2), grad_f, grad_b)


def solution(mesh):
    in_specs = (
        P("seq", "chan"),
        P("seq", None, "chan"),
        P(None, "seq", "chan"),
        P(None, "chan"),
        P("seq", "chan"),
    )
    out_specs = (
        P("seq", "chan"),
        P("seq", "chan"),
        P("seq", None, "chan"),
        P(None, "seq", "chan"),
        P(None, "chan"),
    )
    return jax.shard_map(
        on_device, mesh=mesh, in_specs=in_specs, out_specs=out_specs, check_vma=False
    )
```

```python
import functools
import math

import jax
import jax.numpy as jnp
import ml_dtypes
import numpy as np
from jax import lax
from jax.experimental import pallas as pl
from jax.experimental.pallas import tpu as pltpu
from jax.sharding import PartitionSpec as P

MESH = pl.DeviceIdType.MESH
LANES = 128
BF16 = jnp.bfloat16
F32 = jnp.float32


def tables(blocks):
    period = 2 * blocks * LANES
    chips = blocks // 4
    order = np.array([4 * j + tb for tb in range(4) for j in range(chips)])
    freq = np.arange(blocks) + 0.5
    lane = np.arange(LANES)
    angle = 2.0 * math.pi * freq[:, None] * order[None, :] / (2 * blocks)
    first = np.concatenate([np.cos(angle), -np.sin(angle)], axis=0)
    turn = 2.0 * math.pi * freq[:, None] * lane[None, :] / period
    inner = 2.0 * math.pi * ((lane[:, None] * lane[None, :]) % LANES) / LANES
    cosine, sine = np.cos(inner), np.sin(inner)
    middle = np.block([[cosine, -sine], [sine, cosine]])
    last = first.T * (2.0 / period)

    def parts(table, axis):
        high = table.astype(ml_dtypes.bfloat16)
        low = (table - high.astype(np.float64)).astype(ml_dtypes.bfloat16)
        return np.concatenate([high, low, high], axis=axis)

    return (
        parts(first, 1),
        parts(middle, 0),
        parts(middle.T, 0),
        parts(last, 1),
        np.cos(turn).astype(np.float32),
        np.sin(turn).astype(np.float32),
    )


def matmul(left, right, dims=((1,), (0,))):
    return lax.dot_general(left, right, (dims, ((), ())), preferred_element_type=F32)


def split(value):
    high = value.astype(BF16)
    low = (value - high.astype(F32)).astype(BF16)
    return high, low


def greet(me, peers, group, groups):
    barrier = pltpu.get_barrier_semaphore()

    def one(step, carry):
        pl.semaphore_signal(
            barrier, inc=1, device_id=(lax.rem(me + step, peers), group), device_id_type=MESH
        )
        return carry

    lax.fori_loop(1, peers, one, 0)
    for step in range(1, groups):
        pl.semaphore_signal(
            barrier, inc=1, device_id=(me, lax.rem(group + step, groups)), device_id_type=MESH
        )
    return barrier


def wait_bytes(ref, sem):
    pltpu.make_async_copy(ref, ref, sem).wait()


def send(src, dst, sem_out, sem_in, seq, chan):
    pltpu.make_async_remote_copy(
        src_ref=src, dst_ref=dst, send_sem=sem_out, recv_sem=sem_in,
        device_id=(seq, chan), device_id_type=MESH,
    ).start()


def layer_kernel(
    n, groups, x_ref, w_in_ref, bias_ref, filters_at, cot_at,
    first_at, middle_at, middle_t_at, last_at, cos_at, sin_at,
    b_back, w_own, w_far, u_own,
    filters_ref, cot_ref, first_ref, middle_ref, middle_t_ref, last_ref, cos_ref, sin_ref, load_sems,
    w_ref, wg, w_other, xg, xt, total, stage_a, a_send, a_recv, stage_b, b_send, b_recv,
    spec_h1, spec_h2, spec_v, spec_z, spec_g1, spec_g2,
    stage_c, g_send, g_recv, stage_d, b_give, turned_ref, grad, grad_in,
    w_send, w_in, w_relay, u_acc, u_send, u_in, u_far,
    sems, x_sems, xs_sems, xp_sems, xr_sems, u_sems, us_sems, gs_sems, g_sems, cs_sems, c_sems, bs_sems, b_sems, ws_sems, w_sems,
):
    me = lax.axis_index("seq")
    group = lax.axis_index("chan")
    core = lax.rem(me, 2)
    chip = me // 2
    partner = me + 1 - 2 * core
    chips = n // 2
    ny = min(4, chips // 2)
    nx = chips // (2 * ny)
    plane = nx * ny
    y = lax.rem(chip, ny)
    zl = lax.rem(chip // ny, 2)
    xx = chip // (2 * ny)
    here = (xx * ny + y) * 2 + core
    quota = LANES // chips
    blocks = 4 * chips
    rows_a, rows_b = a_send.shape[1], b_send.shape[1]
    rows_c = 4 * quota
    tokens, depth = x_ref.shape
    cols = wg.shape[2]
    slots = depth // wg.shape[1]

    def in_plane(p, c, z):
        return (((p // ny) * 2 + z) * ny + lax.rem(p, ny)) * 2 + c

    pending = {}

    def expect(key, ref, sem):
        pending[key] = (ref, sem)

    def arrive(*key):
        wait_bytes(*pending.pop(key))

    barrier = greet(me, n, group, groups)

    for k, (here_ref, there_ref) in enumerate(
        (
            (filters_ref, filters_at), (cot_ref, cot_at), (first_ref, first_at), (middle_ref, middle_at),
            (middle_t_ref, middle_t_at), (last_ref, last_at), (cos_ref, cos_at), (sin_ref, sin_at),
        )
    ):
        pltpu.make_async_copy(there_ref, here_ref, load_sems.at[k]).start()
        expect(("load", k), here_ref, load_sems.at[k])

    for half in range(2):
        for a in range(3):
            w_ref[half, :, a * LANES : (a + 1) * LANES] = w_in_ref[a, :, half * LANES : (half + 1) * LANES]

    def spread(value, base):
        turned = value.T
        for half in range(2):
            for q in range(quota):
                top = half * LANES + q * chips
                for tb in range(2):
                    stage_b[pl.ds(half * rows_b + base + q * 2 + tb, chips, stride=2 * rows_b), :] = turned[
                        top : top + chips, tb * LANES : (tb + 1) * LANES
                    ]

    xg[core, group] = x_ref[...]
    pl.semaphore_wait(barrier, n - 1 + groups - 1)

    z_first = in_plane(xx * ny + y, 0, 1 - zl)
    for c in range(2):
        send(w_ref.at[c], wg.at[me], sems.at[0], sems.at[3], z_first + c, group)

    part = tokens // 2
    after, before, across = (lax.rem(group + step, groups) for step in (1, 3, 2))

    def half_x(side, source, half):
        return xg.at[side, source, pl.ds(half * part, part)]

    def send_x(half, target, k):
        own = half_x(core, group, half)
        send(own, own, xs_sems.at[k], x_sems.at[2 * group + half], me, target)
        expect(("x out", k), own, xs_sems.at[k])

    def relay_x(source, half, k):
        ref = half_x(core, source, half)
        send(ref, ref, xr_sems.at[k], xp_sems.at[2 * source + half], partner, group)
        expect(("xp", k), half_x(1 - core, source, half), xp_sems.at[2 * source + half])
        expect(("x relay", k), ref, xr_sems.at[k])

    for k, (half, target) in enumerate(((0, after), (1, before), (1, after), (0, before))):
        send_x(half, target, k)
    arrivals = ((before, 0), (after, 1), (before, 1), (after, 0), (across, 0), (across, 1))
    for k, (source, half) in enumerate(arrivals):
        expect(("x", k), half_x(core, source, half), x_sems.at[2 * source + half])

    def send_w(step, carry):
        peer = lax.rem(here + step, 2 * plane)
        c = lax.rem(peer, 2)
        send(w_ref.at[c], wg.at[me], sems.at[0], sems.at[1], in_plane(peer // 2, c, zl), group)
        return carry

    lax.fori_loop(1, 2 * plane, send_w, 0)
    pltpu.make_async_copy(w_ref.at[core], wg.at[me], sems.at[1]).start()
    expect(("w",), wg.at[pl.ds(0, 2 * plane)], sems.at[1])
    expect(("w out",), wg.at[pl.ds(0, 2 * plane + 1)], sems.at[0])
    for half in range(2):
        relay_x(group, half, 6 + half)

    arrive("load", 0)
    spread(filters_ref[0], 0)
    wait_bytes(wg.at[pl.ds(z_first, 2)], sems.at[3])

    def forward_w(step, carry):
        p = lax.rem(here // 2 + step, plane)
        pair = wg.at[pl.ds(z_first, 2)]
        send(pair, pair, sems.at[4], sems.at[5], in_plane(p, core, zl), group)
        return carry

    lax.fori_loop(1, plane, forward_w, 0)
    expect(("w rest",), wg.at[pl.ds(0, 2 * plane - 2)], sems.at[5])
    expect(("w rest out",), wg.at[pl.ds(0, 2 * plane - 2)], sems.at[4])
    spread(filters_ref[1], 2 * quota)
    for k in range(2):
        arrive("x", k)
        source, half = arrivals[k]
        ref = half_x(core, source, half)
        send(ref, ref, xs_sems.at[4 + k], x_sems.at[2 * source + half], me, after if k == 0 else before)
        expect(("x out", 4 + k), ref, xs_sems.at[4 + k])
        relay_x(source, half, k)
    arrive("load", 1)
    spread(cot_ref[...].astype(F32), 4 * quota)
    for peer in range(n):
        b_send[peer] = stage_b[peer * rows_b : (peer + 1) * rows_b, :].astype(BF16)

    def give_b(step, carry):
        peer = lax.rem(me + step, n)
        send(b_send.at[peer], b_recv.at[me], sems.at[9], sems.at[10], peer, group)
        return carry

    lax.fori_loop(1, n, give_b, 0)
    pltpu.make_async_copy(b_send.at[me], b_recv.at[me], sems.at[10]).start()
    expect(("b",), b_recv, sems.at[10])
    expect(("b out",), b_recv.at[pl.ds(0, n - 1)], sems.at[9])
    for k in (2, 3):
        arrive("x", k)
        relay_x(*arrivals[k], k)
    arrive("w")
    arrive("w rest")

    def weights(ref, c):
        return ref[pl.ds(c * slots, slots)].reshape(depth, cols)

    def project(side, source, first=False):
        at = core if side == 0 else 1 - core
        term = matmul(xg[at, source], weights(wg, source))
        total[at] = term if first else total[at] + term

    project(0, group, True)
    for k in (6, 7):
        arrive("xp", k)
    project(1, group, True)
    project(0, before)
    project(0, after)
    for k in range(4):
        arrive("xp", k)
    project(1, before)
    project(1, after)
    for k in (4, 5):
        arrive("x", k)
        relay_x(*arrivals[k], k)
    project(0, across)
    for k in (4, 5):
        arrive("xp", k)
    project(1, across)
    turned = total[...].reshape(2 * tokens, cols).T
    for a in range(3):
        for q in range(quota):
            top = a * LANES + q * chips
            for tb in range(4):
                stage_a[pl.ds((a * quota + q) * 4 + tb, chips, stride=rows_a), :] = turned[
                    top : top + chips, tb * LANES : (tb + 1) * LANES
                ]
    a_send[...] = stage_a[...].astype(BF16).reshape(a_send.shape)

    def give_a(step, carry):
        peer = lax.rem(chip + step, chips)
        send(a_send.at[peer], a_recv.at[chip], sems.at[11], sems.at[12], 2 * peer + core, group)
        return carry

    lax.fori_loop(1, chips, give_a, 0)
    pltpu.make_async_copy(a_send.at[chip], a_recv.at[chip], sems.at[12]).start()
    expect(("a",), a_recv, sems.at[12])
    expect(("a out",), a_recv.at[pl.ds(0, chips - 1)], sems.at[11])
    send(wg, w_other, sems.at[7], sems.at[8], partner, group)
    expect(("other",), w_other, sems.at[8])
    expect(("other out",), w_other, sems.at[7])
    for k in range(2, 8):
        arrive("load", k)

    def columns(ref, start, stride):
        return jnp.concatenate(
            [
                jnp.concatenate(
                    [ref[pl.ds(start(q, tb), chips, stride=stride), :] for q in range(quota)], axis=1
                )
                for tb in range(4)
            ],
            axis=0,
        )

    def late(a):
        return columns(stage_a, lambda q, tb: (a * quota + q) * 4 + tb, rows_a)

    def early(base):
        return columns(stage_b, lambda q, tb: (tb // 2) * rows_b + base + q * 2 + tb % 2, 2 * rows_b)

    def piece(value, q):
        return value[:, q * LANES : (q + 1) * LANES]

    def forward(value, spec, exact=False):
        high, low = split(value)
        if exact:
            wide = matmul(first_ref[:, : 2 * blocks], jnp.concatenate([high, high], axis=0))
        else:
            wide = matmul(first_ref[...], jnp.concatenate([high, high, low], axis=0))
        turn_cos, turn_sin = cos_ref[...], sin_ref[...]
        for q in range(quota):
            re = piece(wide[:blocks], q)
            im = piece(wide[blocks:], q)
            high, low = split(
                jnp.concatenate([re * turn_cos + im * turn_sin, im * turn_cos - re * turn_sin], axis=1)
            )
            spec[q * blocks : (q + 1) * blocks, :] = matmul(
                jnp.concatenate([high, high, low], axis=1), middle_ref[...]
            )

    def backward(left, right, conj_left, conj_right):
        turn_cos, turn_sin = cos_ref[...], sin_ref[...]
        columns_high, columns_low = [], []
        for q in range(quota):
            rows = slice(q * blocks, (q + 1) * blocks)
            l_re, l_im = left[rows, :LANES], left[rows, LANES:]
            r_re, r_im = right[rows, :LANES], right[rows, LANES:]
            cross = l_im * r_im
            y_re = l_re * r_re - (cross if conj_left == conj_right else -cross)
            if conj_left:
                y_im = l_re * r_im - l_im * r_re
            elif conj_right:
                y_im = l_im * r_re - l_re * r_im
            else:
                y_im = l_re * r_im + l_im * r_re
            high, low = split(jnp.concatenate([y_re, y_im], axis=1))
            out = matmul(jnp.concatenate([high, high, low], axis=1), middle_t_ref[...])
            re, im = out[:, :LANES], out[:, LANES:]
            high, low = split(
                jnp.concatenate([re * turn_cos - im * turn_sin, im * turn_cos + re * turn_sin], axis=0)
            )
            columns_high.append(high)
            columns_low.append(low)
        high = jnp.concatenate(columns_high, axis=1)
        low = jnp.concatenate(columns_low, axis=1)
        return matmul(last_ref[...], jnp.concatenate([high, high, low], axis=0))

    def skip(f):
        return jnp.concatenate(
            [
                jnp.full((1, LANES), bias_ref[f, core * LANES + q * chips + chip], F32)
                for q in range(quota)
            ],
            axis=1,
        )

    def give_late(value, a):
        for q in range(quota):
            for tb in range(4):
                stage_c[pl.ds(q * 4 + tb, chips, stride=rows_c), :] = piece(value, q)[
                    tb * chips : (tb + 1) * chips
                ]
        g_send[a] = stage_c[...].astype(BF16).reshape(chips, rows_c, LANES)

        def one(step, carry):
            peer = lax.rem(chip + step, chips)
            send(g_send.at[a, peer], g_recv.at[a, chip], gs_sems.at[a], g_sems.at[a], 2 * peer + core, group)
            return carry

        lax.fori_loop(1, chips, one, 0)
        pltpu.make_async_copy(g_send.at[a, chip], g_recv.at[a, chip], g_sems.at[a]).start()
        expect(("g", a), g_recv.at[a], g_sems.at[a])
        expect(("g out", a), g_recv.at[a, pl.ds(0, chips - 1)], gs_sems.at[a])

    def put_early(value, base):
        for q in range(quota):
            for tb in range(4):
                at = (tb // 2) * rows_c + base + q * 2 + tb % 2
                stage_d[pl.ds(at, chips, stride=2 * rows_c), :] = piece(value, q)[
                    tb * chips : (tb + 1) * chips
                ]

    def put_skip(product, f):
        lane = lax.broadcasted_iota(jnp.int32, (1, LANES), 1)
        sums = jnp.sum(product, axis=0, keepdims=True)
        for q in range(quota):
            value = jnp.sum(piece(sums, q), axis=1, keepdims=True)
            one = value.astype(BF16).astype(F32)
            two = (value - one).astype(BF16).astype(F32)
            three = value - one - two
            row = jnp.where(lane == chip, one, 0.0)
            row = jnp.where(lane == chips + chip, two, row)
            row = jnp.where(lane == 2 * chips + chip, three, row)
            for half in range(2):
                at = half * rows_c + 2 * quota + f * quota + q
                stage_d[pl.ds(at, chips, stride=2 * rows_c), :] = jnp.broadcast_to(row, (chips, LANES))

    def give_early(k):
        b_give[k] = stage_d[...].astype(BF16).reshape(n, rows_c, LANES)

        def one(step, carry):
            peer = lax.rem(me + step, n)
            send(b_give.at[k, peer], b_back.at[k, me], bs_sems.at[k], b_sems.at[k], peer, group)
            return carry

        lax.fori_loop(1, n, one, 0)
        pltpu.make_async_copy(b_give.at[k, me], b_back.at[k, me], b_sems.at[k]).start()
        expect(("back", k), b_back.at[k], b_sems.at[k])
        expect(("back out", k), b_back.at[k, pl.ds(0, n - 1)], bs_sems.at[k])

    arrive("b")
    for peer in range(n):
        stage_b[peer * rows_b : (peer + 1) * rows_b, :] = b_recv[peer].astype(F32)
    forward(early(0), spec_h1, True)
    forward(early(2 * quota), spec_h2, True)
    for c in range(groups):
        xt[c] = xg[:, c].reshape(2 * tokens, depth).astype(F32).T.astype(BF16)
    arrive("a")
    stage_a[...] = a_recv[...].reshape(stage_a.shape).astype(F32)
    values_v, gate_one, gate_two = late(0), late(1), late(2)
    grad_out = early(4 * quota)
    skip_one, skip_two = skip(0), skip(1)
    grad_conv_two = grad_out * gate_two
    forward(grad_conv_two, spec_g2)
    forward(values_v, spec_v, True)
    grad_mixed = backward(spec_h2, spec_g2, True, False) + skip_two * grad_conv_two
    conv_one = backward(spec_h1, spec_v, False, False) + skip_one * values_v
    mixed = gate_one * conv_one
    grad_conv_one = grad_mixed * gate_one
    give_late(grad_mixed * conv_one, 1)
    forward(grad_conv_one, spec_g1)
    forward(mixed, spec_z)
    grad_v = backward(spec_h1, spec_g1, True, False) + skip_one * grad_conv_one
    conv_two = backward(spec_h2, spec_z, False, False) + skip_two * mixed
    give_late(grad_v, 0)
    give_late(grad_out * conv_two, 2)
    put_early(gate_two * conv_two, 0)
    put_early(backward(spec_g2, spec_z, False, True), 2 * quota)
    give_early(0)
    put_early(backward(spec_g1, spec_v, False, True), 0)
    put_skip(grad_conv_one * values_v, 0)
    put_skip(grad_conv_two * mixed, 1)
    give_early(1)

    def take(a):
        arrive("g", a)
        stage_c[...] = g_recv[a].reshape(stage_c.shape).astype(F32)
        for q in range(quota):
            for tb in range(4):
                turned_ref[q * chips : (q + 1) * chips, tb * LANES : (tb + 1) * LANES] = stage_c[
                    pl.ds(q * 4 + tb, chips, stride=rows_c), :
                ]
        grad[a] = turned_ref[...].T.astype(BF16).reshape(2, tokens, LANES)
        send(grad.at[a, 1 - core], grad_in.at[a], cs_sems.at[a], c_sems.at[a], partner, group)
        expect(("grad", a), grad_in.at[a], c_sems.at[a])
        expect(("grad out", a), grad_in.at[a], cs_sems.at[a])

    def give_w(a):
        block = grad[a].reshape(2 * tokens, LANES)
        for c in range(groups):
            term = matmul(xt[c], block).astype(BF16).reshape(slots, depth // slots, LANES)
            for k in range(slots):
                s = c * slots + k
                w_send[a, s // (4 * ny), (s // (2 * ny)) % 2, s % (2 * ny)] = term[k]

        def one(step, carry):
            peer = lax.rem(here + step, 2 * plane)
            p, c = peer // 2, lax.rem(peer, 2)
            send(
                w_send.at[a, p // ny, :, lax.rem(p, ny) * 2 + c], w_in.at[a, here],
                ws_sems.at[a], w_sems.at[a], in_plane(p, c, zl), group,
            )
            return carry

        lax.fori_loop(1, 2 * plane, one, 0)
        pltpu.make_async_copy(w_send.at[a, xx, :, y * 2 + core], w_in.at[a, here], w_sems.at[a]).start()
        expect(("sum", a), w_in.at[a], w_sems.at[a])
        expect(("sum out", a), w_in.at[a, pl.ds(0, 2 * plane - 1)], ws_sems.at[a])

    def both(arrays, c):
        left = jnp.concatenate([part for a in arrays for part in (grad[a, core], grad_in[a])], axis=1)
        wide = [weights(wg, c), weights(w_other, c)]
        right = jnp.concatenate([piece(part, a) for a in arrays for part in wide], axis=1)
        return matmul(left, right, ((1,), (1,)))

    take(1)
    give_w(1)
    take(0)
    give_w(0)
    arrive("other")
    for a in (1, 0):
        arrive("grad", a)
    for c in range(groups):
        u_acc[c] = both((1, 0), c)
    take(2)
    arrive("grad", 2)

    def send_u(ref, slot, target):
        send(ref, u_in.at[slot], us_sems.at[slot], u_sems.at[slot], me, target)
        expect(("u", slot), u_in.at[slot], u_sems.at[slot])
        expect(("u out", slot), u_in.at[slot], us_sems.at[slot])

    def half_u(dest, half):
        return u_send.at[dest, pl.ds(half * part, part)]

    def finish_u(dest):
        value = u_acc[dest] + both((2,), dest)
        u_acc[dest] = value
        u_send[dest] = value.astype(BF16)

    finish_u(across)
    send_u(half_u(across, 0), 0, after)
    send_u(half_u(across, 1), 1, before)
    finish_u(after)
    send_u(half_u(after, 1), 2, after)
    finish_u(before)
    send_u(half_u(before, 0), 3, before)
    u_own[...] = u_acc[group] + both((2,), group)
    give_w(2)
    arrive("u", 0)
    u_far[0] = (u_acc[after, :part] + u_in[0].astype(F32)).astype(BF16)
    send_u(u_far.at[0], 4, after)
    arrive("u", 1)
    u_far[1] = (u_acc[before, part:] + u_in[1].astype(F32)).astype(BF16)
    send_u(u_far.at[1], 5, before)

    z_device = z_first + core
    for a in (1, 0, 2):
        arrive("sum", a)
        for half in range(2):
            own = w_in[a, half, zl].astype(F32)
            away = w_in[a, half, 1 - zl].astype(F32)
            for p in range(1, plane):
                own = own + w_in[a, 2 * p + half, zl].astype(F32)
                away = away + w_in[a, 2 * p + half, 1 - zl].astype(F32)
            w_own[a, half] = own
            w_relay[a, half] = away
        send(w_relay.at[a], w_far.at[a], ws_sems.at[3 + a], w_sems.at[3 + a], z_device, group)
        expect(("far", a), w_far.at[a], w_sems.at[3 + a])
        expect(("far out", a), w_far.at[a], ws_sems.at[3 + a])

    for slot in range(2, 6):
        arrive("u", slot)
    u_own[:part] = u_own[:part] + u_in[3].astype(F32) + u_in[4].astype(F32)
    u_own[part:] = u_own[part:] + u_in[2].astype(F32) + u_in[5].astype(F32)
    for key in list(pending):
        arrive(*key)


def finish_kernel(
    n, b_back, w_own, w_far, u_own, out_ref, gu_ref, gw_ref, gf_ref, gb_ref, stage, turned_ref
):
    chips = n // 2
    quota = LANES // chips
    rows_c = 4 * quota

    def collect(k, base):
        for half in range(2):
            for q in range(quota):
                top = half * LANES + q * chips
                for tb in range(2):
                    turned_ref[top : top + chips, tb * LANES : (tb + 1) * LANES] = stage[
                        k, pl.ds(half * rows_c + base + q * 2 + tb, chips, stride=2 * rows_c), :
                    ]
        return turned_ref[...].T

    stage[...] = b_back[...].reshape(stage.shape).astype(F32)
    out_ref[...] = collect(0, 0).astype(BF16)
    gf_ref[1] = collect(0, 2 * quota)
    gf_ref[0] = collect(1, 0)
    lane = lax.broadcasted_iota(jnp.int32, (1, LANES), 1)
    for f in range(2):
        for half in range(2):
            line = jnp.zeros((1, LANES), F32)
            for q in range(quota):
                at = half * rows_c + 2 * quota + f * quota + q
                row = jnp.sum(stage[1, pl.ds(at, chips, stride=2 * rows_c), :], axis=0, keepdims=True)
                full = row + pltpu.roll(row, LANES - chips, 1) + pltpu.roll(row, LANES - 2 * chips, 1)
                moved = full if q == 0 else pltpu.roll(full, q * chips, 1)
                line = jnp.where((lane >= q * chips) & (lane < (q + 1) * chips), moved, line)
            gb_ref[f : f + 1, half * LANES : (half + 1) * LANES] = line
    gu_ref[...] = u_own[...].astype(BF16)
    for a in range(3):
        for half in range(2):
            gw_ref[a, :, half * LANES : (half + 1) * LANES] = w_own[a, half] + w_far[a, half]


def on_device(layer_input, w_in, filters, bias, cotangent):
    n = lax.axis_size("seq")
    groups = lax.axis_size("chan")
    tokens, width = layer_input.shape
    rows = w_in.shape[0]
    chips = n // 2
    ny = min(4, chips // 2)
    nx = chips // (2 * ny)
    plane = nx * ny
    quota = LANES // chips
    blocks = 4 * chips
    rows_a, rows_b, rows_c = 12 * quota, 6 * quota, 4 * quota
    cols = 3 * LANES
    vmem = pl.BlockSpec(memory_space=pltpu.VMEM)
    smem = pl.BlockSpec(memory_space=pltpu.SMEM)
    sds = jax.ShapeDtypeStruct
    dma = pltpu.SemaphoreType.DMA
    limit = 58 * 1024 * 1024
    spec = pltpu.VMEM((quota * blocks, 2 * LANES), F32)

    constants = [jnp.asarray(table) for table in tables(blocks)]
    landed = pl.pallas_call(
        functools.partial(layer_kernel, n, groups),
        out_shape=(
            sds((2, n, rows_c, LANES), BF16),
            sds((3, 2, rows, LANES), F32),
            sds((3, 2, rows, LANES), F32),
            sds((tokens, width), F32),
        ),
        in_specs=[vmem, vmem, smem] + [pl.BlockSpec(memory_space=pl.ANY)] * 8,
        out_specs=(vmem,) * 4,
        scratch_shapes=[
            *(pltpu.VMEM(array.shape, array.dtype) for array in (filters, cotangent, *constants)),
            dma((8,)),
            pltpu.VMEM((2, rows, cols), BF16),
            pltpu.VMEM((n, rows, cols), BF16),
            pltpu.VMEM((n, rows, cols), BF16),
            pltpu.VMEM((2, groups, tokens, width), BF16),
            pltpu.VMEM((groups, width, 2 * tokens), BF16),
            pltpu.VMEM((2, tokens, cols), F32),
            pltpu.VMEM((chips * rows_a, LANES), F32),
            pltpu.VMEM((chips, rows_a, LANES), BF16),
            pltpu.VMEM((chips, rows_a, LANES), BF16),
            pltpu.VMEM((n * rows_b, LANES), F32),
            pltpu.VMEM((n, rows_b, LANES), BF16),
            pltpu.VMEM((n, rows_b, LANES), BF16),
            spec, spec, spec, spec, spec, spec,
            pltpu.VMEM((chips * rows_c, LANES), F32),
            pltpu.VMEM((3, chips, rows_c, LANES), BF16),
            pltpu.VMEM((3, chips, rows_c, LANES), BF16),
            pltpu.VMEM((n * rows_c, LANES), F32),
            pltpu.VMEM((2, n, rows_c, LANES), BF16),
            pltpu.VMEM((LANES, 2 * tokens), F32),
            pltpu.VMEM((3, 2, tokens, LANES), BF16),
            pltpu.VMEM((3, tokens, LANES), BF16),
            pltpu.VMEM((3, nx, 2, 2 * ny, rows, LANES), BF16),
            pltpu.VMEM((3, 2 * plane, 2, rows, LANES), BF16),
            pltpu.VMEM((3, 2, rows, LANES), F32),
            pltpu.VMEM((groups, tokens, width), F32),
            pltpu.VMEM((groups, tokens, width), BF16),
            pltpu.VMEM((6, tokens // 2, width), BF16),
            pltpu.VMEM((2, tokens // 2, width), BF16),
            dma((17,)),
            dma((2 * groups,)), dma((6,)), dma((2 * groups,)), dma((8,)), dma((6,)), dma((6,)),
            dma((3,)), dma((3,)), dma((3,)), dma((3,)),
            dma((2,)), dma((2,)), dma((6,)), dma((6,)),
        ],
        compiler_params=pltpu.CompilerParams(
            collective_id=0, has_side_effects=True, vmem_limit_bytes=limit
        ),
        name="layer",
    )(layer_input, w_in.transpose(1, 0, 2), bias, filters, cotangent, *constants)

    out, grad_u, grad_w, grad_f, grad_b = pl.pallas_call(
        functools.partial(finish_kernel, n),
        out_shape=(
            sds((tokens, width), BF16),
            sds((tokens, width), BF16),
            sds((3, rows, width), F32),
            sds((2, tokens, width), F32),
            sds((2, width), F32),
        ),
        in_specs=[vmem] * 4,
        out_specs=(vmem,) * 5,
        scratch_shapes=[
            pltpu.VMEM((2, n * rows_c, LANES), F32),
            pltpu.VMEM((2 * LANES, tokens), F32),
        ],
        compiler_params=pltpu.CompilerParams(vmem_limit_bytes=limit),
        name="finish",
    )(*landed)
    return (out, grad_u, grad_w.transpose(1, 0, 2), grad_f, grad_b)


def solution(mesh):
    in_specs = (
        P("seq", "chan"),
        P("seq", None, "chan"),
        P(None, "seq", "chan"),
        P(None, "chan"),
        P("seq", "chan"),
    )
    out_specs = (
        P("seq", "chan"),
        P("seq", "chan"),
        P("seq", None, "chan"),
        P(None, "seq", "chan"),
        P(None, "chan"),
    )
    return jax.shard_map(
        on_device, mesh=mesh, in_specs=in_specs, out_specs=out_specs, check_vma=False
    )
```

```python
import functools
import math

import jax
import jax.numpy as jnp
import ml_dtypes
import numpy as np
from jax import lax
from jax.experimental import pallas as pl
from jax.experimental.pallas import tpu as pltpu
from jax.sharding import PartitionSpec as P

MESH = pl.DeviceIdType.MESH
LANES = 128
BF16 = jnp.bfloat16
F32 = jnp.float32


def tables(blocks):
    period = 2 * blocks * LANES
    chips = blocks // 4
    order = np.array([4 * j + tb for tb in range(4) for j in range(chips)])
    freq = np.arange(blocks) + 0.5
    lane = np.arange(LANES)
    angle = 2.0 * math.pi * freq[:, None] * order[None, :] / (2 * blocks)
    first = np.concatenate([np.cos(angle), -np.sin(angle)], axis=0)
    turn = 2.0 * math.pi * freq[:, None] * lane[None, :] / period
    inner = 2.0 * math.pi * ((lane[:, None] * lane[None, :]) % LANES) / LANES
    cosine, sine = np.cos(inner), np.sin(inner)
    middle = np.block([[cosine, -sine], [sine, cosine]])
    last = first.T * (2.0 / period)

    def parts(table, axis):
        high = table.astype(ml_dtypes.bfloat16)
        low = (table - high.astype(np.float64)).astype(ml_dtypes.bfloat16)
        return np.concatenate([high, low], axis=axis)

    return (
        parts(first, 1),
        parts(middle, 0),
        parts(middle.T, 0),
        parts(last, 1),
        np.cos(turn).astype(np.float32),
        np.sin(turn).astype(np.float32),
    )


def matmul(left, right, dims=((1,), (0,))):
    return lax.dot_general(left, right, (dims, ((), ())), preferred_element_type=F32)


def greet(me, peers, group, groups):
    barrier = pltpu.get_barrier_semaphore()

    def one(step, carry):
        pl.semaphore_signal(
            barrier, inc=1, device_id=(lax.rem(me + step, peers), group), device_id_type=MESH
        )
        return carry

    lax.fori_loop(1, peers, one, 0)
    for step in range(1, groups):
        pl.semaphore_signal(
            barrier, inc=1, device_id=(me, lax.rem(group + step, groups)), device_id_type=MESH
        )
    return barrier


def wait_bytes(ref, sem):
    pltpu.make_async_copy(ref, ref, sem).wait()


def send(src, dst, sem_out, sem_in, seq, chan):
    pltpu.make_async_remote_copy(
        src_ref=src, dst_ref=dst, send_sem=sem_out, recv_sem=sem_in,
        device_id=(seq, chan), device_id_type=MESH,
    ).start()


def layer_kernel(
    n, groups, x_ref, w_in_ref, bias_ref, filters_at, cot_at,
    first_at, middle_at, middle_t_at, last_at, cos_at, sin_at,
    b_back, w_own, w_far, u_own,
    filters_ref, cot_ref, first_ref, middle_ref, middle_t_ref, last_ref, cos_ref, sin_ref, load_sems,
    w_ref, wg, w_other, xg, xt, total, stage_a, a_send, a_recv, stage_b, b_send, b_recv,
    spec_h1, spec_h2, spec_v, spec_z, spec_g1, spec_g2,
    stage_c, g_send, g_recv, stage_d, b_give, turned_ref, grad, grad_in,
    w_send, w_in, w_relay, u_acc, u_send, u_in, u_far,
    sems, x_sems, xs_sems, xp_sems, xr_sems, u_sems, us_sems, gs_sems, g_sems, cs_sems, c_sems, ws_sems, w_sems,
):
    me = lax.axis_index("seq")
    group = lax.axis_index("chan")
    core = lax.rem(me, 2)
    chip = me // 2
    partner = me + 1 - 2 * core
    chips = n // 2
    ny = min(4, chips // 2)
    nx = chips // (2 * ny)
    plane = nx * ny
    y = lax.rem(chip, ny)
    zl = lax.rem(chip // ny, 2)
    xx = chip // (2 * ny)
    here = (xx * ny + y) * 2 + core
    quota = LANES // chips
    blocks = 4 * chips
    rows_a, rows_b = a_send.shape[1], b_send.shape[1]
    rows_c, rows_d = 4 * quota, 8 * quota
    tokens, depth = x_ref.shape
    cols = wg.shape[2]
    slots = depth // wg.shape[1]

    def in_plane(p, c, z):
        return (((p // ny) * 2 + z) * ny + lax.rem(p, ny)) * 2 + c

    pending = {}

    def expect(key, ref, sem):
        pending[key] = (ref, sem)

    def arrive(*key):
        wait_bytes(*pending.pop(key))

    barrier = greet(me, n, group, groups)

    for k, (here_ref, there_ref) in enumerate(
        (
            (filters_ref, filters_at), (cot_ref, cot_at), (first_ref, first_at), (middle_ref, middle_at),
            (middle_t_ref, middle_t_at), (last_ref, last_at), (cos_ref, cos_at), (sin_ref, sin_at),
        )
    ):
        pltpu.make_async_copy(there_ref, here_ref, load_sems.at[k]).start()
        expect(("load", k), here_ref, load_sems.at[k])

    for half in range(2):
        for a in range(3):
            w_ref[half, :, a * LANES : (a + 1) * LANES] = w_in_ref[a, :, half * LANES : (half + 1) * LANES]

    def spread(value, base):
        turned = value.T
        for half in range(2):
            for q in range(quota):
                top = half * LANES + q * chips
                for tb in range(2):
                    stage_b[pl.ds(half * rows_b + base + q * 2 + tb, chips, stride=2 * rows_b), :] = turned[
                        top : top + chips, tb * LANES : (tb + 1) * LANES
                    ]

    xg[core, group] = x_ref[...]
    pl.semaphore_wait(barrier, n - 1 + groups - 1)

    z_first = in_plane(xx * ny + y, 0, 1 - zl)
    for c in range(2):
        send(w_ref.at[c], wg.at[me], sems.at[0], sems.at[3], z_first + c, group)

    part = tokens // 2
    after, before, across = (lax.rem(group + step, groups) for step in (1, 3, 2))

    def half_x(side, source, half):
        return xg.at[side, source, pl.ds(half * part, part)]

    def send_x(half, target, k):
        own = half_x(core, group, half)
        send(own, own, xs_sems.at[k], x_sems.at[2 * group + half], me, target)
        expect(("x out", k), own, xs_sems.at[k])

    def relay_x(source, half, k):
        ref = half_x(core, source, half)
        send(ref, ref, xr_sems.at[k], xp_sems.at[2 * source + half], partner, group)
        expect(("xp", k), half_x(1 - core, source, half), xp_sems.at[2 * source + half])
        expect(("x relay", k), ref, xr_sems.at[k])

    for k, (half, target) in enumerate(((0, after), (1, before), (1, after), (0, before))):
        send_x(half, target, k)
    arrivals = ((before, 0), (after, 1), (before, 1), (after, 0), (across, 0), (across, 1))
    for k, (source, half) in enumerate(arrivals):
        expect(("x", k), half_x(core, source, half), x_sems.at[2 * source + half])

    def send_w(step, carry):
        peer = lax.rem(here + step, 2 * plane)
        c = lax.rem(peer, 2)
        send(w_ref.at[c], wg.at[me], sems.at[0], sems.at[1], in_plane(peer // 2, c, zl), group)
        return carry

    lax.fori_loop(1, 2 * plane, send_w, 0)
    pltpu.make_async_copy(w_ref.at[core], wg.at[me], sems.at[1]).start()
    expect(("w",), wg.at[pl.ds(0, 2 * plane)], sems.at[1])
    expect(("w out",), wg.at[pl.ds(0, 2 * plane + 1)], sems.at[0])
    for half in range(2):
        relay_x(group, half, 6 + half)

    arrive("load", 0)
    spread(filters_ref[0], 0)
    wait_bytes(wg.at[pl.ds(z_first, 2)], sems.at[3])

    def forward_w(step, carry):
        p = lax.rem(here // 2 + step, plane)
        pair = wg.at[pl.ds(z_first, 2)]
        send(pair, pair, sems.at[4], sems.at[5], in_plane(p, core, zl), group)
        return carry

    lax.fori_loop(1, plane, forward_w, 0)
    expect(("w rest",), wg.at[pl.ds(0, 2 * plane - 2)], sems.at[5])
    expect(("w rest out",), wg.at[pl.ds(0, 2 * plane - 2)], sems.at[4])
    spread(filters_ref[1], 2 * quota)
    for k in range(2):
        arrive("x", k)
        source, half = arrivals[k]
        ref = half_x(core, source, half)
        send(ref, ref, xs_sems.at[4 + k], x_sems.at[2 * source + half], me, after if k == 0 else before)
        expect(("x out", 4 + k), ref, xs_sems.at[4 + k])
        relay_x(source, half, k)
    arrive("load", 1)
    spread(cot_ref[...].astype(F32), 4 * quota)
    for peer in range(n):
        b_send[peer] = stage_b[peer * rows_b : (peer + 1) * rows_b, :].astype(BF16)

    def give_b(step, carry):
        peer = lax.rem(me + step, n)
        send(b_send.at[peer], b_recv.at[me], sems.at[9], sems.at[10], peer, group)
        return carry

    lax.fori_loop(1, n, give_b, 0)
    pltpu.make_async_copy(b_send.at[me], b_recv.at[me], sems.at[10]).start()
    expect(("b",), b_recv, sems.at[10])
    expect(("b out",), b_recv.at[pl.ds(0, n - 1)], sems.at[9])
    for k in (2, 3):
        arrive("x", k)
        relay_x(*arrivals[k], k)
    arrive("w")
    arrive("w rest")

    def weights(ref, c):
        return ref[pl.ds(c * slots, slots)].reshape(depth, cols)

    def project(side, source, first=False):
        at = core if side == 0 else 1 - core
        term = matmul(xg[at, source], weights(wg, source))
        total[at] = term if first else total[at] + term

    project(0, group, True)
    for k in (6, 7):
        arrive("xp", k)
    project(1, group, True)
    project(0, before)
    project(0, after)
    for k in range(4):
        arrive("xp", k)
    project(1, before)
    project(1, after)
    for k in (4, 5):
        arrive("x", k)
        relay_x(*arrivals[k], k)
    def lay_out(at):
        turned = total[at].T
        for a in range(3):
            for q in range(quota):
                top = a * LANES + q * chips
                for tb in range(2):
                    row = (a * quota + q) * 4 + 2 * at + tb
                    stage_a[pl.ds(row, chips, stride=rows_a), :] = turned[
                        top : top + chips, tb * LANES : (tb + 1) * LANES
                    ]

    project(0, across)
    lay_out(core)
    for k in (4, 5):
        arrive("xp", k)
    project(1, across)
    lay_out(1 - core)
    a_send[...] = stage_a[...].astype(BF16).reshape(a_send.shape)

    def give_a(step, carry):
        peer = lax.rem(chip + step, chips)
        send(a_send.at[peer], a_recv.at[chip], sems.at[11], sems.at[12], 2 * peer + core, group)
        return carry

    lax.fori_loop(1, chips, give_a, 0)
    pltpu.make_async_copy(a_send.at[chip], a_recv.at[chip], sems.at[12]).start()
    expect(("a",), a_recv, sems.at[12])
    expect(("a out",), a_recv.at[pl.ds(0, chips - 1)], sems.at[11])
    send(wg, w_other, sems.at[7], sems.at[8], partner, group)
    expect(("other",), w_other, sems.at[8])
    expect(("other out",), w_other, sems.at[7])
    for k in range(2, 8):
        arrive("load", k)

    def columns(ref, start, stride):
        return jnp.concatenate(
            [
                jnp.concatenate(
                    [ref[pl.ds(start(q, tb), chips, stride=stride), :] for q in range(quota)], axis=1
                )
                for tb in range(4)
            ],
            axis=0,
        )

    def late(a):
        return columns(stage_a, lambda q, tb: (a * quota + q) * 4 + tb, rows_a)

    def early(base):
        return columns(stage_b, lambda q, tb: (tb // 2) * rows_b + base + q * 2 + tb % 2, 2 * rows_b)

    def piece(value, q):
        return value[:, q * LANES : (q + 1) * LANES]

    def twice(value, axis):
        high = value.astype(BF16)
        return jnp.concatenate([high, high], axis=axis)

    def forward(value, spec):
        wide = matmul(first_ref[...], twice(value, 0))
        turn_cos, turn_sin = cos_ref[...], sin_ref[...]
        for q in range(quota):
            re = piece(wide[:blocks], q)
            im = piece(wide[blocks:], q)
            turned = jnp.concatenate([re * turn_cos + im * turn_sin, im * turn_cos - re * turn_sin], axis=1)
            spec[q * blocks : (q + 1) * blocks, :] = matmul(twice(turned, 1), middle_ref[...])

    def backward(left, right, conj_left, conj_right):
        turn_cos, turn_sin = cos_ref[...], sin_ref[...]
        parts = []
        for q in range(quota):
            rows = slice(q * blocks, (q + 1) * blocks)
            l_re, l_im = left[rows, :LANES], left[rows, LANES:]
            r_re, r_im = right[rows, :LANES], right[rows, LANES:]
            cross = l_im * r_im
            y_re = l_re * r_re - (cross if conj_left == conj_right else -cross)
            if conj_left:
                y_im = l_re * r_im - l_im * r_re
            elif conj_right:
                y_im = l_im * r_re - l_re * r_im
            else:
                y_im = l_re * r_im + l_im * r_re
            out = matmul(twice(jnp.concatenate([y_re, y_im], axis=1), 1), middle_t_ref[...])
            re, im = out[:, :LANES], out[:, LANES:]
            parts.append(jnp.concatenate([re * turn_cos - im * turn_sin, im * turn_cos + re * turn_sin], axis=0))
        return matmul(last_ref[...], twice(jnp.concatenate(parts, axis=1), 0))

    def skip(f):
        return jnp.concatenate(
            [
                jnp.full((1, LANES), bias_ref[f, core * LANES + q * chips + chip], F32)
                for q in range(quota)
            ],
            axis=1,
        )

    order = {1: 0, 0: 1, 2: 2}

    def put_late(value, a):
        for q in range(quota):
            for tb in range(4):
                stage_c[pl.ds(q * 4 + tb, chips, stride=rows_c), :] = piece(value, q)[
                    tb * chips : (tb + 1) * chips
                ]
        g_send[:, order[a]] = stage_c[...].astype(BF16).reshape(chips, rows_c, LANES)

    def give_late(k, span):
        def one(step, carry):
            peer = lax.rem(chip + step, chips)
            send(g_send.at[peer, span], g_recv.at[chip, span], gs_sems.at[k], g_sems.at[k], 2 * peer + core, group)
            return carry

        lax.fori_loop(1, chips, one, 0)
        pltpu.make_async_copy(g_send.at[chip, span], g_recv.at[chip, span], g_sems.at[k]).start()
        expect(("g", k), g_recv.at[:, span], g_sems.at[k])
        expect(("g out", k), g_recv.at[pl.ds(0, chips - 1), span], gs_sems.at[k])

    def put_early(value, base):
        for q in range(quota):
            for tb in range(4):
                at = (tb // 2) * rows_d + base + q * 2 + tb % 2
                stage_d[pl.ds(at, chips, stride=2 * rows_d), :] = piece(value, q)[
                    tb * chips : (tb + 1) * chips
                ]

    def put_skip(product, f):
        lane = lax.broadcasted_iota(jnp.int32, (1, LANES), 1)
        sums = jnp.sum(product, axis=0, keepdims=True)
        for q in range(quota):
            value = jnp.sum(piece(sums, q), axis=1, keepdims=True)
            one = value.astype(BF16).astype(F32)
            two = (value - one).astype(BF16).astype(F32)
            three = value - one - two
            row = jnp.where(lane == chip, one, 0.0)
            row = jnp.where(lane == chips + chip, two, row)
            row = jnp.where(lane == 2 * chips + chip, three, row)
            for half in range(2):
                at = half * rows_d + 6 * quota + f * quota + q
                stage_d[pl.ds(at, chips, stride=2 * rows_d), :] = jnp.broadcast_to(row, (chips, LANES))

    def give_early():
        for peer in range(n):
            b_give[peer] = stage_d[peer * rows_d : (peer + 1) * rows_d, :].astype(BF16)

        def one(step, carry):
            peer = lax.rem(me + step, n)
            send(b_give.at[peer], b_back.at[me], sems.at[14], sems.at[15], peer, group)
            return carry

        lax.fori_loop(1, n, one, 0)
        pltpu.make_async_copy(b_give.at[me], b_back.at[me], sems.at[15]).start()
        expect(("back",), b_back, sems.at[15])
        expect(("back out",), b_back.at[pl.ds(0, n - 1)], sems.at[14])

    arrive("b")
    for peer in range(n):
        stage_b[peer * rows_b : (peer + 1) * rows_b, :] = b_recv[peer].astype(F32)
    forward(early(0), spec_h1)
    forward(early(2 * quota), spec_h2)
    for c in range(groups):
        xt[c] = xg[:, c].reshape(2 * tokens, depth).astype(F32).T.astype(BF16)
    arrive("a")
    stage_a[...] = a_recv[...].reshape(stage_a.shape).astype(F32)
    values_v, gate_one, gate_two = late(0), late(1), late(2)
    grad_out = early(4 * quota)
    skip_one, skip_two = skip(0), skip(1)
    grad_conv_two = grad_out * gate_two
    forward(grad_conv_two, spec_g2)
    forward(values_v, spec_v)
    grad_mixed = backward(spec_h2, spec_g2, True, False) + skip_two * grad_conv_two
    conv_one = backward(spec_h1, spec_v, False, False) + skip_one * values_v
    mixed = gate_one * conv_one
    grad_conv_one = grad_mixed * gate_one
    put_late(grad_mixed * conv_one, 1)
    give_late(0, pl.ds(0, 1))
    forward(grad_conv_one, spec_g1)
    forward(mixed, spec_z)
    grad_v = backward(spec_h1, spec_g1, True, False) + skip_one * grad_conv_one
    conv_two = backward(spec_h2, spec_z, False, False) + skip_two * mixed
    put_late(grad_v, 0)
    put_late(grad_out * conv_two, 2)
    give_late(1, pl.ds(1, 2))
    put_early(gate_two * conv_two, 0)
    put_early(backward(spec_g2, spec_z, False, True), 2 * quota)
    put_early(backward(spec_g1, spec_v, False, True), 4 * quota)
    put_skip(grad_conv_one * values_v, 0)
    put_skip(grad_conv_two * mixed, 1)
    give_early()

    def take(a):
        stage_c[...] = g_recv[:, order[a]].reshape(stage_c.shape).astype(F32)
        for q in range(quota):
            for tb in range(4):
                turned_ref[q * chips : (q + 1) * chips, tb * LANES : (tb + 1) * LANES] = stage_c[
                    pl.ds(q * 4 + tb, chips, stride=rows_c), :
                ]
        grad[a] = turned_ref[...].T.astype(BF16).reshape(2, tokens, LANES)
        send(grad.at[a, 1 - core], grad_in.at[a], cs_sems.at[a], c_sems.at[a], partner, group)
        expect(("grad", a), grad_in.at[a], c_sems.at[a])
        expect(("grad out", a), grad_in.at[a], cs_sems.at[a])

    def give_w(a):
        block = grad[a].reshape(2 * tokens, LANES)
        for c in range(groups):
            term = matmul(xt[c], block).astype(BF16).reshape(slots, depth // slots, LANES)
            for k in range(slots):
                s = c * slots + k
                w_send[a, s // (4 * ny), (s // (2 * ny)) % 2, s % (2 * ny)] = term[k]

        def one(step, carry):
            peer = lax.rem(here + step, 2 * plane)
            p, c = peer // 2, lax.rem(peer, 2)
            send(
                w_send.at[a, p // ny, :, lax.rem(p, ny) * 2 + c], w_in.at[a, here],
                ws_sems.at[a], w_sems.at[a], in_plane(p, c, zl), group,
            )
            return carry

        lax.fori_loop(1, 2 * plane, one, 0)
        pltpu.make_async_copy(w_send.at[a, xx, :, y * 2 + core], w_in.at[a, here], w_sems.at[a]).start()
        expect(("sum", a), w_in.at[a], w_sems.at[a])
        expect(("sum out", a), w_in.at[a, pl.ds(0, 2 * plane - 1)], ws_sems.at[a])

    def into_u(terms, c):
        left, right = [], []
        for a, own in terms:
            left.append(grad[a, core] if own else grad_in[a])
            right.append(piece(weights(wg if own else w_other, c), a))
        return matmul(jnp.concatenate(left, axis=1), jnp.concatenate(right, axis=1), ((1,), (1,)))

    arrive("g", 0)
    take(1)
    give_w(1)
    arrive("other")
    arrive("grad", 1)
    for c in range(groups):
        u_acc[c] = into_u(((1, True), (1, False)), c)
    arrive("g", 1)
    take(0)
    take(2)
    for c in range(groups):
        u_acc[c] = u_acc[c] + into_u(((0, True), (2, True)), c)
    arrive("grad", 0)
    arrive("grad", 2)

    def send_u(ref, slot, target):
        send(ref, u_in.at[slot], us_sems.at[slot], u_sems.at[slot], me, target)
        expect(("u", slot), u_in.at[slot], u_sems.at[slot])
        expect(("u out", slot), u_in.at[slot], us_sems.at[slot])

    def half_u(dest, half):
        return u_send.at[dest, pl.ds(half * part, part)]

    def into_last(dest):
        return into_u(((0, False), (2, False)), dest)

    def finish_u(dest):
        value = u_acc[dest] + into_last(dest)
        u_acc[dest] = value
        u_send[dest] = value.astype(BF16)

    finish_u(across)
    send_u(half_u(across, 0), 0, after)
    send_u(half_u(across, 1), 1, before)
    finish_u(after)
    send_u(half_u(after, 1), 2, after)
    finish_u(before)
    send_u(half_u(before, 0), 3, before)
    u_own[...] = u_acc[group] + into_last(group)
    give_w(0)
    arrive("u", 0)
    u_far[0] = (u_acc[after, :part] + u_in[0].astype(F32)).astype(BF16)
    send_u(u_far.at[0], 4, after)
    arrive("u", 1)
    u_far[1] = (u_acc[before, part:] + u_in[1].astype(F32)).astype(BF16)
    send_u(u_far.at[1], 5, before)
    give_w(2)

    z_device = z_first + core
    for a in (1, 0, 2):
        arrive("sum", a)
        for half in range(2):
            own = w_in[a, half, zl].astype(F32)
            away = w_in[a, half, 1 - zl].astype(F32)
            for p in range(1, plane):
                own = own + w_in[a, 2 * p + half, zl].astype(F32)
                away = away + w_in[a, 2 * p + half, 1 - zl].astype(F32)
            w_own[a, half] = own
            w_relay[a, half] = away
        send(w_relay.at[a], w_far.at[a], ws_sems.at[3 + a], w_sems.at[3 + a], z_device, group)
        expect(("far", a), w_far.at[a], w_sems.at[3 + a])
        expect(("far out", a), w_far.at[a], ws_sems.at[3 + a])

    for slot in range(2, 6):
        arrive("u", slot)
    u_own[:part] = u_own[:part] + u_in[3].astype(F32) + u_in[4].astype(F32)
    u_own[part:] = u_own[part:] + u_in[2].astype(F32) + u_in[5].astype(F32)
    for key in list(pending):
        arrive(*key)


def finish_kernel(
    n, b_back, w_own, w_far, u_own, out_ref, gu_ref, gw_ref, gf_ref, gb_ref, stage, turned_ref
):
    chips = n // 2
    quota = LANES // chips
    rows_d = 8 * quota

    def collect(base):
        for half in range(2):
            for q in range(quota):
                top = half * LANES + q * chips
                for tb in range(2):
                    turned_ref[top : top + chips, tb * LANES : (tb + 1) * LANES] = stage[
                        pl.ds(half * rows_d + base + q * 2 + tb, chips, stride=2 * rows_d), :
                    ]
        return turned_ref[...].T

    stage[...] = b_back[...].reshape(stage.shape).astype(F32)
    out_ref[...] = collect(0).astype(BF16)
    gf_ref[1] = collect(2 * quota)
    gf_ref[0] = collect(4 * quota)
    lane = lax.broadcasted_iota(jnp.int32, (1, LANES), 1)
    for f in range(2):
        for half in range(2):
            line = jnp.zeros((1, LANES), F32)
            for q in range(quota):
                at = half * rows_d + 6 * quota + f * quota + q
                row = jnp.sum(stage[pl.ds(at, chips, stride=2 * rows_d), :], axis=0, keepdims=True)
                full = row + pltpu.roll(row, LANES - chips, 1) + pltpu.roll(row, LANES - 2 * chips, 1)
                moved = full if q == 0 else pltpu.roll(full, q * chips, 1)
                line = jnp.where((lane >= q * chips) & (lane < (q + 1) * chips), moved, line)
            gb_ref[f : f + 1, half * LANES : (half + 1) * LANES] = line
    gu_ref[...] = u_own[...].astype(BF16)
    for a in range(3):
        for half in range(2):
            gw_ref[a, :, half * LANES : (half + 1) * LANES] = w_own[a, half] + w_far[a, half]


def on_device(layer_input, w_in, filters, bias, cotangent):
    n = lax.axis_size("seq")
    groups = lax.axis_size("chan")
    tokens, width = layer_input.shape
    rows = w_in.shape[0]
    chips = n // 2
    ny = min(4, chips // 2)
    nx = chips // (2 * ny)
    plane = nx * ny
    quota = LANES // chips
    blocks = 4 * chips
    rows_a, rows_b, rows_c, rows_d = 12 * quota, 6 * quota, 4 * quota, 8 * quota
    cols = 3 * LANES
    vmem = pl.BlockSpec(memory_space=pltpu.VMEM)
    smem = pl.BlockSpec(memory_space=pltpu.SMEM)
    sds = jax.ShapeDtypeStruct
    dma = pltpu.SemaphoreType.DMA
    limit = 58 * 1024 * 1024
    spec = pltpu.VMEM((quota * blocks, 2 * LANES), F32)

    constants = [jnp.asarray(table) for table in tables(blocks)]
    landed = pl.pallas_call(
        functools.partial(layer_kernel, n, groups),
        out_shape=(
            sds((n, rows_d, LANES), BF16),
            sds((3, 2, rows, LANES), F32),
            sds((3, 2, rows, LANES), F32),
            sds((tokens, width), F32),
        ),
        in_specs=[vmem, vmem, smem] + [pl.BlockSpec(memory_space=pl.ANY)] * 8,
        out_specs=(vmem,) * 4,
        scratch_shapes=[
            *(pltpu.VMEM(array.shape, array.dtype) for array in (filters, cotangent, *constants)),
            dma((8,)),
            pltpu.VMEM((2, rows, cols), BF16),
            pltpu.VMEM((n, rows, cols), BF16),
            pltpu.VMEM((n, rows, cols), BF16),
            pltpu.VMEM((2, groups, tokens, width), BF16),
            pltpu.VMEM((groups, width, 2 * tokens), BF16),
            pltpu.VMEM((2, tokens, cols), F32),
            pltpu.VMEM((chips * rows_a, LANES), F32),
            pltpu.VMEM((chips, rows_a, LANES), BF16),
            pltpu.VMEM((chips, rows_a, LANES), BF16),
            pltpu.VMEM((n * rows_b, LANES), F32),
            pltpu.VMEM((n, rows_b, LANES), BF16),
            pltpu.VMEM((n, rows_b, LANES), BF16),
            spec, spec, spec, spec, spec, spec,
            pltpu.VMEM((chips * rows_c, LANES), F32),
            pltpu.VMEM((chips, 3, rows_c, LANES), BF16),
            pltpu.VMEM((chips, 3, rows_c, LANES), BF16),
            pltpu.VMEM((n * rows_d, LANES), F32),
            pltpu.VMEM((n, rows_d, LANES), BF16),
            pltpu.VMEM((LANES, 2 * tokens), F32),
            pltpu.VMEM((3, 2, tokens, LANES), BF16),
            pltpu.VMEM((3, tokens, LANES), BF16),
            pltpu.VMEM((3, nx, 2, 2 * ny, rows, LANES), BF16),
            pltpu.VMEM((3, 2 * plane, 2, rows, LANES), BF16),
            pltpu.VMEM((3, 2, rows, LANES), F32),
            pltpu.VMEM((groups, tokens, width), F32),
            pltpu.VMEM((groups, tokens, width), BF16),
            pltpu.VMEM((6, tokens // 2, width), BF16),
            pltpu.VMEM((2, tokens // 2, width), BF16),
            dma((17,)),
            dma((2 * groups,)), dma((6,)), dma((2 * groups,)), dma((8,)), dma((6,)), dma((6,)),
            dma((3,)), dma((3,)), dma((3,)), dma((3,)),
            dma((6,)), dma((6,)),
        ],
        compiler_params=pltpu.CompilerParams(
            collective_id=0, has_side_effects=True, vmem_limit_bytes=limit
        ),
        name="layer",
    )(layer_input, w_in.transpose(1, 0, 2), bias, filters, cotangent, *constants)

    out, grad_u, grad_w, grad_f, grad_b = pl.pallas_call(
        functools.partial(finish_kernel, n),
        out_shape=(
            sds((tokens, width), BF16),
            sds((tokens, width), BF16),
            sds((3, rows, width), F32),
            sds((2, tokens, width), F32),
            sds((2, width), F32),
        ),
        in_specs=[vmem] * 4,
        out_specs=(vmem,) * 5,
        scratch_shapes=[
            pltpu.VMEM((n * rows_d, LANES), F32),
            pltpu.VMEM((2 * LANES, tokens), F32),
        ],
        compiler_params=pltpu.CompilerParams(vmem_limit_bytes=limit),
        name="finish",
    )(*landed)
    return (out, grad_u, grad_w.transpose(1, 0, 2), grad_f, grad_b)


def solution(mesh):
    in_specs = (
        P("seq", "chan"),
        P("seq", None, "chan"),
        P(None, "seq", "chan"),
        P(None, "chan"),
        P("seq", "chan"),
    )
    out_specs = (
        P("seq", "chan"),
        P("seq", "chan"),
        P("seq", None, "chan"),
        P(None, "seq", "chan"),
        P(None, "chan"),
    )
    return jax.shard_map(
        on_device, mesh=mesh, in_specs=in_specs, out_specs=out_specs, check_vma=False
    )
```

```python
import functools
import math

import jax
import jax.numpy as jnp
import ml_dtypes
import numpy as np
from jax import lax
from jax.experimental import pallas as pl
from jax.experimental.pallas import tpu as pltpu
from jax.sharding import PartitionSpec as P

MESH = pl.DeviceIdType.MESH
LANES = 128
BF16 = jnp.bfloat16
F32 = jnp.float32


def tables(blocks):
    period = 2 * blocks * LANES
    chips = blocks // 4
    order = np.array([4 * j + tb for tb in range(4) for j in range(chips)])
    freq = np.arange(blocks) + 0.5
    lane = np.arange(LANES)
    angle = 2.0 * math.pi * freq[:, None] * order[None, :] / (2 * blocks)
    first = np.concatenate([np.cos(angle), -np.sin(angle)], axis=0)
    turn = 2.0 * math.pi * freq[:, None] * lane[None, :] / period
    inner = 2.0 * math.pi * ((lane[:, None] * lane[None, :]) % LANES) / LANES
    cosine, sine = np.cos(inner), np.sin(inner)
    middle = np.block([[cosine, -sine], [sine, cosine]])
    last = first.T * (2.0 / period)

    def parts(table, axis):
        high = table.astype(ml_dtypes.bfloat16)
        low = (table - high.astype(np.float64)).astype(ml_dtypes.bfloat16)
        return np.concatenate([high, low], axis=axis)

    return (
        parts(first, 1),
        parts(middle, 0),
        parts(middle.T, 0),
        parts(last, 1),
        np.cos(turn).astype(np.float32),
        np.sin(turn).astype(np.float32),
    )


def matmul(left, right, dims=((1,), (0,))):
    return lax.dot_general(left, right, (dims, ((), ())), preferred_element_type=F32)


def greet(me, peers, group, groups):
    barrier = pltpu.get_barrier_semaphore()

    def one(step, carry):
        pl.semaphore_signal(
            barrier, inc=1, device_id=(lax.rem(me + step, peers), group), device_id_type=MESH
        )
        return carry

    lax.fori_loop(1, peers, one, 0)
    for step in range(1, groups):
        pl.semaphore_signal(
            barrier, inc=1, device_id=(me, lax.rem(group + step, groups)), device_id_type=MESH
        )
    return barrier


def wait_bytes(ref, sem):
    pltpu.make_async_copy(ref, ref, sem).wait()


def send(src, dst, sem_out, sem_in, seq, chan):
    pltpu.make_async_remote_copy(
        src_ref=src, dst_ref=dst, send_sem=sem_out, recv_sem=sem_in,
        device_id=(seq, chan), device_id_type=MESH,
    ).start()


def layer_kernel(
    n, groups, x_ref, w_in_ref, bias_ref, filters_at, cot_at,
    first_at, middle_at, middle_t_at, last_at, cos_at, sin_at,
    b_back, w_own, w_far, u_own,
    filters_ref, cot_ref, first_ref, middle_ref, middle_t_ref, last_ref, cos_ref, sin_ref, load_sems,
    w_ref, wg, w_other, xg, xt, total, stage_a, a_send, a_recv, stage_b, b_send, b_recv,
    spec_h1, spec_h2, spec_v, spec_z, spec_g1, spec_g2,
    stage_c, g_send, g_recv, stage_d, b_give, turned_ref, grad, grad_in,
    w_send, w_in, w_relay, u_acc, u_send, u_in, u_far,
    sems, x_sems, xs_sems, xp_sems, xr_sems, u_sems, us_sems, gs_sems, g_sems, cs_sems, c_sems, ws_sems, w_sems,
):
    me = lax.axis_index("seq")
    group = lax.axis_index("chan")
    core = lax.rem(me, 2)
    chip = me // 2
    partner = me + 1 - 2 * core
    chips = n // 2
    ny = min(4, chips // 2)
    nx = chips // (2 * ny)
    plane = nx * ny
    y = lax.rem(chip, ny)
    zl = lax.rem(chip // ny, 2)
    xx = chip // (2 * ny)
    here = (xx * ny + y) * 2 + core
    quota = LANES // chips
    blocks = 4 * chips
    rows_a, rows_b = a_send.shape[1], b_send.shape[1]
    rows_c, rows_d = 4 * quota, 8 * quota
    tokens, depth = x_ref.shape
    cols = wg.shape[2]
    slots = depth // wg.shape[1]

    def in_plane(p, c, z):
        return (((p // ny) * 2 + z) * ny + lax.rem(p, ny)) * 2 + c

    def hops(step, extent):
        return min(step, extent - step)

    moves = sorted(
        ((dx, dz, dy) for dx in range(nx) for dz in range(2) for dy in range(ny)),
        key=lambda move: -(hops(move[0], nx) + move[1] + hops(move[2], ny)),
    )[:-1]

    def moved(dx, dz, dy, c):
        return (
            (lax.rem(xx + dx, nx) * 2 + lax.rem(zl + dz, 2)) * ny + lax.rem(y + dy, ny)
        ) * 2 + c

    pending = {}

    def expect(key, ref, sem):
        pending[key] = (ref, sem)

    def arrive(*key):
        wait_bytes(*pending.pop(key))

    barrier = greet(me, n, group, groups)

    for k, (here_ref, there_ref) in enumerate(
        (
            (filters_ref, filters_at), (cot_ref, cot_at), (first_ref, first_at), (middle_ref, middle_at),
            (middle_t_ref, middle_t_at), (last_ref, last_at), (cos_ref, cos_at), (sin_ref, sin_at),
        )
    ):
        pltpu.make_async_copy(there_ref, here_ref, load_sems.at[k]).start()
        expect(("load", k), here_ref, load_sems.at[k])

    for half in range(2):
        for a in range(3):
            w_ref[half, :, a * LANES : (a + 1) * LANES] = w_in_ref[a, :, half * LANES : (half + 1) * LANES]

    def spread(value, base):
        turned = value.T
        for half in range(2):
            for q in range(quota):
                top = half * LANES + q * chips
                for tb in range(2):
                    stage_b[pl.ds(half * rows_b + base + q * 2 + tb, chips, stride=2 * rows_b), :] = turned[
                        top : top + chips, tb * LANES : (tb + 1) * LANES
                    ]

    xg[core, group] = x_ref[...]
    pl.semaphore_wait(barrier, n - 1 + groups - 1)

    z_first = in_plane(xx * ny + y, 0, 1 - zl)
    for c in range(2):
        send(w_ref.at[c], wg.at[me], sems.at[0], sems.at[3], z_first + c, group)

    part = tokens // 2
    after, before, across = (lax.rem(group + step, groups) for step in (1, 3, 2))

    def half_x(side, source, half):
        return xg.at[side, source, pl.ds(half * part, part)]

    def send_x(half, target, k):
        own = half_x(core, group, half)
        send(own, own, xs_sems.at[k], x_sems.at[2 * group + half], me, target)
        expect(("x out", k), own, xs_sems.at[k])

    def relay_x(source, half, k):
        ref = half_x(core, source, half)
        send(ref, ref, xr_sems.at[k], xp_sems.at[2 * source + half], partner, group)
        expect(("xp", k), half_x(1 - core, source, half), xp_sems.at[2 * source + half])
        expect(("x relay", k), ref, xr_sems.at[k])

    for k, (half, target) in enumerate(((0, after), (1, before), (1, after), (0, before))):
        send_x(half, target, k)
    arrivals = ((before, 0), (after, 1), (before, 1), (after, 0), (across, 0), (across, 1))
    for k, (source, half) in enumerate(arrivals):
        expect(("x", k), half_x(core, source, half), x_sems.at[2 * source + half])

    for dx, dz, dy in moves:
        if dz == 0:
            for c in range(2):
                send(w_ref.at[c], wg.at[me], sems.at[0], sems.at[1], moved(dx, 0, dy, c), group)
    send(w_ref.at[1 - core], wg.at[me], sems.at[0], sems.at[1], partner, group)
    pltpu.make_async_copy(w_ref.at[core], wg.at[me], sems.at[1]).start()
    expect(("w",), wg.at[pl.ds(0, 2 * plane)], sems.at[1])
    expect(("w out",), wg.at[pl.ds(0, 2 * plane + 1)], sems.at[0])
    for half in range(2):
        relay_x(group, half, 6 + half)

    arrive("load", 0)
    spread(filters_ref[0], 0)
    wait_bytes(wg.at[pl.ds(z_first, 2)], sems.at[3])

    pair = wg.at[pl.ds(z_first, 2)]
    for dx, dz, dy in moves:
        if dz == 0:
            send(pair, pair, sems.at[4], sems.at[5], moved(dx, 0, dy, core), group)
    expect(("w rest",), wg.at[pl.ds(0, 2 * plane - 2)], sems.at[5])
    expect(("w rest out",), wg.at[pl.ds(0, 2 * plane - 2)], sems.at[4])
    spread(filters_ref[1], 2 * quota)
    for k in range(2):
        arrive("x", k)
        source, half = arrivals[k]
        ref = half_x(core, source, half)
        send(ref, ref, xs_sems.at[4 + k], x_sems.at[2 * source + half], me, after if k == 0 else before)
        expect(("x out", 4 + k), ref, xs_sems.at[4 + k])
        relay_x(source, half, k)
    arrive("load", 1)
    spread(cot_ref[...].astype(F32), 4 * quota)
    for peer in range(n):
        b_send[peer] = stage_b[peer * rows_b : (peer + 1) * rows_b, :].astype(BF16)

    def give_b(step, carry):
        peer = lax.rem(me + step, n)
        send(b_send.at[peer], b_recv.at[me], sems.at[9], sems.at[10], peer, group)
        return carry

    for k in (2, 3):
        arrive("x", k)
        relay_x(*arrivals[k], k)
    arrive("w")
    arrive("w rest")
    lax.fori_loop(1, n, give_b, 0)
    pltpu.make_async_copy(b_send.at[me], b_recv.at[me], sems.at[10]).start()
    expect(("b",), b_recv, sems.at[10])
    expect(("b out",), b_recv.at[pl.ds(0, n - 1)], sems.at[9])

    def weights(ref, c):
        return ref[pl.ds(c * slots, slots)].reshape(depth, cols)

    def project(side, source, first=False):
        at = core if side == 0 else 1 - core
        term = matmul(xg[at, source], weights(wg, source))
        total[at] = term if first else total[at] + term

    project(0, group, True)
    for k in (6, 7):
        arrive("xp", k)
    project(1, group, True)
    project(0, before)
    project(0, after)
    for k in range(4):
        arrive("xp", k)
    project(1, before)
    project(1, after)
    for k in (4, 5):
        arrive("x", k)
        relay_x(*arrivals[k], k)
    def lay_out(at):
        turned = total[at].T
        for a in range(3):
            for q in range(quota):
                top = a * LANES + q * chips
                for tb in range(2):
                    row = (a * quota + q) * 4 + 2 * at + tb
                    stage_a[pl.ds(row, chips, stride=rows_a), :] = turned[
                        top : top + chips, tb * LANES : (tb + 1) * LANES
                    ]

    project(0, across)
    lay_out(core)
    for k in (4, 5):
        arrive("xp", k)
    project(1, across)
    lay_out(1 - core)
    a_send[...] = stage_a[...].astype(BF16).reshape(a_send.shape)

    for move in moves:
        peer = moved(*move, core)
        send(a_send.at[peer // 2], a_recv.at[chip], sems.at[11], sems.at[12], peer, group)
    pltpu.make_async_copy(a_send.at[chip], a_recv.at[chip], sems.at[12]).start()
    expect(("a",), a_recv, sems.at[12])
    expect(("a out",), a_recv.at[pl.ds(0, chips - 1)], sems.at[11])
    send(wg, w_other, sems.at[7], sems.at[8], partner, group)
    expect(("other",), w_other, sems.at[8])
    expect(("other out",), w_other, sems.at[7])
    for k in range(2, 8):
        arrive("load", k)

    def columns(ref, start, stride):
        return jnp.concatenate(
            [
                jnp.concatenate(
                    [ref[pl.ds(start(q, tb), chips, stride=stride), :] for q in range(quota)], axis=1
                )
                for tb in range(4)
            ],
            axis=0,
        )

    def late(a):
        return columns(stage_a, lambda q, tb: (a * quota + q) * 4 + tb, rows_a)

    def early(base):
        return columns(stage_b, lambda q, tb: (tb // 2) * rows_b + base + q * 2 + tb % 2, 2 * rows_b)

    def piece(value, q):
        return value[:, q * LANES : (q + 1) * LANES]

    def twice(value, axis):
        high = value.astype(BF16)
        return jnp.concatenate([high, high], axis=axis)

    def forward(value, spec):
        wide = matmul(first_ref[...], twice(value, 0))
        turn_cos, turn_sin = cos_ref[...], sin_ref[...]
        for q in range(quota):
            re = piece(wide[:blocks], q)
            im = piece(wide[blocks:], q)
            turned = jnp.concatenate([re * turn_cos + im * turn_sin, im * turn_cos - re * turn_sin], axis=1)
            spec[q * blocks : (q + 1) * blocks, :] = matmul(twice(turned, 1), middle_ref[...])

    def backward(left, right, conj_left, conj_right):
        turn_cos, turn_sin = cos_ref[...], sin_ref[...]
        parts = []
        for q in range(quota):
            rows = slice(q * blocks, (q + 1) * blocks)
            l_re, l_im = left[rows, :LANES], left[rows, LANES:]
            r_re, r_im = right[rows, :LANES], right[rows, LANES:]
            cross = l_im * r_im
            y_re = l_re * r_re - (cross if conj_left == conj_right else -cross)
            if conj_left:
                y_im = l_re * r_im - l_im * r_re
            elif conj_right:
                y_im = l_im * r_re - l_re * r_im
            else:
                y_im = l_re * r_im + l_im * r_re
            out = matmul(twice(jnp.concatenate([y_re, y_im], axis=1), 1), middle_t_ref[...])
            re, im = out[:, :LANES], out[:, LANES:]
            parts.append(jnp.concatenate([re * turn_cos - im * turn_sin, im * turn_cos + re * turn_sin], axis=0))
        return matmul(last_ref[...], twice(jnp.concatenate(parts, axis=1), 0))

    def skip(f):
        return jnp.concatenate(
            [
                jnp.full((1, LANES), bias_ref[f, core * LANES + q * chips + chip], F32)
                for q in range(quota)
            ],
            axis=1,
        )

    order = {1: 0, 0: 1, 2: 2}

    def put_late(value, a):
        for q in range(quota):
            for tb in range(4):
                stage_c[pl.ds(q * 4 + tb, chips, stride=rows_c), :] = piece(value, q)[
                    tb * chips : (tb + 1) * chips
                ]
        g_send[:, order[a]] = stage_c[...].astype(BF16).reshape(chips, rows_c, LANES)

    def give_late(k, span):
        for move in moves:
            peer = moved(*move, core)
            send(g_send.at[peer // 2, span], g_recv.at[chip, span], gs_sems.at[k], g_sems.at[k], peer, group)
        pltpu.make_async_copy(g_send.at[chip, span], g_recv.at[chip, span], g_sems.at[k]).start()
        expect(("g", k), g_recv.at[:, span], g_sems.at[k])
        expect(("g out", k), g_recv.at[pl.ds(0, chips - 1), span], gs_sems.at[k])

    def put_early(value, base):
        for q in range(quota):
            for tb in range(4):
                at = (tb // 2) * rows_d + base + q * 2 + tb % 2
                stage_d[pl.ds(at, chips, stride=2 * rows_d), :] = piece(value, q)[
                    tb * chips : (tb + 1) * chips
                ]

    def put_skip(product, f):
        lane = lax.broadcasted_iota(jnp.int32, (1, LANES), 1)
        sums = jnp.sum(product, axis=0, keepdims=True)
        for q in range(quota):
            value = jnp.sum(piece(sums, q), axis=1, keepdims=True)
            one = value.astype(BF16).astype(F32)
            two = (value - one).astype(BF16).astype(F32)
            three = value - one - two
            row = jnp.where(lane == chip, one, 0.0)
            row = jnp.where(lane == chips + chip, two, row)
            row = jnp.where(lane == 2 * chips + chip, three, row)
            for half in range(2):
                at = half * rows_d + 6 * quota + f * quota + q
                stage_d[pl.ds(at, chips, stride=2 * rows_d), :] = jnp.broadcast_to(row, (chips, LANES))

    def give_early():
        for peer in range(n):
            b_give[peer] = stage_d[peer * rows_d : (peer + 1) * rows_d, :].astype(BF16)

        def one(step, carry):
            peer = lax.rem(me + step, n)
            send(b_give.at[peer], b_back.at[me], sems.at[14], sems.at[15], peer, group)
            return carry

        lax.fori_loop(1, n, one, 0)
        pltpu.make_async_copy(b_give.at[me], b_back.at[me], sems.at[15]).start()
        expect(("back",), b_back, sems.at[15])
        expect(("back out",), b_back.at[pl.ds(0, n - 1)], sems.at[14])

    arrive("b")
    for peer in range(n):
        stage_b[peer * rows_b : (peer + 1) * rows_b, :] = b_recv[peer].astype(F32)
    forward(early(0), spec_h1)
    forward(early(2 * quota), spec_h2)
    for c in range(groups):
        xt[c] = xg[:, c].reshape(2 * tokens, depth).astype(F32).T.astype(BF16)
    arrive("a")
    stage_a[...] = a_recv[...].reshape(stage_a.shape).astype(F32)
    values_v, gate_one, gate_two = late(0), late(1), late(2)
    grad_out = early(4 * quota)
    skip_one, skip_two = skip(0), skip(1)
    grad_conv_two = grad_out * gate_two
    forward(grad_conv_two, spec_g2)
    forward(values_v, spec_v)
    grad_mixed = backward(spec_h2, spec_g2, True, False) + skip_two * grad_conv_two
    conv_one = backward(spec_h1, spec_v, False, False) + skip_one * values_v
    mixed = gate_one * conv_one
    grad_conv_one = grad_mixed * gate_one
    put_late(grad_mixed * conv_one, 1)
    give_late(0, pl.ds(0, 1))
    forward(grad_conv_one, spec_g1)
    forward(mixed, spec_z)
    grad_v = backward(spec_h1, spec_g1, True, False) + skip_one * grad_conv_one
    conv_two = backward(spec_h2, spec_z, False, False) + skip_two * mixed
    put_late(grad_v, 0)
    give_late(1, pl.ds(1, 1))
    put_late(grad_out * conv_two, 2)
    give_late(2, pl.ds(2, 1))
    put_early(gate_two * conv_two, 0)
    put_early(backward(spec_g2, spec_z, False, True), 2 * quota)
    put_early(backward(spec_g1, spec_v, False, True), 4 * quota)
    put_skip(grad_conv_one * values_v, 0)
    put_skip(grad_conv_two * mixed, 1)

    def take(a):
        stage_c[...] = g_recv[:, order[a]].reshape(stage_c.shape).astype(F32)
        for q in range(quota):
            for tb in range(4):
                turned_ref[q * chips : (q + 1) * chips, tb * LANES : (tb + 1) * LANES] = stage_c[
                    pl.ds(q * 4 + tb, chips, stride=rows_c), :
                ]
        grad[a] = turned_ref[...].T.astype(BF16).reshape(2, tokens, LANES)
        send(grad.at[a, 1 - core], grad_in.at[a], cs_sems.at[a], c_sems.at[a], partner, group)
        expect(("grad", a), grad_in.at[a], c_sems.at[a])
        expect(("grad out", a), grad_in.at[a], cs_sems.at[a])

    def give_w(a):
        block = grad[a].reshape(2 * tokens, LANES)
        for c in range(groups):
            term = matmul(xt[c], block).astype(BF16).reshape(slots, depth // slots, LANES)
            for k in range(slots):
                s = c * slots + k
                w_send[a, s // (4 * ny), (s // (2 * ny)) % 2, s % (2 * ny)] = term[k]

        def one(step, carry):
            peer = lax.rem(here + step, 2 * plane)
            p, c = peer // 2, lax.rem(peer, 2)
            send(
                w_send.at[a, p // ny, :, lax.rem(p, ny) * 2 + c], w_in.at[a, here],
                ws_sems.at[a], w_sems.at[a], in_plane(p, c, zl), group,
            )
            return carry

        lax.fori_loop(1, 2 * plane, one, 0)
        pltpu.make_async_copy(w_send.at[a, xx, :, y * 2 + core], w_in.at[a, here], w_sems.at[a]).start()
        expect(("sum", a), w_in.at[a], w_sems.at[a])
        expect(("sum out", a), w_in.at[a, pl.ds(0, 2 * plane - 1)], ws_sems.at[a])

    def into_u(terms, c):
        left, right = [], []
        for a, own in terms:
            left.append(grad[a, core] if own else grad_in[a])
            right.append(piece(weights(wg if own else w_other, c), a))
        return matmul(jnp.concatenate(left, axis=1), jnp.concatenate(right, axis=1), ((1,), (1,)))

    arrive("g", 0)
    take(1)
    give_early()
    give_w(1)
    arrive("other")
    arrive("grad", 1)
    for c in range(groups):
        u_acc[c] = into_u(((1, True), (1, False)), c)
    arrive("g", 1)
    take(0)
    arrive("g", 2)
    take(2)
    give_w(0)
    for c in range(groups):
        u_acc[c] = u_acc[c] + into_u(((0, True), (2, True)), c)
    arrive("grad", 0)
    arrive("grad", 2)

    def send_u(ref, slot, target):
        send(ref, u_in.at[slot], us_sems.at[slot], u_sems.at[slot], me, target)
        expect(("u", slot), u_in.at[slot], u_sems.at[slot])
        expect(("u out", slot), u_in.at[slot], us_sems.at[slot])

    def half_u(dest, half):
        return u_send.at[dest, pl.ds(half * part, part)]

    def into_last(dest):
        return into_u(((0, False), (2, False)), dest)

    def finish_u(dest):
        value = u_acc[dest] + into_last(dest)
        u_acc[dest] = value
        u_send[dest] = value.astype(BF16)

    finish_u(across)
    send_u(half_u(across, 0), 0, after)
    send_u(half_u(across, 1), 1, before)
    finish_u(after)
    send_u(half_u(after, 1), 2, after)
    finish_u(before)
    send_u(half_u(before, 0), 3, before)
    give_w(2)
    u_own[...] = u_acc[group] + into_last(group)
    arrive("u", 0)
    u_far[0] = (u_acc[after, :part] + u_in[0].astype(F32)).astype(BF16)
    send_u(u_far.at[0], 4, after)
    arrive("u", 1)
    u_far[1] = (u_acc[before, part:] + u_in[1].astype(F32)).astype(BF16)
    send_u(u_far.at[1], 5, before)

    z_device = z_first + core
    for a in (1, 0, 2):
        arrive("sum", a)
        for half in range(2):
            own = w_in[a, half, zl].astype(F32)
            away = w_in[a, half, 1 - zl].astype(F32)
            for p in range(1, plane):
                own = own + w_in[a, 2 * p + half, zl].astype(F32)
                away = away + w_in[a, 2 * p + half, 1 - zl].astype(F32)
            w_own[a, half] = own
            w_relay[a, half] = away
        send(w_relay.at[a], w_far.at[a], ws_sems.at[3 + a], w_sems.at[3 + a], z_device, group)
        expect(("far", a), w_far.at[a], w_sems.at[3 + a])
        expect(("far out", a), w_far.at[a], ws_sems.at[3 + a])

    for slot in range(2, 6):
        arrive("u", slot)
    u_own[:part] = u_own[:part] + u_in[3].astype(F32) + u_in[4].astype(F32)
    u_own[part:] = u_own[part:] + u_in[2].astype(F32) + u_in[5].astype(F32)
    for key in list(pending):
        arrive(*key)


def finish_kernel(
    n, b_back, w_own, w_far, u_own, out_ref, gu_ref, gw_ref, gf_ref, gb_ref, stage, turned_ref
):
    chips = n // 2
    quota = LANES // chips
    rows_d = 8 * quota

    def collect(base):
        for half in range(2):
            for q in range(quota):
                top = half * LANES + q * chips
                for tb in range(2):
                    turned_ref[top : top + chips, tb * LANES : (tb + 1) * LANES] = stage[
                        pl.ds(half * rows_d + base + q * 2 + tb, chips, stride=2 * rows_d), :
                    ]
        return turned_ref[...].T

    stage[...] = b_back[...].reshape(stage.shape).astype(F32)
    out_ref[...] = collect(0).astype(BF16)
    gf_ref[1] = collect(2 * quota)
    gf_ref[0] = collect(4 * quota)
    lane = lax.broadcasted_iota(jnp.int32, (1, LANES), 1)
    for f in range(2):
        for half in range(2):
            line = jnp.zeros((1, LANES), F32)
            for q in range(quota):
                at = half * rows_d + 6 * quota + f * quota + q
                row = jnp.sum(stage[pl.ds(at, chips, stride=2 * rows_d), :], axis=0, keepdims=True)
                full = row + pltpu.roll(row, LANES - chips, 1) + pltpu.roll(row, LANES - 2 * chips, 1)
                moved = full if q == 0 else pltpu.roll(full, q * chips, 1)
                line = jnp.where((lane >= q * chips) & (lane < (q + 1) * chips), moved, line)
            gb_ref[f : f + 1, half * LANES : (half + 1) * LANES] = line
    gu_ref[...] = u_own[...].astype(BF16)
    for a in range(3):
        for half in range(2):
            gw_ref[a, :, half * LANES : (half + 1) * LANES] = w_own[a, half] + w_far[a, half]


def on_device(layer_input, w_in, filters, bias, cotangent):
    n = lax.axis_size("seq")
    groups = lax.axis_size("chan")
    tokens, width = layer_input.shape
    rows = w_in.shape[0]
    chips = n // 2
    ny = min(4, chips // 2)
    nx = chips // (2 * ny)
    plane = nx * ny
    quota = LANES // chips
    blocks = 4 * chips
    rows_a, rows_b, rows_c, rows_d = 12 * quota, 6 * quota, 4 * quota, 8 * quota
    cols = 3 * LANES
    vmem = pl.BlockSpec(memory_space=pltpu.VMEM)
    smem = pl.BlockSpec(memory_space=pltpu.SMEM)
    sds = jax.ShapeDtypeStruct
    dma = pltpu.SemaphoreType.DMA
    limit = 58 * 1024 * 1024
    spec = pltpu.VMEM((quota * blocks, 2 * LANES), F32)

    constants = [jnp.asarray(table) for table in tables(blocks)]
    landed = pl.pallas_call(
        functools.partial(layer_kernel, n, groups),
        out_shape=(
            sds((n, rows_d, LANES), BF16),
            sds((3, 2, rows, LANES), F32),
            sds((3, 2, rows, LANES), F32),
            sds((tokens, width), F32),
        ),
        in_specs=[vmem, vmem, smem] + [pl.BlockSpec(memory_space=pl.ANY)] * 8,
        out_specs=(vmem,) * 4,
        scratch_shapes=[
            *(pltpu.VMEM(array.shape, array.dtype) for array in (filters, cotangent, *constants)),
            dma((8,)),
            pltpu.VMEM((2, rows, cols), BF16),
            pltpu.VMEM((n, rows, cols), BF16),
            pltpu.VMEM((n, rows, cols), BF16),
            pltpu.VMEM((2, groups, tokens, width), BF16),
            pltpu.VMEM((groups, width, 2 * tokens), BF16),
            pltpu.VMEM((2, tokens, cols), F32),
            pltpu.VMEM((chips * rows_a, LANES), F32),
            pltpu.VMEM((chips, rows_a, LANES), BF16),
            pltpu.VMEM((chips, rows_a, LANES), BF16),
            pltpu.VMEM((n * rows_b, LANES), F32),
            pltpu.VMEM((n, rows_b, LANES), BF16),
            pltpu.VMEM((n, rows_b, LANES), BF16),
            spec, spec, spec, spec, spec, spec,
            pltpu.VMEM((chips * rows_c, LANES), F32),
            pltpu.VMEM((chips, 3, rows_c, LANES), BF16),
            pltpu.VMEM((chips, 3, rows_c, LANES), BF16),
            pltpu.VMEM((n * rows_d, LANES), F32),
            pltpu.VMEM((n, rows_d, LANES), BF16),
            pltpu.VMEM((LANES, 2 * tokens), F32),
            pltpu.VMEM((3, 2, tokens, LANES), BF16),
            pltpu.VMEM((3, tokens, LANES), BF16),
            pltpu.VMEM((3, nx, 2, 2 * ny, rows, LANES), BF16),
            pltpu.VMEM((3, 2 * plane, 2, rows, LANES), BF16),
            pltpu.VMEM((3, 2, rows, LANES), F32),
            pltpu.VMEM((groups, tokens, width), F32),
            pltpu.VMEM((groups, tokens, width), BF16),
            pltpu.VMEM((6, tokens // 2, width), BF16),
            pltpu.VMEM((2, tokens // 2, width), BF16),
            dma((17,)),
            dma((2 * groups,)), dma((6,)), dma((2 * groups,)), dma((8,)), dma((6,)), dma((6,)),
            dma((3,)), dma((3,)), dma((3,)), dma((3,)),
            dma((6,)), dma((6,)),
        ],
        compiler_params=pltpu.CompilerParams(
            collective_id=0, has_side_effects=True, vmem_limit_bytes=limit
        ),
        name="layer",
    )(layer_input, w_in.transpose(1, 0, 2), bias, filters, cotangent, *constants)

    out, grad_u, grad_w, grad_f, grad_b = pl.pallas_call(
        functools.partial(finish_kernel, n),
        out_shape=(
            sds((tokens, width), BF16),
            sds((tokens, width), BF16),
            sds((3, rows, width), F32),
            sds((2, tokens, width), F32),
            sds((2, width), F32),
        ),
        in_specs=[vmem] * 4,
        out_specs=(vmem,) * 5,
        scratch_shapes=[
            pltpu.VMEM((n * rows_d, LANES), F32),
            pltpu.VMEM((2 * LANES, tokens), F32),
        ],
        compiler_params=pltpu.CompilerParams(vmem_limit_bytes=limit),
        name="finish",
    )(*landed)
    return (out, grad_u, grad_w.transpose(1, 0, 2), grad_f, grad_b)


def solution(mesh):
    in_specs = (
        P("seq", "chan"),
        P("seq", None, "chan"),
        P(None, "seq", "chan"),
        P(None, "chan"),
        P("seq", "chan"),
    )
    out_specs = (
        P("seq", "chan"),
        P("seq", "chan"),
        P("seq", None, "chan"),
        P(None, "seq", "chan"),
        P(None, "chan"),
    )
    return jax.shard_map(
        on_device, mesh=mesh, in_specs=in_specs, out_specs=out_specs, check_vma=False
    )
```

```python
import functools
import math

import jax
import jax.numpy as jnp
import ml_dtypes
import numpy as np
from jax import lax
from jax.experimental import pallas as pl
from jax.experimental.pallas import tpu as pltpu
from jax.sharding import PartitionSpec as P

MESH = pl.DeviceIdType.MESH
LANES = 128
BF16 = jnp.bfloat16
F32 = jnp.float32


def tables(blocks):
    period = 2 * blocks * LANES
    chips = blocks // 4
    order = np.array([4 * j + tb for tb in range(4) for j in range(chips)])
    freq = np.arange(blocks) + 0.5
    lane = np.arange(LANES)
    angle = 2.0 * math.pi * freq[:, None] * order[None, :] / (2 * blocks)
    first = np.concatenate([np.cos(angle), -np.sin(angle)], axis=0)
    turn = 2.0 * math.pi * freq[:, None] * lane[None, :] / period
    inner = 2.0 * math.pi * ((lane[:, None] * lane[None, :]) % LANES) / LANES
    cosine, sine = np.cos(inner), np.sin(inner)
    middle = np.block([[cosine, -sine], [sine, cosine]])
    last = first.T * (2.0 / period)

    def parts(table, axis):
        high = table.astype(ml_dtypes.bfloat16)
        low = (table - high.astype(np.float64)).astype(ml_dtypes.bfloat16)
        return np.concatenate([high, low], axis=axis)

    return (
        parts(first, 1),
        parts(middle, 0),
        parts(middle.T, 0),
        parts(last, 1),
        np.cos(turn).astype(np.float32),
        np.sin(turn).astype(np.float32),
    )


def matmul(left, right, dims=((1,), (0,))):
    return lax.dot_general(left, right, (dims, ((), ())), preferred_element_type=F32)


def greet(me, peers, group, groups):
    barrier = pltpu.get_barrier_semaphore()

    def one(step, carry):
        pl.semaphore_signal(
            barrier, inc=1, device_id=(lax.rem(me + step, peers), group), device_id_type=MESH
        )
        return carry

    lax.fori_loop(1, peers, one, 0)
    for step in range(1, groups):
        pl.semaphore_signal(
            barrier, inc=1, device_id=(me, lax.rem(group + step, groups)), device_id_type=MESH
        )
    return barrier


def wait_bytes(ref, sem):
    pltpu.make_async_copy(ref, ref, sem).wait()


def send(src, dst, sem_out, sem_in, seq, chan):
    pltpu.make_async_remote_copy(
        src_ref=src, dst_ref=dst, send_sem=sem_out, recv_sem=sem_in,
        device_id=(seq, chan), device_id_type=MESH,
    ).start()


def layer_kernel(
    n, groups, x_ref, w_in_ref, bias_ref, filters_at, cot_at,
    first_at, middle_at, middle_t_at, last_at, cos_at, sin_at,
    b_back, w_own, w_far, u_own,
    filters_ref, cot_ref, first_ref, middle_ref, middle_t_ref, last_ref, cos_ref, sin_ref, load_sems,
    w_ref, wg, w_other, xg, xt, total, stage_a, a_send, a_recv, stage_b, b_send, b_recv,
    spec_h1, spec_h2, spec_v, spec_z, spec_g1, spec_g2,
    stage_c, g_send, g_recv, stage_d, b_give, turned_ref, grad, grad_in,
    w_send, w_in, w_relay, u_acc, u_send, u_in, u_far,
    sems, x_sems, xs_sems, xp_sems, xr_sems, u_sems, us_sems, gs_sems, g_sems, cs_sems, c_sems, ws_sems, w_sems,
):
    me = lax.axis_index("seq")
    group = lax.axis_index("chan")
    core = lax.rem(me, 2)
    chip = me // 2
    partner = me + 1 - 2 * core
    chips = n // 2
    ny = min(4, chips // 2)
    nx = chips // (2 * ny)
    plane = nx * ny
    y = lax.rem(chip, ny)
    zl = lax.rem(chip // ny, 2)
    xx = chip // (2 * ny)
    here = (xx * ny + y) * 2 + core
    quota = LANES // chips
    blocks = 4 * chips
    rows_a, rows_b = a_send.shape[1], b_send.shape[1]
    rows_c, rows_d = 4 * quota, 8 * quota
    tokens, depth = x_ref.shape
    cols = wg.shape[2]
    slots = depth // wg.shape[1]

    def in_plane(p, c, z):
        return (((p // ny) * 2 + z) * ny + lax.rem(p, ny)) * 2 + c

    def hops(step, extent):
        return min(step, extent - step)

    moves = sorted(
        ((dx, dz, dy) for dx in range(nx) for dz in range(2) for dy in range(ny)),
        key=lambda move: -(hops(move[0], nx) + move[1] + hops(move[2], ny)),
    )[:-1]

    def moved(dx, dz, dy, c):
        return (
            (lax.rem(xx + dx, nx) * 2 + lax.rem(zl + dz, 2)) * ny + lax.rem(y + dy, ny)
        ) * 2 + c

    pending = {}

    def expect(key, ref, sem):
        pending[key] = (ref, sem)

    def arrive(*key):
        wait_bytes(*pending.pop(key))

    barrier = greet(me, n, group, groups)

    for k, (here_ref, there_ref) in enumerate(
        (
            (filters_ref, filters_at), (cot_ref, cot_at), (first_ref, first_at), (middle_ref, middle_at),
            (middle_t_ref, middle_t_at), (last_ref, last_at), (cos_ref, cos_at), (sin_ref, sin_at),
        )
    ):
        pltpu.make_async_copy(there_ref, here_ref, load_sems.at[k]).start()
        expect(("load", k), here_ref, load_sems.at[k])

    for half in range(2):
        for a in range(3):
            w_ref[half, :, a * LANES : (a + 1) * LANES] = w_in_ref[a, :, half * LANES : (half + 1) * LANES]

    def spread(value, base):
        turned = value.T
        for half in range(2):
            for q in range(quota):
                top = half * LANES + q * chips
                for tb in range(2):
                    stage_b[pl.ds(half * rows_b + base + q * 2 + tb, chips, stride=2 * rows_b), :] = turned[
                        top : top + chips, tb * LANES : (tb + 1) * LANES
                    ]

    xg[core, group] = x_ref[...]
    pl.semaphore_wait(barrier, n - 1 + groups - 1)

    z_first = in_plane(xx * ny + y, 0, 1 - zl)
    for c in range(2):
        send(w_ref.at[c], wg.at[me], sems.at[0], sems.at[3], z_first + c, group)

    part = tokens // 2
    after, before, across = (lax.rem(group + step, groups) for step in (1, 3, 2))

    def half_x(side, source, half):
        return xg.at[side, source, pl.ds(half * part, part)]

    def send_x(half, target, k):
        own = half_x(core, group, half)
        send(own, own, xs_sems.at[k], x_sems.at[2 * group + half], me, target)
        expect(("x out", k), own, xs_sems.at[k])

    def relay_x(source, half, k):
        ref = half_x(core, source, half)
        send(ref, ref, xr_sems.at[k], xp_sems.at[2 * source + half], partner, group)
        expect(("xp", k), half_x(1 - core, source, half), xp_sems.at[2 * source + half])
        expect(("x relay", k), ref, xr_sems.at[k])

    for k, (half, target) in enumerate(((0, after), (1, before), (1, after), (0, before))):
        send_x(half, target, k)
    arrivals = ((before, 0), (after, 1), (before, 1), (after, 0), (across, 0), (across, 1))
    for k, (source, half) in enumerate(arrivals):
        expect(("x", k), half_x(core, source, half), x_sems.at[2 * source + half])

    for dx, dz, dy in moves:
        if dz == 0:
            for c in range(2):
                send(w_ref.at[c], wg.at[me], sems.at[0], sems.at[1], moved(dx, 0, dy, c), group)
    send(w_ref.at[1 - core], wg.at[me], sems.at[0], sems.at[1], partner, group)
    pltpu.make_async_copy(w_ref.at[core], wg.at[me], sems.at[1]).start()
    expect(("w",), wg.at[pl.ds(0, 2 * plane)], sems.at[1])
    expect(("w out",), wg.at[pl.ds(0, 2 * plane + 1)], sems.at[0])
    for half in range(2):
        relay_x(group, half, 6 + half)

    arrive("load", 0)
    spread(filters_ref[0], 0)
    wait_bytes(wg.at[pl.ds(z_first, 2)], sems.at[3])

    pair = wg.at[pl.ds(z_first, 2)]
    for dx, dz, dy in moves:
        if dz == 0:
            send(pair, pair, sems.at[4], sems.at[5], moved(dx, 0, dy, core), group)
    expect(("w rest",), wg.at[pl.ds(0, 2 * plane - 2)], sems.at[5])
    expect(("w rest out",), wg.at[pl.ds(0, 2 * plane - 2)], sems.at[4])
    spread(filters_ref[1], 2 * quota)
    for k in range(2):
        arrive("x", k)
        source, half = arrivals[k]
        ref = half_x(core, source, half)
        send(ref, ref, xs_sems.at[4 + k], x_sems.at[2 * source + half], me, after if k == 0 else before)
        expect(("x out", 4 + k), ref, xs_sems.at[4 + k])
        relay_x(source, half, k)
    arrive("load", 1)
    spread(cot_ref[...].astype(F32), 4 * quota)
    for peer in range(n):
        b_send[peer] = stage_b[peer * rows_b : (peer + 1) * rows_b, :].astype(BF16)

    def give_b(step, carry):
        peer = lax.rem(me + step, n)
        send(b_send.at[peer], b_recv.at[me], sems.at[9], sems.at[10], peer, group)
        return carry

    for k in (2, 3):
        arrive("x", k)
        relay_x(*arrivals[k], k)
    arrive("w")
    arrive("w rest")
    lax.fori_loop(1, n, give_b, 0)
    pltpu.make_async_copy(b_send.at[me], b_recv.at[me], sems.at[10]).start()
    expect(("b",), b_recv, sems.at[10])
    expect(("b out",), b_recv.at[pl.ds(0, n - 1)], sems.at[9])

    def weights(ref, c):
        return ref[pl.ds(c * slots, slots)].reshape(depth, cols)

    def project(side, source, first=False):
        at = core if side == 0 else 1 - core
        term = matmul(xg[at, source], weights(wg, source))
        total[at] = term if first else total[at] + term

    project(0, group, True)
    for k in (6, 7):
        arrive("xp", k)
    project(1, group, True)
    project(0, before)
    project(0, after)
    for k in range(4):
        arrive("xp", k)
    project(1, before)
    project(1, after)
    for k in (4, 5):
        arrive("x", k)
        relay_x(*arrivals[k], k)
    def lay_out(at):
        turned = total[at].T
        for a in range(3):
            for q in range(quota):
                top = a * LANES + q * chips
                for tb in range(2):
                    row = (a * quota + q) * 4 + 2 * at + tb
                    stage_a[pl.ds(row, chips, stride=rows_a), :] = turned[
                        top : top + chips, tb * LANES : (tb + 1) * LANES
                    ]

    project(0, across)
    lay_out(core)
    for k in (4, 5):
        arrive("xp", k)
    project(1, across)
    lay_out(1 - core)
    a_send[...] = stage_a[...].astype(BF16).reshape(a_send.shape)

    for move in moves:
        peer = moved(*move, core)
        send(a_send.at[peer // 2], a_recv.at[chip], sems.at[11], sems.at[12], peer, group)
    pltpu.make_async_copy(a_send.at[chip], a_recv.at[chip], sems.at[12]).start()
    expect(("a",), a_recv, sems.at[12])
    expect(("a out",), a_recv.at[pl.ds(0, chips - 1)], sems.at[11])
    send(wg, w_other, sems.at[7], sems.at[8], partner, group)
    expect(("other",), w_other, sems.at[8])
    expect(("other out",), w_other, sems.at[7])
    for k in range(2, 8):
        arrive("load", k)

    def columns(ref, start, stride):
        return jnp.concatenate(
            [
                jnp.concatenate(
                    [ref[pl.ds(start(q, tb), chips, stride=stride), :] for q in range(quota)], axis=1
                )
                for tb in range(4)
            ],
            axis=0,
        )

    def late(a):
        return columns(stage_a, lambda q, tb: (a * quota + q) * 4 + tb, rows_a)

    def early(base):
        return columns(stage_b, lambda q, tb: (tb // 2) * rows_b + base + q * 2 + tb % 2, 2 * rows_b)

    def piece(value, q):
        return value[:, q * LANES : (q + 1) * LANES]

    def twice(value, axis):
        high = value.astype(BF16)
        return jnp.concatenate([high, high], axis=axis)

    def forward(value, spec):
        wide = matmul(first_ref[...], twice(value, 0))
        turn_cos, turn_sin = cos_ref[...], sin_ref[...]
        for q in range(quota):
            re = piece(wide[:blocks], q)
            im = piece(wide[blocks:], q)
            turned = jnp.concatenate([re * turn_cos + im * turn_sin, im * turn_cos - re * turn_sin], axis=1)
            spec[q * blocks : (q + 1) * blocks, :] = matmul(twice(turned, 1), middle_ref[...])

    def backward(left, right, conj_left, conj_right):
        turn_cos, turn_sin = cos_ref[...], sin_ref[...]
        parts = []
        for q in range(quota):
            rows = slice(q * blocks, (q + 1) * blocks)
            l_re, l_im = left[rows, :LANES], left[rows, LANES:]
            r_re, r_im = right[rows, :LANES], right[rows, LANES:]
            cross = l_im * r_im
            y_re = l_re * r_re - (cross if conj_left == conj_right else -cross)
            if conj_left:
                y_im = l_re * r_im - l_im * r_re
            elif conj_right:
                y_im = l_im * r_re - l_re * r_im
            else:
                y_im = l_re * r_im + l_im * r_re
            out = matmul(twice(jnp.concatenate([y_re, y_im], axis=1), 1), middle_t_ref[...])
            re, im = out[:, :LANES], out[:, LANES:]
            parts.append(jnp.concatenate([re * turn_cos - im * turn_sin, im * turn_cos + re * turn_sin], axis=0))
        return matmul(last_ref[...], twice(jnp.concatenate(parts, axis=1), 0))

    def skip(f):
        return jnp.concatenate(
            [
                jnp.full((1, LANES), bias_ref[f, core * LANES + q * chips + chip], F32)
                for q in range(quota)
            ],
            axis=1,
        )

    order = {1: 0, 0: 1, 2: 2}

    def put_late(value, a):
        for q in range(quota):
            for tb in range(4):
                stage_c[pl.ds(q * 4 + tb, chips, stride=rows_c), :] = piece(value, q)[
                    tb * chips : (tb + 1) * chips
                ]
        g_send[:, order[a]] = stage_c[...].astype(BF16).reshape(chips, rows_c, LANES)

    def give_late(k, span):
        for move in moves:
            peer = moved(*move, core)
            send(g_send.at[peer // 2, span], g_recv.at[chip, span], gs_sems.at[k], g_sems.at[k], peer, group)
        pltpu.make_async_copy(g_send.at[chip, span], g_recv.at[chip, span], g_sems.at[k]).start()
        expect(("g", k), g_recv.at[:, span], g_sems.at[k])
        expect(("g out", k), g_recv.at[pl.ds(0, chips - 1), span], gs_sems.at[k])

    def put_early(value, base):
        for q in range(quota):
            for tb in range(4):
                at = (tb // 2) * rows_d + base + q * 2 + tb % 2
                stage_d[pl.ds(at, chips, stride=2 * rows_d), :] = piece(value, q)[
                    tb * chips : (tb + 1) * chips
                ]

    def put_skip(product, f):
        lane = lax.broadcasted_iota(jnp.int32, (1, LANES), 1)
        sums = jnp.sum(product, axis=0, keepdims=True)
        for q in range(quota):
            value = jnp.sum(piece(sums, q), axis=1, keepdims=True)
            one = value.astype(BF16).astype(F32)
            two = (value - one).astype(BF16).astype(F32)
            three = value - one - two
            row = jnp.where(lane == chip, one, 0.0)
            row = jnp.where(lane == chips + chip, two, row)
            row = jnp.where(lane == 2 * chips + chip, three, row)
            for half in range(2):
                at = half * rows_d + 6 * quota + f * quota + q
                stage_d[pl.ds(at, chips, stride=2 * rows_d), :] = jnp.broadcast_to(row, (chips, LANES))

    def give_early():
        for peer in range(n):
            b_give[peer] = stage_d[peer * rows_d : (peer + 1) * rows_d, :].astype(BF16)

        def one(step, carry):
            peer = lax.rem(me + step, n)
            send(b_give.at[peer], b_back.at[me], sems.at[14], sems.at[15], peer, group)
            return carry

        lax.fori_loop(1, n, one, 0)
        pltpu.make_async_copy(b_give.at[me], b_back.at[me], sems.at[15]).start()
        expect(("back",), b_back, sems.at[15])
        expect(("back out",), b_back.at[pl.ds(0, n - 1)], sems.at[14])

    arrive("b")
    for peer in range(n):
        stage_b[peer * rows_b : (peer + 1) * rows_b, :] = b_recv[peer].astype(F32)
    forward(early(0), spec_h1)
    forward(early(2 * quota), spec_h2)
    for c in range(groups):
        xt[c] = xg[:, c].reshape(2 * tokens, depth).astype(F32).T.astype(BF16)
    arrive("a")
    stage_a[...] = a_recv[...].reshape(stage_a.shape).astype(F32)
    values_v, gate_one, gate_two = late(0), late(1), late(2)
    grad_out = early(4 * quota)
    skip_one, skip_two = skip(0), skip(1)
    grad_conv_two = grad_out * gate_two
    forward(grad_conv_two, spec_g2)
    forward(values_v, spec_v)
    grad_mixed = backward(spec_h2, spec_g2, True, False) + skip_two * grad_conv_two
    conv_one = backward(spec_h1, spec_v, False, False) + skip_one * values_v
    mixed = gate_one * conv_one
    grad_conv_one = grad_mixed * gate_one
    put_late(grad_mixed * conv_one, 1)
    give_late(0, pl.ds(0, 1))
    forward(grad_conv_one, spec_g1)
    forward(mixed, spec_z)
    grad_v = backward(spec_h1, spec_g1, True, False) + skip_one * grad_conv_one
    conv_two = backward(spec_h2, spec_z, False, False) + skip_two * mixed
    put_late(grad_v, 0)
    give_late(1, pl.ds(1, 1))
    put_late(grad_out * conv_two, 2)
    give_late(2, pl.ds(2, 1))
    put_early(gate_two * conv_two, 0)
    put_early(backward(spec_g2, spec_z, False, True), 2 * quota)
    put_early(backward(spec_g1, spec_v, False, True), 4 * quota)
    put_skip(grad_conv_one * values_v, 0)
    put_skip(grad_conv_two * mixed, 1)

    def take(a):
        stage_c[...] = g_recv[:, order[a]].reshape(stage_c.shape).astype(F32)
        for q in range(quota):
            for tb in range(4):
                turned_ref[q * chips : (q + 1) * chips, tb * LANES : (tb + 1) * LANES] = stage_c[
                    pl.ds(q * 4 + tb, chips, stride=rows_c), :
                ]
        grad[a] = turned_ref[...].T.astype(BF16).reshape(2, tokens, LANES)
        send(grad.at[a, 1 - core], grad_in.at[a], cs_sems.at[a], c_sems.at[a], partner, group)
        expect(("grad", a), grad_in.at[a], c_sems.at[a])
        expect(("grad out", a), grad_in.at[a], cs_sems.at[a])

    def give_w(a):
        block = grad[a].reshape(2 * tokens, LANES)
        for c in range(groups):
            term = matmul(xt[c], block).astype(BF16).reshape(slots, depth // slots, LANES)
            for k in range(slots):
                s = c * slots + k
                w_send[a, s // (4 * ny), (s // (2 * ny)) % 2, s % (2 * ny)] = term[k]

        for dx, dz, dy in moves + [(0, 0, 0)]:
            for c in range(2) if dx + dy else ([1 - core] if dz == 0 else []):
                if dz == 0:
                    px, py = lax.rem(xx + dx, nx), lax.rem(y + dy, ny)
                    send(
                        w_send.at[a, px, :, py * 2 + c], w_in.at[a, here],
                        ws_sems.at[a], w_sems.at[a], moved(dx, 0, dy, c), group,
                    )
        pltpu.make_async_copy(w_send.at[a, xx, :, y * 2 + core], w_in.at[a, here], w_sems.at[a]).start()
        expect(("sum", a), w_in.at[a], w_sems.at[a])
        expect(("sum out", a), w_in.at[a, pl.ds(0, 2 * plane - 1)], ws_sems.at[a])

    def relay_w(a):
        arrive("sum", a)
        for half in range(2):
            own = w_in[a, half, zl].astype(F32)
            away = w_in[a, half, 1 - zl].astype(F32)
            for p in range(1, plane):
                own = own + w_in[a, 2 * p + half, zl].astype(F32)
                away = away + w_in[a, 2 * p + half, 1 - zl].astype(F32)
            w_own[a, half] = own
            w_relay[a, half] = away
        send(w_relay.at[a], w_far.at[a], ws_sems.at[3 + a], w_sems.at[3 + a], z_first + core, group)
        expect(("far", a), w_far.at[a], w_sems.at[3 + a])
        expect(("far out", a), w_far.at[a], ws_sems.at[3 + a])

    def into_u(terms, c):
        left, right = [], []
        for a, own in terms:
            left.append(grad[a, core] if own else grad_in[a])
            right.append(piece(weights(wg if own else w_other, c), a))
        return matmul(jnp.concatenate(left, axis=1), jnp.concatenate(right, axis=1), ((1,), (1,)))

    arrive("g", 0)
    take(1)
    give_early()
    give_w(1)
    arrive("other")
    arrive("grad", 1)
    for c in range(groups):
        u_acc[c] = into_u(((1, True), (1, False)), c)
    arrive("g", 1)
    take(0)
    arrive("g", 2)
    take(2)
    give_w(0)
    for c in range(groups):
        u_acc[c] = u_acc[c] + into_u(((0, True), (2, True)), c)
    arrive("grad", 0)
    arrive("grad", 2)

    def send_u(ref, slot, target):
        send(ref, u_in.at[slot], us_sems.at[slot], u_sems.at[slot], me, target)
        expect(("u", slot), u_in.at[slot], u_sems.at[slot])
        expect(("u out", slot), u_in.at[slot], us_sems.at[slot])

    def half_u(dest, half):
        return u_send.at[dest, pl.ds(half * part, part)]

    def into_last(dest):
        return into_u(((0, False), (2, False)), dest)

    def finish_u(dest):
        value = u_acc[dest] + into_last(dest)
        u_acc[dest] = value
        u_send[dest] = value.astype(BF16)

    finish_u(across)
    send_u(half_u(across, 0), 0, after)
    send_u(half_u(across, 1), 1, before)
    finish_u(after)
    send_u(half_u(after, 1), 2, after)
    finish_u(before)
    send_u(half_u(before, 0), 3, before)
    give_w(2)
    u_own[...] = u_acc[group] + into_last(group)
    relay_w(1)
    arrive("u", 0)
    u_far[0] = (u_acc[after, :part] + u_in[0].astype(F32)).astype(BF16)
    send_u(u_far.at[0], 4, after)
    arrive("u", 1)
    u_far[1] = (u_acc[before, part:] + u_in[1].astype(F32)).astype(BF16)
    send_u(u_far.at[1], 5, before)

    relay_w(0)
    relay_w(2)

    for slot in range(2, 6):
        arrive("u", slot)
    u_own[:part] = u_own[:part] + u_in[3].astype(F32) + u_in[4].astype(F32)
    u_own[part:] = u_own[part:] + u_in[2].astype(F32) + u_in[5].astype(F32)
    for key in list(pending):
        arrive(*key)


def finish_kernel(
    n, b_back, w_own, w_far, u_own, out_ref, gu_ref, gw_ref, gf_ref, gb_ref, stage, turned_ref
):
    chips = n // 2
    quota = LANES // chips
    rows_d = 8 * quota

    def collect(base):
        for half in range(2):
            for q in range(quota):
                top = half * LANES + q * chips
                for tb in range(2):
                    turned_ref[top : top + chips, tb * LANES : (tb + 1) * LANES] = stage[
                        pl.ds(half * rows_d + base + q * 2 + tb, chips, stride=2 * rows_d), :
                    ]
        return turned_ref[...].T

    stage[...] = b_back[...].reshape(stage.shape).astype(F32)
    out_ref[...] = collect(0).astype(BF16)
    gf_ref[1] = collect(2 * quota)
    gf_ref[0] = collect(4 * quota)
    lane = lax.broadcasted_iota(jnp.int32, (1, LANES), 1)
    for f in range(2):
        for half in range(2):
            line = jnp.zeros((1, LANES), F32)
            for q in range(quota):
                at = half * rows_d + 6 * quota + f * quota + q
                row = jnp.sum(stage[pl.ds(at, chips, stride=2 * rows_d), :], axis=0, keepdims=True)
                full = row + pltpu.roll(row, LANES - chips, 1) + pltpu.roll(row, LANES - 2 * chips, 1)
                moved = full if q == 0 else pltpu.roll(full, q * chips, 1)
                line = jnp.where((lane >= q * chips) & (lane < (q + 1) * chips), moved, line)
            gb_ref[f : f + 1, half * LANES : (half + 1) * LANES] = line
    gu_ref[...] = u_own[...].astype(BF16)
    for a in range(3):
        for half in range(2):
            gw_ref[a, :, half * LANES : (half + 1) * LANES] = w_own[a, half] + w_far[a, half]


def on_device(layer_input, w_in, filters, bias, cotangent):
    n = lax.axis_size("seq")
    groups = lax.axis_size("chan")
    tokens, width = layer_input.shape
    rows = w_in.shape[0]
    chips = n // 2
    ny = min(4, chips // 2)
    nx = chips // (2 * ny)
    plane = nx * ny
    quota = LANES // chips
    blocks = 4 * chips
    rows_a, rows_b, rows_c, rows_d = 12 * quota, 6 * quota, 4 * quota, 8 * quota
    cols = 3 * LANES
    vmem = pl.BlockSpec(memory_space=pltpu.VMEM)
    smem = pl.BlockSpec(memory_space=pltpu.SMEM)
    sds = jax.ShapeDtypeStruct
    dma = pltpu.SemaphoreType.DMA
    limit = 58 * 1024 * 1024
    spec = pltpu.VMEM((quota * blocks, 2 * LANES), F32)

    constants = [jnp.asarray(table) for table in tables(blocks)]
    landed = pl.pallas_call(
        functools.partial(layer_kernel, n, groups),
        out_shape=(
            sds((n, rows_d, LANES), BF16),
            sds((3, 2, rows, LANES), F32),
            sds((3, 2, rows, LANES), F32),
            sds((tokens, width), F32),
        ),
        in_specs=[vmem, vmem, smem] + [pl.BlockSpec(memory_space=pl.ANY)] * 8,
        out_specs=(vmem,) * 4,
        scratch_shapes=[
            *(pltpu.VMEM(array.shape, array.dtype) for array in (filters, cotangent, *constants)),
            dma((8,)),
            pltpu.VMEM((2, rows, cols), BF16),
            pltpu.VMEM((n, rows, cols), BF16),
            pltpu.VMEM((n, rows, cols), BF16),
            pltpu.VMEM((2, groups, tokens, width), BF16),
            pltpu.VMEM((groups, width, 2 * tokens), BF16),
            pltpu.VMEM((2, tokens, cols), F32),
            pltpu.VMEM((chips * rows_a, LANES), F32),
            pltpu.VMEM((chips, rows_a, LANES), BF16),
            pltpu.VMEM((chips, rows_a, LANES), BF16),
            pltpu.VMEM((n * rows_b, LANES), F32),
            pltpu.VMEM((n, rows_b, LANES), BF16),
            pltpu.VMEM((n, rows_b, LANES), BF16),
            spec, spec, spec, spec, spec, spec,
            pltpu.VMEM((chips * rows_c, LANES), F32),
            pltpu.VMEM((chips, 3, rows_c, LANES), BF16),
            pltpu.VMEM((chips, 3, rows_c, LANES), BF16),
            pltpu.VMEM((n * rows_d, LANES), F32),
            pltpu.VMEM((n, rows_d, LANES), BF16),
            pltpu.VMEM((LANES, 2 * tokens), F32),
            pltpu.VMEM((3, 2, tokens, LANES), BF16),
            pltpu.VMEM((3, tokens, LANES), BF16),
            pltpu.VMEM((3, nx, 2, 2 * ny, rows, LANES), BF16),
            pltpu.VMEM((3, 2 * plane, 2, rows, LANES), BF16),
            pltpu.VMEM((3, 2, rows, LANES), F32),
            pltpu.VMEM((groups, tokens, width), F32),
            pltpu.VMEM((groups, tokens, width), BF16),
            pltpu.VMEM((6, tokens // 2, width), BF16),
            pltpu.VMEM((2, tokens // 2, width), BF16),
            dma((17,)),
            dma((2 * groups,)), dma((6,)), dma((2 * groups,)), dma((8,)), dma((6,)), dma((6,)),
            dma((3,)), dma((3,)), dma((3,)), dma((3,)),
            dma((6,)), dma((6,)),
        ],
        compiler_params=pltpu.CompilerParams(
            collective_id=0, has_side_effects=True, vmem_limit_bytes=limit
        ),
        name="layer",
    )(layer_input, w_in.transpose(1, 0, 2), bias, filters, cotangent, *constants)

    out, grad_u, grad_w, grad_f, grad_b = pl.pallas_call(
        functools.partial(finish_kernel, n),
        out_shape=(
            sds((tokens, width), BF16),
            sds((tokens, width), BF16),
            sds((3, rows, width), F32),
            sds((2, tokens, width), F32),
            sds((2, width), F32),
        ),
        in_specs=[vmem] * 4,
        out_specs=(vmem,) * 5,
        scratch_shapes=[
            pltpu.VMEM((n * rows_d, LANES), F32),
            pltpu.VMEM((2 * LANES, tokens), F32),
        ],
        compiler_params=pltpu.CompilerParams(vmem_limit_bytes=limit),
        name="finish",
    )(*landed)
    return (out, grad_u, grad_w.transpose(1, 0, 2), grad_f, grad_b)


def solution(mesh):
    in_specs = (
        P("seq", "chan"),
        P("seq", None, "chan"),
        P(None, "seq", "chan"),
        P(None, "chan"),
        P("seq", "chan"),
    )
    out_specs = (
        P("seq", "chan"),
        P("seq", "chan"),
        P("seq", None, "chan"),
        P(None, "seq", "chan"),
        P(None, "chan"),
    )
    return jax.shard_map(
        on_device, mesh=mesh, in_specs=in_specs, out_specs=out_specs, check_vma=False
    )
```
